32 devices in a mesh: ctx: 8 (over z, x), wa: 4 (over y, core).
Axes of the slice: x: 2, y: 2, z: 4, core: 2. Of those that a mesh axis runs over, the one named last changes fastest.
Arguments:
- tokens: bfloat16 [4, 1024, 960], P('wa', 'ctx'), may hold values from -6 to 6
- cotangent: bfloat16 [4, 1024, 960], P('wa', 'ctx'), may hold values from -6 to 6
- segment_ids: int32 [4, 1024], P('wa'), may hold values from 0 to 7, never falling along the last dimension, each value on 1 to 512 neighbouring positions
- block_order: int32 [4, 8], P('wa'), may hold values from 0 to 7, each once within a row
- gain_attn: float32 [960], P('wa'), may hold values from 0.5 to 1.5
- w_query: float32 [960, 960], P('wa'), may hold values from -0.1875 to 0.1875
- key_projection: float32 [960, 320], P('wa'), may hold values from -0.1875 to 0.1875
- value_projection: float32 [960, 320], P('wa'), may hold values from -0.1875 to 0.1875
- w_out: float32 [960, 960], P('wa'), may hold values from -0.75 to 0.75
- gain_mlp: float32 [960], P('wa'), may hold values from 0.5 to 1.5
- w_gate: float32 [960, 2560], P('wa'), may hold values from -0.1875 to 0.1875
- w_up: float32 [960, 2560], P('wa'), may hold values from -0.1875 to 0.1875
- w_down: float32 [2560, 960], P('wa'), may hold values from -0.125 to 0.125
Outputs:
- output: bfloat16 [4, 1024, 960], P('wa', 'ctx')
- input_grad: bfloat16 [4, 1024, 960], P('wa', 'ctx')
- grad_gain_attn: float32 [960], P('wa')
- grad_query: float32 [960, 960], P('wa')
- grad_key: float32 [960, 320], P('wa')
- grad_value: float32 [960, 320], P('wa')
- grad_out: float32 [960, 960], P('wa')
- grad_gain_mlp: float32 [960], P('wa')
- grad_gate: float32 [960, 2560], P('wa')
- grad_up: float32 [960, 2560], P('wa')
- grad_down: float32 [2560, 960], P('wa')
The draws below stay inside these ranges and needn't reach their ends.
Inputs may be any that keep to these rules, and one draw needn't show every extreme that they name: `segment_ids`: in each group ids never fall along the given order; each of the 8 sequences has 1 to 512 tokens, and one has exactly 512. `block_order`: each row names every block of its group once.
All inputs are finite; a program needn't handle non-finite values.
Results may differ from the reference program's by a relative error of at most 0.023.
Values may be sent and summed in bfloat16 or wider, within the bound.
No kernel may reach another device: no remote copies, remote signals or barrier semaphores. Data moves between devices by JAX's collectives and lax.ppermute only.
A program may use at most 256 MiB of HBM per device.

```python
import math
import jax
import jax.numpy as jnp
import numpy as np
from jax import lax

MODEL_WIDTH = 960
QUERY_HEADS = 15
KEY_VALUE_HEADS = 5
HEAD_SIZE = 64
FF = 2560
BLK = 128
SEQS = 8
REPEATS = 2
GROUPS = 4
NBLK = 8
GROUP_TOKENS = 1024
LONGEST = 512


def levels(stream_key, dims, pieces, smallest, top_value):
    loudness = 1.0
    for position, parts in pieces:
        draws = jax.random.uniform(jax.random.fold_in(jax.random.fold_in(stream_key, 6), position), (parts,), jnp.float32, smallest / len(pieces), top_value / len(pieces))
        loudness = loudness * jnp.repeat(jnp.exp(draws), dims[position] // parts).reshape((-1,) + (1,) * (len(dims) - 1 - position))
    return loudness


def profile(number_of, total, reach, skew):
    weights = [(1 << 20) // math.isqrt(rank ** skew) + 1 for rank in range(2, number_of + 1)]
    spare, given = total - reach - (number_of - 1), [1] * (number_of - 1)
    while spare > 0:
        movable = [i for i in range(number_of - 1) if given[i] < reach]
        whole, left = sum([weights[i] for i in movable]), spare
        for i in movable:
            extra = min(reach - given[i], max(1, left * weights[i] // whole), spare)
            given[i] = given[i] + extra
            spare = spare - extra
    return np.array([reach] + given)


def ragged(rng, number_of, total, bound, slope):
    if number_of == 2:
        one = jax.random.randint(rng, (), max(1, total - bound), min(bound, total - 1) + 1)
        return jnp.stack([one, total - one])
    lengths = jnp.asarray(profile(number_of, total, bound, slope), jnp.int32)
    couples = (number_of - 1) // 2
    donor, taker = lengths[1:1 + 2 * couples:2], lengths[2:2 + 2 * couples:2]
    slack = jnp.minimum(donor - 1, bound - taker)
    shifted = jax.random.randint(jax.random.fold_in(rng, 1), (couples,), 0, 1 << 20) % (slack + 1)
    lengths = lengths.at[1:1 + 2 * couples:2].set(donor - shifted).at[2:2 + 2 * couples:2].set(taker + shifted)
    return lengths[jax.random.permutation(jax.random.fold_in(rng, 2), number_of)]


def scatter_about(key, dims, width, reach, split=(), kind=jnp.bfloat16):
    level = levels(key, dims, split, -0.22, 0.18) if split else 1.0
    result = jax.random.normal(key, dims, jnp.float32) * width * level
    return jnp.minimum(jnp.maximum(result, -reach), reach).astype(kind)


def setup_inputs(seed: int = 0) -> dict:
    streams_of = jax.random.split(jax.random.key(seed), 14)
    tokens = scatter_about(streams_of[0], (GROUPS, GROUP_TOKENS, MODEL_WIDTH), 1.0, 6.0, ((0, 4), (1, 8)))
    cotangent = scatter_about(streams_of[1], (GROUPS, GROUP_TOKENS, MODEL_WIDTH), 1.0, 6.0, ((0, 4), (1, 8)))
    segment_ids = jax.vmap(lambda own: jnp.searchsorted(jnp.cumsum(ragged(own, SEQS, GROUP_TOKENS, LONGEST, 2)), jnp.arange(GROUP_TOKENS), side="right"))(jax.random.split(streams_of[2], GROUPS)).reshape((GROUPS, GROUP_TOKENS)).astype(jnp.int32)
    block_order = jax.vmap(lambda own: jax.random.permutation(own, NBLK))(jax.random.split(streams_of[3], GROUPS)).reshape((GROUPS, NBLK)).astype(jnp.int32)
    gain_attn = jnp.clip(1.0 + 0.1 * jax.random.normal(streams_of[4], (MODEL_WIDTH,), jnp.float32), 0.5, 1.5)
    w_query = scatter_about(streams_of[5], (MODEL_WIDTH, MODEL_WIDTH), MODEL_WIDTH ** -0.5, 0.1875, ((0, 4),), jnp.float32)
    key_projection = scatter_about(streams_of[6], (MODEL_WIDTH, KEY_VALUE_HEADS * HEAD_SIZE), MODEL_WIDTH ** -0.5, 0.1875, ((0, 4),), jnp.float32)
    value_projection = scatter_about(streams_of[7], (MODEL_WIDTH, KEY_VALUE_HEADS * HEAD_SIZE), MODEL_WIDTH ** -0.5, 0.1875, ((0, 4),), jnp.float32)
    w_out = scatter_about(streams_of[8], (MODEL_WIDTH, MODEL_WIDTH), (MODEL_WIDTH // 16) ** -0.5, 0.75, ((0, 4),), jnp.float32)
    gain_mlp = jnp.clip(1.0 + 0.1 * jax.random.normal(streams_of[9], (MODEL_WIDTH,), jnp.float32), 0.5, 1.5)
    w_gate = scatter_about(streams_of[10], (MODEL_WIDTH, FF), MODEL_WIDTH ** -0.5, 0.1875, ((0, 4),), jnp.float32)
    w_up = scatter_about(streams_of[11], (MODEL_WIDTH, FF), MODEL_WIDTH ** -0.5, 0.1875, ((0, 4),), jnp.float32)
    w_down = scatter_about(streams_of[12], (FF, MODEL_WIDTH), FF ** -0.5, 0.125, ((0, 4),), jnp.float32)
    return {"tokens": tokens, "cotangent": cotangent, "segment_ids": segment_ids, "block_order": block_order, "gain_attn": gain_attn, "w_query": w_query, "key_projection": key_projection, "value_projection": value_projection, "w_out": w_out, "gain_mlp": gain_mlp, "w_gate": w_gate, "w_up": w_up, "w_down": w_down}


@jax.custom_vjp
def lowered_input(v):
    return lax.optimization_barrier(v.astype(jnp.bfloat16)).astype(jnp.float32)

@jax.custom_vjp
def lowered_gradient(v):
    return v

def low_keep(v):
    return (lowered_input(v), None)

def low_pass(kept, grad):
    return (grad,)

def back_keep(v):
    return (v, None)

def back_low(kept, grad):
    return (lowered_input(grad),)
lowered_input.defvjp(low_keep, low_pass)
lowered_gradient.defvjp(back_keep, back_low)
epsilon = 1e-05
masked_score = -1e+30
rope_base = 10000.0
highest_precision = lax.Precision.HIGHEST

def token_layout(segment_row, order_row):
    dealt_index = jnp.arange(GROUP_TOKENS, dtype=jnp.int32)
    natural = (order_row[dealt_index // BLK] * BLK + dealt_index % BLK).astype(jnp.int32)
    segment_of = segment_row[natural]
    labels = jnp.arange(SEQS, dtype=jnp.int32)
    segment_sizes = lax.optimization_barrier(jnp.sum((segment_row[None, :] == labels[:, None]).astype(jnp.int32), axis=1)).astype(jnp.int32)
    segment_start = jnp.cumsum(segment_sizes).astype(jnp.int32) - segment_sizes
    positions = natural - segment_start[segment_of]
    return (natural, segment_of, positions)

def rope_tables(positions):
    half_size = HEAD_SIZE // 2
    frequency = rope_base ** (-jnp.arange(half_size, dtype=jnp.float32) * 2.0 / HEAD_SIZE)
    angles = positions.astype(jnp.float32)[:, None] * frequency[None, :]
    cosine_table = jnp.concatenate([jnp.cos(angles), jnp.cos(angles)], axis=1)
    sine_values = jnp.concatenate([jnp.sin(angles), jnp.sin(angles)], axis=1)
    return (cosine_table[:, None, :], sine_values[:, None, :])

def rotate_heads(value_rows, cosine_table, sine_values):
    half_size = value_rows.shape[-1] // 2
    turned = jnp.concatenate([-value_rows[..., half_size:], value_rows[..., :half_size]], axis=-1)
    return value_rows * cosine_table + turned * sine_values

def attend_group(query, keys, value_rows, natural, segment_of):
    tokens_per_group = QUERY_HEADS // KEY_VALUE_HEADS
    keys_wide = jnp.repeat(keys, tokens_per_group, axis=1)
    values_wide = jnp.repeat(value_rows, tokens_per_group, axis=1)
    query_block = min(512, GROUP_TOKENS)
    score_scale = HEAD_SIZE ** (-0.5)

    def one_block(block_index):
        start_row = block_index * query_block
        query_rows = lax.dynamic_slice_in_dim(query, start_row, query_block, 0)
        natural_rows = lax.dynamic_slice_in_dim(natural, start_row, query_block, 0)
        segment_rows = lax.dynamic_slice_in_dim(segment_of, start_row, query_block, 0)
        scores = lowered_gradient(jnp.einsum('thd,shd->hts', query_rows, keys_wide, precision=highest_precision)) * score_scale
        allowed = (segment_rows[:, None] == segment_of[None, :]) & (natural[None, :] <= natural_rows[:, None])
        scores = jnp.where(allowed[None], scores, masked_score)
        weights = jax.nn.softmax(scores, axis=-1)
        return jnp.einsum('hts,shd->thd', lowered_input(weights), values_wide, precision=highest_precision)
    blocks_out = lax.map(jax.checkpoint(one_block), jnp.arange(GROUP_TOKENS // query_block, dtype=jnp.int32))
    return blocks_out.reshape(GROUP_TOKENS, QUERY_HEADS * HEAD_SIZE)

def norm_rows(hidden, gain):
    ratio = lax.rsqrt(lax.optimization_barrier(jnp.mean(hidden * hidden, axis=-1, keepdims=True)) + epsilon)
    return hidden * ratio * gain

def block_layer(hidden, weights, cosine_table, sine_values, natural, segment_of):
    attn_gain, query_weight, key_matrix, value_matrix, out_weight, mlp_gain, gate_weight, up_weight, down_weight = weights
    normalized_rows = lowered_input(norm_rows(hidden, attn_gain))
    query_lin = lowered_gradient(jnp.dot(normalized_rows, query_weight, precision=highest_precision)).reshape(GROUP_TOKENS, QUERY_HEADS, HEAD_SIZE)
    query = lowered_input(rotate_heads(query_lin, cosine_table, sine_values))
    key_projected = lowered_gradient(jnp.dot(normalized_rows, key_matrix, precision=highest_precision)).reshape(GROUP_TOKENS, KEY_VALUE_HEADS, HEAD_SIZE)
    keys = lowered_input(rotate_heads(key_projected, cosine_table, sine_values))
    value_rows = lowered_input(lowered_gradient(jnp.dot(normalized_rows, value_matrix, precision=highest_precision))).reshape(GROUP_TOKENS, KEY_VALUE_HEADS, HEAD_SIZE)
    attended = lowered_input(lowered_gradient(attend_group(query, keys, value_rows, natural, segment_of)))
    middle = hidden + lowered_gradient(jnp.dot(attended, out_weight, precision=highest_precision))
    normed_mid = lowered_input(norm_rows(middle, mlp_gain))
    gate_lin = lowered_gradient(jnp.dot(normed_mid, gate_weight, precision=highest_precision))
    up_lin = lowered_gradient(jnp.dot(normed_mid, up_weight, precision=highest_precision))
    mixed = lowered_input(jax.nn.silu(gate_lin) * up_lin)
    return middle + lowered_gradient(jnp.dot(mixed, down_weight, precision=highest_precision))

def reference(tokens, cotangent, segment_ids, block_order, gain_attn, w_query, key_projection, value_projection, w_out, gain_mlp, w_gate, w_up, w_down):
    params = (gain_attn, w_query, key_projection, value_projection, w_out, gain_mlp, w_gate, w_up, w_down)
    hidden_in = tokens.astype(jnp.float32)
    seed_grad = cotangent.astype(jnp.float32)
    layouts = [token_layout(segment_ids[group_index], block_order[group_index]) for group_index in range(GROUPS)]
    tables = [rope_tables(layout[2]) for layout in layouts]

    def forward_all(parameters, hidden_all):
        weights = tuple((lowered_input(parameter) for parameter in parameters))
        outputs = []
        for group_index in range(GROUPS):
            hidden = hidden_all[group_index]
            natural, segment_of, positions = layouts[group_index]
            cosine_table, sine_values = tables[group_index]
            for repeat_index in range(REPEATS):
                hidden = block_layer(hidden, weights, cosine_table, sine_values, natural, segment_of)
            outputs.append(hidden)
        return jnp.stack(outputs)
    output, pullback = jax.vjp(forward_all, params, hidden_in)
    param_grads, input_grad = pullback(seed_grad)
    return (output.astype(jnp.bfloat16), input_grad.astype(jnp.bfloat16), param_grads[0], param_grads[1], param_grads[2], param_grads[3], param_grads[4], param_grads[5], param_grads[6], param_grads[7], param_grads[8])
```

```python
import jax
import jax.numpy as jnp
from jax import lax
from jax.sharding import PartitionSpec as P

QUERY_HEADS = 15
KEY_VALUE_HEADS = 5
HEAD_SIZE = 64
SEQS = 8
REPEATS = 2
WA = 4

epsilon = 1e-05
masked_score = -1e30
rope_base = 10000.0
bf16 = jnp.bfloat16
f32 = jnp.float32


def swap(x, mask):
    return lax.ppermute(x, "wa", [(i, i ^ mask) for i in range(WA)])


def ring_order(n):
    return [i for i in range(0, n, 2)] + [i for i in range(n - 1, 0, -2)]


def ring_shift(x, n, step):
    order = ring_order(n)
    return lax.ppermute(x, "ctx", [(order[i], order[(i + step) % n]) for i in range(n)])


def ring_position(r, n):
    return jnp.where(r % 2 == 0, r // 2, n - 1 - r // 2)


def ring_device(p, n):
    return jnp.where(p < n // 2, 2 * p, 2 * (n - 1 - p) + 1)


def ring_gather(x, n):
    half = n // 2
    rows = x.shape[0] // 2
    ahead = [x]
    behind = [x]
    for _ in range(half - 1):
        ahead.append(ring_shift(ahead[-1], n, 1))
        behind.append(ring_shift(behind[-1], n, -1))
    far = jnp.concatenate(
        [ring_shift(ahead[-1][:rows], n, 1), ring_shift(behind[-1][rows:], n, -1)], axis=0
    )
    return ahead + [far] + behind[:0:-1]


def add_low(x, y):
    return (x.astype(f32) + y.astype(f32)).astype(bf16)


def ring_scatter(piece, n):
    half = n // 2
    far = piece(half)
    rows = far.shape[0] // 2
    go = ring_shift(far[:rows], n, 1)
    back = ring_shift(far[rows:], n, -1)
    own = piece(half + 1)
    go = jnp.concatenate([add_low(own[:rows], go), own[rows:]], axis=0)
    own = piece(half - 1)
    back = jnp.concatenate([own[:rows], add_low(own[rows:], back)], axis=0)
    for k in range(half - 2, 0, -1):
        go = add_low(ring_shift(go, n, 1), piece(n - k))
        back = add_low(ring_shift(back, n, -1), piece(k))
    go = ring_shift(go, n, 1)
    back = ring_shift(back, n, -1)
    return piece(0).astype(f32) + go.astype(f32) + back.astype(f32)


def ring_all_reduce(pieces, n, position):
    def piece(k):
        return lax.dynamic_index_in_dim(pieces, (position - k) % n, 0, keepdims=False)

    mine = ring_scatter(piece, n).astype(bf16)
    gathered = ring_gather(mine, n)
    out = jnp.zeros(pieces.shape, bf16)
    for k in range(n):
        out = lax.dynamic_update_index_in_dim(out, gathered[k], (position - k) % n, 0)
    return out


def cut(x, n):
    if x.shape[0] % (2 * n) == 0:
        return x.reshape(n, x.shape[0] // n, x.shape[1])
    return x.reshape(n, -1)


def all_sum(x, n):
    for mask in (1, 2):
        x = x + swap(x, mask)
    step = 1
    while step < n:
        x = x + lax.ppermute(x, "ctx", [(i, i ^ step) for i in range(n)])
        step *= 2
    return x


def everyone(x):
    side = swap(x, 1)
    across = swap(x, 2)
    return jnp.concatenate([x, side, across, swap(across, 1)], axis=0)


def own_slices(x, w):
    rows, width = x.shape
    parts = x.reshape(rows, WA, width // WA).transpose(1, 0, 2)

    def of(mask):
        part = lax.dynamic_index_in_dim(parts, w ^ mask, 0, keepdims=False)
        return swap(part, mask) if mask else part

    return jnp.concatenate([of(m) for m in range(WA)], axis=0)


def whole_rows(x, w):
    across = swap(x, 2)
    parts = jnp.stack([x, swap(x, 1), across, swap(across, 1)])
    return jnp.concatenate(
        [lax.dynamic_index_in_dim(parts, w ^ j, 0, keepdims=False) for j in range(WA)], axis=0
    )


def in_order(first, second, flag):
    return jnp.stack([jnp.where(flag, second, first), jnp.where(flag, first, second)])


def token_layout(segment_row, order_row, blocks):
    key_count = segment_row.shape[0]
    count_of_blocks = order_row.shape[0]
    block_size = key_count // count_of_blocks
    labels = jnp.arange(count_of_blocks, dtype=jnp.int32)
    anchor = jnp.sum(jnp.where(blocks[:, None] == labels[None, :], order_row[None, :], 0), axis=1)
    natural = (
        anchor[:, None] * block_size + jnp.arange(block_size, dtype=jnp.int32)[None, :]
    ).reshape(-1)
    labels = jnp.arange(SEQS, dtype=jnp.int32)
    segment_sizes = jnp.sum((segment_row[None, :] == labels[:, None]).astype(jnp.int32), axis=1)
    segment_start = jnp.cumsum(segment_sizes) - segment_sizes
    inside = (segment_start[None, :] <= natural[:, None]).astype(jnp.int32)
    segment_of = jnp.sum(inside, axis=1) - 1
    start_of = jnp.max(jnp.where(inside > 0, segment_start[None, :], 0), axis=1)
    return (natural, segment_of, natural - start_of)


def rope_tables(positions, head_size):
    half_size = head_size // 2
    frequency = rope_base ** (-jnp.arange(half_size, dtype=jnp.float32) * 2.0 / head_size)
    angles = positions.astype(jnp.float32)[:, None] * frequency[None, :]
    cosine_table = jnp.concatenate([jnp.cos(angles), jnp.cos(angles)], axis=1)
    sine_values = jnp.concatenate([jnp.sin(angles), jnp.sin(angles)], axis=1)
    return (cosine_table[:, None, :], sine_values[:, None, :])


def rotate_heads(value_rows, cosine_table, sine_values):
    half_size = value_rows.shape[-1] // 2
    turned = jnp.concatenate([-value_rows[..., half_size:], value_rows[..., :half_size]], axis=-1)
    return value_rows * cosine_table + turned * sine_values


def inverse_rotation(grads, cosine_table, sine_values):
    half_size = grads.shape[-1] // 2
    scaled = grads * sine_values
    turned = jnp.concatenate([scaled[..., half_size:], -scaled[..., :half_size]], axis=-1)
    return grads * cosine_table + turned


def matrix_product(left, right):
    return jnp.dot(left, right, preferred_element_type=jnp.float32)


def times_transposed(left, right):
    return lax.dot_general(
        left, right, (((1,), (1,)), ((), ())), preferred_element_type=jnp.float32
    )


def weight_grad(inputs, grads):
    return lax.dot_general(
        inputs, grads, (((0,), (0,)), ((), ())), preferred_element_type=jnp.float32
    )


def norm_forward(hidden, gain):
    ratio = lax.rsqrt(jnp.mean(hidden * hidden, axis=-1, keepdims=True) + epsilon)
    return (hidden * ratio * gain, ratio)


def norm_backward(grads, hidden, ratio, gain):
    scaled = hidden * ratio
    gain_grad = jnp.sum(grads * scaled, axis=0)
    inner = grads * gain
    hidden_grad = ratio * (inner - scaled * jnp.mean(inner * scaled, axis=-1, keepdims=True))
    return (hidden_grad, gain_grad)


def masks_for(query_nat, query_seg, nat_block, seg_block):
    return (seg_block[None, :] == query_seg[:, None]) & (nat_block[None, :] <= query_nat[:, None])


def block_scores(queries, key_block, allowed, score_scale):
    raw = jnp.einsum("tkgd,skd->kgts", queries, key_block, preferred_element_type=jnp.float32)
    return jnp.where(allowed[None, None], raw * score_scale, masked_score)


def attend_forward(
    queries, blocks_of_keys, blocks_of_values, nat_blocks, seg_blocks, query_nat, query_seg
):
    number_of_tokens, heads_kv, tokens_per_group, head_size = queries.shape
    score_scale = head_size ** (-0.5)
    start_state = (
        jnp.full((heads_kv, tokens_per_group, number_of_tokens), masked_score, jnp.float32),
        jnp.zeros((heads_kv, tokens_per_group, number_of_tokens), jnp.float32),
    )

    def first_pass(state, inputs):
        key_block, nat_block, seg_block = inputs
        allowed = masks_for(query_nat, query_seg, nat_block, seg_block)
        scores = block_scores(queries, key_block, allowed, score_scale)
        largest = jnp.maximum(state[0], jnp.max(scores, axis=-1))
        weights = jnp.where(allowed[None, None], jnp.exp(scores - largest[..., None]), 0.0)
        return ((largest, state[1] * jnp.exp(state[0] - largest) + jnp.sum(weights, axis=-1)), None)

    (largest, total), ignored = lax.scan(
        first_pass, start_state, (blocks_of_keys, nat_blocks, seg_blocks)
    )
    log_total = largest + jnp.log(total)

    def second_pass(summed, inputs):
        key_block, value_block, nat_block, seg_block = inputs
        allowed = masks_for(query_nat, query_seg, nat_block, seg_block)
        scores = block_scores(queries, key_block, allowed, score_scale)
        weights = jnp.where(
            allowed[None, None], jnp.exp(scores - log_total[..., None]), 0.0
        ).astype(jnp.bfloat16)
        return (
            summed
            + jnp.einsum(
                "kgts,skd->tkgd", weights, value_block, preferred_element_type=jnp.float32
            ),
            None,
        )

    start_sum = jnp.zeros(queries.shape, jnp.float32)
    attended, ignored = lax.scan(
        second_pass, start_sum, (blocks_of_keys, blocks_of_values, nat_blocks, seg_blocks)
    )
    return (log_total, attended)


def attend_backward(
    queries,
    blocks_of_keys,
    blocks_of_values,
    nat_blocks,
    seg_blocks,
    query_nat,
    query_seg,
    log_total,
    attended,
    out_grad,
):
    head_size = queries.shape[-1]
    score_scale = head_size ** (-0.5)
    row_dots = jnp.einsum("tkgd,tkgd->kgt", out_grad.astype(jnp.float32), attended)

    def backward_step(query_sum, inputs):
        key_block, value_block, nat_block, seg_block = inputs
        allowed = masks_for(query_nat, query_seg, nat_block, seg_block)
        scores = block_scores(queries, key_block, allowed, score_scale)
        weights = jnp.where(allowed[None, None], jnp.exp(scores - log_total[..., None]), 0.0)
        weight_grads = jnp.einsum(
            "tkgd,skd->kgts", out_grad, value_block, preferred_element_type=jnp.float32
        )
        score_grad = (weights * (weight_grads - row_dots[..., None]) * score_scale).astype(
            jnp.bfloat16
        )
        query_part = query_sum + jnp.einsum(
            "kgts,skd->tkgd", score_grad, key_block, preferred_element_type=jnp.float32
        )
        key_part = jnp.einsum(
            "kgts,tkgd->skd", score_grad, queries, preferred_element_type=jnp.float32
        )
        value_part = jnp.einsum(
            "kgts,tkgd->skd",
            weights.astype(jnp.bfloat16),
            out_grad,
            preferred_element_type=jnp.float32,
        )
        return (query_part, (key_part, value_part))

    start_sum = jnp.zeros(queries.shape, jnp.float32)
    query_grad, (key_grads, value_grads) = lax.scan(
        backward_step, start_sum, (blocks_of_keys, blocks_of_values, nat_blocks, seg_blocks)
    )
    return (query_grad, key_grads, value_grads)


def forward_layer(hidden, weights, context):
    gain_attn, w_qkv, w_out, gain_mlp, w_gate, w_up, w_down = weights
    cosine, sine, query_nat, query_seg, nat_blocks, seg_blocks, w, n = context
    tokens = hidden.shape[0]
    kv_width = KEY_VALUE_HEADS * HEAD_SIZE
    q_width = QUERY_HEADS * HEAD_SIZE
    normed_pre, first_ratio = norm_forward(hidden, gain_attn)
    normed = normed_pre.astype(bf16)
    qkv = matrix_product(normed, w_qkv)
    turned = rotate_heads(
        qkv[:, : q_width + kv_width].reshape(tokens, -1, HEAD_SIZE), cosine, sine
    ).astype(bf16)
    queries = turned[:, :QUERY_HEADS].reshape(
        tokens, KEY_VALUE_HEADS, QUERY_HEADS // KEY_VALUE_HEADS, HEAD_SIZE
    )
    pair = jnp.concatenate(
        [turned[:, QUERY_HEADS:].reshape(tokens, kv_width), qkv[:, q_width + kv_width :].astype(bf16)],
        axis=1,
    )
    every = jnp.stack(ring_gather(pair, n))
    count = nat_blocks.shape[0]
    blocks_of_keys = every[:, :, :kv_width].reshape(count, -1, KEY_VALUE_HEADS, HEAD_SIZE)
    blocks_of_values = every[:, :, kv_width:].reshape(count, -1, KEY_VALUE_HEADS, HEAD_SIZE)
    log_total, attended = attend_forward(
        queries, blocks_of_keys, blocks_of_values, nat_blocks, seg_blocks, query_nat, query_seg
    )
    attended_low = attended.reshape(tokens, q_width).astype(bf16)
    middle = hidden + matrix_product(attended_low, w_out)
    normed_mid_pre, second_ratio = norm_forward(middle, gain_mlp)
    normed_mid = normed_mid_pre.astype(bf16)
    both = jnp.concatenate([normed_mid, swap(normed_mid, 1)], axis=0)
    gate_lin = matrix_product(both, w_gate)
    up_lin = matrix_product(both, w_up)
    mixed = (jax.nn.silu(gate_lin) * up_lin).astype(bf16)
    partial = matrix_product(mixed, w_down)
    result = middle + partial[:tokens] + swap(partial[tokens:], 1)
    quarter = mixed.shape[1] // 2
    halves = mixed.reshape(2 * tokens, 2, quarter)
    mine = jnp.where(w < 2, halves[:, 0], halves[:, 1])
    other = jnp.where(w < 2, halves[:, 1], halves[:, 0])
    mixed_all = jnp.concatenate([mine, swap(other, 2)], axis=0)
    kept = dict(
        hidden=hidden,
        first_ratio=first_ratio,
        queries=queries,
        keys=blocks_of_keys,
        values=blocks_of_values,
        log_total=log_total,
        attended=attended,
        middle=middle,
        second_ratio=second_ratio,
        gate_lin=gate_lin,
        up_lin=up_lin,
        normed_slices=own_slices(normed, w),
        attended_slices=own_slices(attended_low, w),
        mid_slices=own_slices(normed_mid, w),
        mixed_all=mixed_all,
    )
    return (result, kept)


def flip(x):
    rows = x.shape[0] // 2
    return jnp.concatenate([x[rows:], x[:rows]], axis=0)


def backward_layer(incoming, kept, weights, context):
    gain_attn, w_qkv, w_out, gain_mlp, w_gate, w_up, w_down = weights
    cosine, sine, query_nat, query_seg, nat_blocks, seg_blocks, w, n = context
    tokens = incoming.shape[0]
    kv_width = KEY_VALUE_HEADS * HEAD_SIZE
    q_width = QUERY_HEADS * HEAD_SIZE
    low = incoming.astype(bf16)
    side = swap(low, 1)
    across = swap(low, 2)
    both = jnp.concatenate([low, side], axis=0)
    mixed_grad = times_transposed(both, w_down)
    gate_lin = kept["gate_lin"]
    up_lin = kept["up_lin"]
    gate_sig = jax.nn.sigmoid(gate_lin)
    gate_low = (mixed_grad * up_lin * gate_sig * (1.0 + gate_lin * (1.0 - gate_sig))).astype(bf16)
    up_low = (mixed_grad * gate_lin * gate_sig).astype(bf16)
    partial = times_transposed(gate_low, w_gate) + times_transposed(up_low, w_up)
    mid_normed_grad = partial[:tokens] + swap(partial[tokens:], 1)
    mid_part, gain_mlp_grad = norm_backward(
        mid_normed_grad, kept["middle"], kept["second_ratio"], gain_mlp
    )
    middle_grad = incoming + mid_part
    low_all = jnp.concatenate([both, across, swap(across, 1)], axis=0)
    down_grad = weight_grad(kept["mixed_all"], low_all)
    pair = jnp.concatenate([gate_low, up_low], axis=1)
    pair_far = swap(pair, 2)
    mine_cols = jnp.concatenate([pair, pair_far], axis=0)
    other_cols = jnp.concatenate([flip(swap(pair, 1)), flip(swap(pair_far, 1))], axis=0)
    mine_grad = weight_grad(kept["mid_slices"], mine_cols)
    other_grad = weight_grad(kept["mid_slices"], other_cols)

    out_in = middle_grad.astype(bf16)
    attended_grad = (
        times_transposed(out_in, w_out)
        .astype(bf16)
        .reshape(tokens, KEY_VALUE_HEADS, QUERY_HEADS // KEY_VALUE_HEADS, HEAD_SIZE)
    )
    out_grad = weight_grad(kept["attended_slices"], everyone(out_in))
    query_grad, key_grads, value_grads = attend_backward(
        kept["queries"],
        kept["keys"],
        kept["values"],
        nat_blocks,
        seg_blocks,
        query_nat,
        query_seg,
        kept["log_total"],
        kept["attended"],
        attended_grad,
    )
    joined = jnp.concatenate(
        [
            key_grads.reshape(n, tokens, kv_width).astype(bf16),
            value_grads.reshape(n, tokens, kv_width).astype(bf16),
        ],
        axis=2,
    )
    summed = ring_scatter(lambda k: joined[k], n)
    heads = jnp.concatenate(
        [
            query_grad.reshape(tokens, QUERY_HEADS, HEAD_SIZE),
            summed[:, :kv_width].reshape(tokens, KEY_VALUE_HEADS, HEAD_SIZE),
        ],
        axis=1,
    )
    lin_grad = jnp.concatenate(
        [
            inverse_rotation(heads, cosine, sine).reshape(tokens, q_width + kv_width).astype(bf16),
            summed[:, kv_width:].astype(bf16),
        ],
        axis=1,
    )
    normed_grad = times_transposed(lin_grad, w_qkv)
    qkv_grad = weight_grad(kept["normed_slices"], everyone(lin_grad))
    first_part, gain_attn_grad = norm_backward(
        normed_grad, kept["hidden"], kept["first_ratio"], gain_attn
    )
    gains = jnp.stack([gain_attn_grad, gain_mlp_grad])
    return (
        middle_grad + first_part,
        (gains, qkv_grad, out_grad, mine_grad, other_grad, down_grad),
    )


def body(
    tokens,
    cotangent,
    segment_ids,
    block_order,
    gain_attn,
    w_query,
    key_projection,
    value_projection,
    w_out,
    gain_mlp,
    w_gate,
    w_up,
    w_down,
):
    n = block_order.shape[1]
    w = lax.axis_index("wa")
    core = w % 2
    row = w // 2
    position = ring_position(lax.axis_index("ctx"), n)
    blocks = ring_device((position - jnp.arange(n, dtype=jnp.int32)) % n, n)
    natural, segment_of, positions = token_layout(segment_ids[0], block_order[0], blocks)
    count = tokens.shape[1]
    cosine, sine = rope_tables(positions[:count], HEAD_SIZE)
    key_block = min(1024, natural.shape[0])
    context = (
        cosine,
        sine,
        natural[:count],
        segment_of[:count],
        natural.reshape(-1, key_block),
        segment_of.reshape(-1, key_block),
        w,
        n,
    )

    gains = jnp.stack([gain_attn, gain_mlp]).astype(bf16)
    gains = whole_rows(gains.T, w).T.astype(f32)
    qkv = jnp.concatenate([w_query, key_projection, value_projection], axis=1).astype(bf16)
    qkv_whole = whole_rows(qkv, w)
    out_whole = whole_rows(w_out.astype(bf16), w)

    rows, ff = w_gate.shape
    quarter = ff // WA
    gate_up = (
        jnp.stack([w_gate, w_up]).astype(bf16).reshape(2, rows, 2, 2, quarter).transpose(0, 2, 3, 1, 4)
    )
    keep = lax.dynamic_index_in_dim(gate_up, core, 2, keepdims=False)
    give = lax.dynamic_index_in_dim(gate_up, 1 - core, 2, keepdims=False)
    chip = in_order(keep, swap(give, 1), core == 1)
    everything = in_order(chip, swap(chip, 2), row == 1)
    everything = everything.transpose(2, 0, 1, 4, 3, 5).reshape(2, WA * rows, 2 * quarter)
    down = w_down.astype(bf16)
    down_half = in_order(down, swap(down, 2), row == 1).reshape(2 * quarter, -1)
    weights = (gains[0], qkv_whole, out_whole, gains[1], everything[0], everything[1], down_half)

    hidden = tokens[0].astype(f32)
    kept_layers = []
    for repeat_index in range(REPEATS):
        hidden, kept = forward_layer(hidden, weights, context)
        kept_layers.append(kept)
    output = hidden.astype(bf16)[None]
    grad_now = cotangent[0].astype(f32)
    totals = None
    for kept in reversed(kept_layers):
        grad_now, grads = backward_layer(grad_now, kept, weights, context)
        totals = grads if totals is None else jax.tree.map(jnp.add, totals, grads)
    input_grad = grad_now.astype(bf16)[None]

    gain_sum, qkv_grad, out_grad, mine_grad, other_grad, down_grad = totals
    gain_sum = lax.dynamic_slice_in_dim(all_sum(gain_sum, n), w * rows, rows, 1)

    def reduced(x):
        return ring_all_reduce(cut(x.astype(bf16), n), n, position).reshape(x.shape).astype(f32)

    down_total = reduced(down_grad)
    both_grad = jnp.stack([mine_grad, other_grad], axis=1).reshape(rows, n, -1)
    both_total = (
        ring_all_reduce(both_grad.transpose(1, 0, 2).astype(bf16), n, position)
        .transpose(1, 0, 2)
        .reshape(rows, 2, 2, 2, quarter)
    )
    mine_total = both_total[:, 0]
    other_total = both_total[:, 1]
    low_cols = jnp.where(core == 0, mine_total, other_total)
    high_cols = jnp.where(core == 0, other_total, mine_total)
    gate_up_total = jnp.stack([low_cols, high_cols], axis=3).reshape(rows, 2, ff).astype(f32)
    out_total = reduced(out_grad)
    qkv_total = reduced(qkv_grad)
    q_width = w_query.shape[1]
    kv_width = key_projection.shape[1]
    return (
        output,
        input_grad,
        gain_sum[0],
        qkv_total[:, :q_width],
        qkv_total[:, q_width : q_width + kv_width],
        qkv_total[:, q_width + kv_width :],
        out_total,
        gain_sum[1],
        gate_up_total[:, 0],
        gate_up_total[:, 1],
        down_total,
    )


def solution(mesh):
    rows = P("wa", None)
    return jax.shard_map(
        body,
        mesh=mesh,
        in_specs=(
            P("wa", "ctx", None),
            P("wa", "ctx", None),
            rows,
            rows,
            P("wa"),
            rows,
            rows,
            rows,
            rows,
            P("wa"),
            rows,
            rows,
            rows,
        ),
        out_specs=(
            P("wa", "ctx", None),
            P("wa", "ctx", None),
            P("wa"),
            rows,
            rows,
            rows,
            rows,
            P("wa"),
            rows,
            rows,
            rows,
        ),
        check_vma=False,
    )
```

```python
import functools

import jax
import jax.numpy as jnp
from jax import lax
from jax.experimental import pallas as pl
from jax.experimental.pallas import tpu as pltpu
from jax.sharding import PartitionSpec as P

QH = 15
KVH = 5
GQ = QH // KVH
HS = 64
SEQS = 8
REPEATS = 2
WA = 4
BLK = 128
D = 960
SL = D // WA
KV = KVH * HS
QKV = 2 * KV + D
FFQ = 640
R3 = GQ * BLK

epsilon = 1e-05
masked_score = -1e30
rope_base = 10000.0
bf16 = jnp.bfloat16
f32 = jnp.float32
i32 = jnp.int32
MB = 1 << 20


def swap(x, mask):
    return lax.ppermute(x, "wa", [(i, i ^ mask) for i in range(WA)])


def side_swap(x, n):
    return lax.ppermute(x, "ctx", [(i, i ^ 1) for i in range(n)])


def ring_order(n):
    return [i for i in range(0, n, 2)] + [i for i in range(n - 1, 0, -2)]


def ring_shift(x, n, step):
    order = ring_order(n)
    return lax.ppermute(x, "ctx", [(order[i], order[(i + step) % n]) for i in range(n)])


def ring_position(r, n):
    return jnp.where(r % 2 == 0, r // 2, n - 1 - r // 2)


def ring_device(p, n):
    return jnp.where(p < n // 2, 2 * p, 2 * (n - 1 - p) + 1)


def ring_gather(x, n):
    half = n // 2
    rows = x.shape[0] // 2
    ahead = [x]
    behind = [x]
    for _ in range(half - 1):
        ahead.append(ring_shift(ahead[-1], n, 1))
        behind.append(ring_shift(behind[-1], n, -1))
    far = jnp.concatenate(
        [ring_shift(ahead[-1][:rows], n, 1), ring_shift(behind[-1][rows:], n, -1)], axis=0
    )
    return ahead + [far] + behind[:0:-1]


def add_low(x, y):
    return (x.astype(f32) + y.astype(f32)).astype(bf16)


def ring_scatter(piece, n):
    half = n // 2
    far = piece(half)
    rows = far.shape[0] // 2
    go = ring_shift(far[:rows], n, 1)
    back = ring_shift(far[rows:], n, -1)
    own = piece(half + 1)
    go = jnp.concatenate([add_low(own[:rows], go), own[rows:]], axis=0)
    own = piece(half - 1)
    back = jnp.concatenate([own[:rows], add_low(own[rows:], back)], axis=0)
    for k in range(half - 2, 0, -1):
        go = add_low(ring_shift(go, n, 1), piece(n - k))
        back = add_low(ring_shift(back, n, -1), piece(k))
    go = ring_shift(go, n, 1)
    back = ring_shift(back, n, -1)
    return piece(0), go, back


def ring_sum(pieces, n, position):
    def piece(k):
        return lax.dynamic_index_in_dim(pieces, (position - k) % n, 0, keepdims=False)

    own, go, back = ring_scatter(piece, n)
    mine = (own.astype(f32) + go.astype(f32) + back.astype(f32)).astype(bf16)
    return ring_gather(mine, n)


def placed(gathered, n, position):
    out = jnp.zeros((n,) + gathered[0].shape, bf16)
    for k in range(n):
        out = lax.dynamic_update_index_in_dim(out, gathered[k], (position - k) % n, 0)
    return out


def all_sum(x, n):
    for mask in (1, 2):
        x = x + swap(x, mask)
    step = 1
    while step < n:
        x = x + lax.ppermute(x, "ctx", [(i, i ^ step) for i in range(n)])
        step *= 2
    return x


def everyone(x):
    side = swap(x, 1)
    across = swap(x, 2)
    return [x, side, across, swap(across, 1)]


def own_slices(chunks, w):
    out = []
    for mask in range(WA):
        part = jnp.stack(
            [lax.dynamic_index_in_dim(c, w ^ mask, 0, keepdims=False) for c in chunks]
        )
        out.append(swap(part, mask) if mask else part)
    return out


VMEM = pl.BlockSpec(memory_space=pltpu.VMEM)
SMEM = pl.BlockSpec(memory_space=pltpu.SMEM)


def call(body, name, n_scalar, ins, outs, scratch=(), flops=0, limit=40):
    size = sum(x.size * x.dtype.itemsize for x in list(ins) + list(outs))
    return pl.pallas_call(
        body,
        name=name,
        in_specs=[SMEM] * n_scalar + [VMEM] * (len(ins) - n_scalar),
        out_specs=[VMEM] * len(outs),
        out_shape=list(outs),
        scratch_shapes=list(scratch),
        cost_estimate=pl.CostEstimate(flops=flops, transcendentals=0, bytes_accessed=size),
        compiler_params=pltpu.CompilerParams(vmem_limit_bytes=limit * MB),
    )(*ins)


def shape(dims, dtype):
    return jax.ShapeDtypeStruct(dims, dtype)


def mm(a, b):
    return jnp.dot(a, b, preferred_element_type=f32)


def nt(a, b):
    return lax.dot_general(a, b, (((1,), (1,)), ((), ())), preferred_element_type=f32)


def tn(a, b):
    return lax.dot_general(a, b, (((0,), (0,)), ((), ())), preferred_element_type=f32)


def turn(u):
    lane = lax.broadcasted_iota(i32, u.shape, 1) % HS
    return jnp.where(lane < HS // 2, -pltpu.roll(u, 128 - HS // 2, 1), pltpu.roll(u, HS // 2, 1))


def turn_back(u):
    lane = lax.broadcasted_iota(i32, u.shape, 1) % HS
    return jnp.where(lane < HS // 2, pltpu.roll(u, 128 - HS // 2, 1), -pltpu.roll(u, HS // 2, 1))


def rope(u, cos, sin):
    return u * cos + turn(u) * sin


def rope_back(u, cos, sin):
    return u * cos + turn_back(u * sin)


def head_only(tables):
    cos, sin = tables
    lane = lax.broadcasted_iota(i32, cos.shape, 1)
    return jnp.where(lane < HS, cos, 1.0), jnp.where(lane < HS, sin, 0.0)


def project_body(n_in, sc, *refs):
    xs = refs[:n_in]
    gain, cos_ref, sin_ref, p0, p1, p2, p3 = refs[n_in : n_in + 7]
    x_ref, a4, q3, kv, acc_ref = refs[n_in + 7 :]
    x = xs[0][...].astype(f32)
    for r in xs[1:]:
        x = x + r[...]
    x_ref[...] = x
    ratio = lax.rsqrt(jnp.mean(x * x, axis=1, keepdims=True) + epsilon)
    a = (x * ratio * gain[...]).astype(bf16)
    for j in range(WA):
        a4[j] = a[:, SL * j : SL * (j + 1)]
    acc = None
    for m, p in enumerate((p0, p1, p2, p3)):
        part = mm(a4[sc[0] ^ m], p[...])
        acc = part if acc is None else acc + part
    acc_ref[:, :QKV] = acc
    cos, sin = cos_ref[...], sin_ref[...]
    edge = head_only((cos, sin))
    for i in range(2):
        kv[:, 128 * i : 128 * (i + 1)] = rope(acc_ref[:, 128 * i : 128 * (i + 1)], cos, sin).astype(bf16)
    kv[:, 256:384] = rope(acc_ref[:, 256:384], *edge).astype(bf16)
    kv[:, 384:640] = acc_ref[:, 384:640].astype(bf16)
    for i in range(8):
        lo = 2 * KV + 128 * i
        u = rope(acc_ref[:, lo : lo + 128], cos, sin).astype(bf16) * bf16(0.125)
        for j in range(2):
            h = 2 * i + j
            if h < QH:
                q3[h // GQ, BLK * (h % GQ) : BLK * (h % GQ + 1), :] = u[:, HS * j : HS * (j + 1)]


def project(scal, xs, gain, tables, parts):
    return call(
        functools.partial(project_body, len(xs)),
        "project",
        1,
        [scal, *xs, gain, *tables, *parts],
        [
            shape((BLK, D), f32),
            shape((WA, BLK, SL), bf16),
            shape((KVH, R3, HS), bf16),
            shape((BLK, 2 * KV), bf16),
        ],
        [pltpu.VMEM((BLK, QKV + 64), f32)],
        flops=2 * BLK * D * QKV,
    )


def list_blocks(sched, lst, n):
    def step(k, count):
        first = sched[k] * BLK
        seen = (sched[k] <= sched[0]) & (first + BLK > sched[n])

        @pl.when(seen)
        def _():
            lst[count] = k

        return count + seen.astype(i32)

    return lax.fori_loop(0, n, step, jnp.int32(0))


def block_bias(sched, qinfo, k):
    key = sched[k] * BLK + lax.broadcasted_iota(i32, (BLK, R3), 0)
    ok = (key <= qinfo[0:1, :]) & (key >= qinfo[1:2, :])
    return jnp.where(ok, 0.0, masked_score).astype(f32)


def attend_body(n, sc, sched, qinfo, q3, kv, x, gain, p0, p1, p2, p3, *refs):
    ol4, o_t, lse, m_ref, b_ref, b4, lst, s_scr, bias, o_scr = refs
    count = list_blocks(sched, lst, n)

    @pl.loop(0, count)
    def _(i):
        bias[i] = block_bias(sched, qinfo, lst[i])

    for h in range(KVH):
        q = q3[h]

        def first(i, top):
            keys = kv[lst[i], :, HS * h : HS * (h + 1)]
            s = nt(keys, q) + bias[i]
            s_scr[i] = s
            return jnp.maximum(top, jnp.max(s.reshape(BLK // 8, 8, R3), axis=0))

        top = lax.fori_loop(0, count, first, jnp.full((8, R3), masked_score, f32))
        top = jnp.max(top, axis=0, keepdims=True)

        def second(i, state):
            total, out = state
            p = jnp.exp(s_scr[i] - top)
            total = total + jnp.sum(p.reshape(BLK // 8, 8, R3), axis=0)
            values = kv[lst[i], :, KV + HS * h : KV + HS * (h + 1)]
            return total, out + tn(values, p.astype(bf16))

        total, out = lax.fori_loop(
            0, count, second, (jnp.zeros((8, R3), f32), jnp.zeros((HS, R3), f32))
        )
        total = jnp.sum(total, axis=0, keepdims=True)
        out = out * (1.0 / total)
        o_t[h] = out
        lse[h : h + 1, :] = top + jnp.log(total)
        rows = out.T
        for g in range(GQ):
            j = GQ * h + g
            o_scr[:, HS * j : HS * (j + 1)] = rows[BLK * g : BLK * (g + 1), :]
    low = o_scr[...].astype(bf16)
    for j in range(WA):
        ol4[j] = low[:, SL * j : SL * (j + 1)]
    m = x[...]
    for k, p in enumerate((p0, p1, p2, p3)):
        m = m + mm(ol4[sc[0] ^ k], p[...])
    m_ref[...] = m
    ratio = lax.rsqrt(jnp.mean(m * m, axis=1, keepdims=True) + epsilon)
    b = (m * ratio * gain[...]).astype(bf16)
    b_ref[...] = b
    for j in range(WA):
        b4[j] = b[:, SL * j : SL * (j + 1)]


def attend(scal, sched, qinfo, q3, kv, x, gain, parts):
    n = kv.shape[0]
    return call(
        functools.partial(attend_body, n),
        "attend",
        2,
        [scal, sched, qinfo, q3, kv, x, gain, *parts],
        [
            shape((WA, BLK, SL), bf16),
            shape((KVH, HS, R3), f32),
            shape((8, R3), f32),
            shape((BLK, D), f32),
            shape((BLK, D), bf16),
            shape((WA, BLK, SL), bf16),
        ],
        [
            pltpu.SMEM((n,), i32),
            pltpu.VMEM((n, BLK, R3), f32),
            pltpu.VMEM((n, BLK, R3), f32),
            pltpu.VMEM((BLK, D), f32),
        ],
        flops=2 * BLK * D * D + 4 * BLK * D * 6 * BLK,
        limit=24 if n <= 8 else 60,
    )


def hidden_units(sc, chunk_of, keep, core, y_mine, y_other, which, j, is_mine):
    pass


def mlp_body(sc, b_own, b_side, keep, core, ym, yo, d_own, d_far, *refs):
    z_ref, gu_ref, y_own, y_side, bs = refs
    w = sc[0]
    for half, b in enumerate((b_own, b_side)):
        for j in range(WA):
            bs[j, BLK * half : BLK * (half + 1), :] = b[:, SL * j : SL * (j + 1)]
    for t, far in ((sc[1], ym), (1 - sc[1], yo)):
        lin = []
        for gu in range(2):
            acc = mm(bs[w], keep[gu, t]) + mm(bs[w ^ 1], core[gu, t])
            acc = acc + mm(bs[w ^ 2], far[gu, 0]) + mm(bs[w ^ 3], far[gu, 1])
            gu_ref[gu, t] = acc
            lin.append(acc)
        gate, up = lin
        z_ref[t] = (gate / (1.0 + jnp.exp(-gate)) * up).astype(bf16)
    row = sc[2]
    out = mm(z_ref[row], d_own[...]) + mm(z_ref[1 - row], d_far[...])
    y_own[...] = out[:BLK]
    y_side[...] = out[BLK:]


def mlp(scal, b_own, b_side, wts):
    return call(
        mlp_body,
        "mlp",
        1,
        [scal, b_own, b_side, *wts],
        [
            shape((2, 2 * BLK, FFQ), bf16),
            shape((2, 2, 2 * BLK, FFQ), f32),
            shape((BLK, D), f32),
            shape((BLK, D), f32),
        ],
        [pltpu.VMEM((WA, 2 * BLK, SL), bf16)],
        flops=2 * 2 * BLK * 3 * D * 2 * FFQ,
        limit=56,
    )


def mlp_back_body(sc, l_own, l_side, gu_ref, keep, core, ym, yo, d_own, d_far, *refs):
    pair, db_own, db_side, low, acc = refs
    w, row = sc[0], sc[2]
    low[:BLK] = l_own[...]
    low[BLK:] = l_side[...]
    for first, (t, far) in enumerate(((sc[1], ym), (1 - sc[1], yo))):
        ds = []
        dz = jnp.where(t == row, nt(low[...], d_own[...]), nt(low[...], d_far[...]))
        gate, up = gu_ref[0, t], gu_ref[1, t]
        sig = 1.0 / (1.0 + jnp.exp(-gate))
        dg = (dz * up * sig * (1.0 + gate * (1.0 - sig))).astype(bf16)
        du = (dz * gate * sig).astype(bf16)
        lo = pl.multiple_of(t * FFQ, 128)
        pair[:, pl.ds(lo, FFQ)] = dg
        lo = pl.multiple_of(t * FFQ + 2 * FFQ, 128)
        pair[:, pl.ds(lo, FFQ)] = du
        for j, p in ((w, keep.at[0, t]), (w ^ 1, core.at[0, t]), (w ^ 2, far.at[0, 0]), (w ^ 3, far.at[0, 1])):
            part = nt(dg, p[...])
            acc[j] = part if first == 0 else acc[j] + part
        for j, p in ((w, keep.at[1, t]), (w ^ 1, core.at[1, t]), (w ^ 2, far.at[1, 0]), (w ^ 3, far.at[1, 1])):
            acc[j] = acc[j] + nt(du, p[...])
    for j in range(WA):
        db_own[:, SL * j : SL * (j + 1)] = acc[j, :BLK, :]
        db_side[:, SL * j : SL * (j + 1)] = acc[j, BLK:, :]


def mlp_back(scal, l_own, l_side, gu, wts):
    return call(
        mlp_back_body,
        "mlp_back",
        1,
        [scal, l_own, l_side, gu, *wts],
        [shape((2 * BLK, 4 * FFQ), bf16), shape((BLK, D), f32), shape((BLK, D), f32)],
        [pltpu.VMEM((2 * BLK, D), bf16), pltpu.VMEM((WA, 2 * BLK, SL), f32)],
        flops=2 * 2 * BLK * 3 * D * 2 * FFQ,
        limit=56,
    )


def norm_back(grads, hidden, gain):
    ratio = lax.rsqrt(jnp.mean(hidden * hidden, axis=1, keepdims=True) + epsilon)
    scaled = hidden * ratio
    gain_grad = jnp.sum(grads * scaled, axis=0, keepdims=True)
    inner = grads * gain
    out = ratio * (inner - scaled * jnp.mean(inner * scaled, axis=1, keepdims=True))
    return out, gain_grad


def attend_back_body(n, sc, sched, qinfo, dy, db_own, db_got, m, gain, p0, p1, p2, p3, q3, kv, o_t, lse, cos_ref, sin_ref, *refs):
    dm_ref, dml_ref, gg, dq_ref, dkv_ref, lst, do3, d_scr, dq_scr = refs
    count = list_blocks(sched, lst, n)
    part, gain_grad = norm_back(db_own[...] + db_got[...], m[...], gain[...])
    gg[...] = gain_grad
    dm = dy[...].astype(f32) + part
    dm_ref[...] = dm
    dml = dm.astype(bf16)
    dml_ref[...] = dml
    for k, p in enumerate((p0, p1, p2, p3)):
        d_scr[sc[0] ^ k] = nt(dml, p[...]).astype(bf16).astype(f32)
    whole = jnp.concatenate([d_scr[j] for j in range(WA)], axis=1)
    for j in range(QH):
        do3[j // GQ, BLK * (j % GQ) : BLK * (j % GQ + 1), :] = whole[:, HS * j : HS * (j + 1)].astype(bf16)

    @pl.loop(1, n)
    def _(k):
        seen = (sched[k] <= sched[0]) & (sched[k] * BLK + BLK > sched[n])

        @pl.when(jnp.logical_not(seen))
        def _():
            dkv_ref[k] = jnp.zeros((BLK, 2 * KV), bf16)

    for h in range(KVH):
        q = q3[h]
        do = do3[h]
        delta = jnp.sum(do.astype(f32).T * o_t[h], axis=0, keepdims=True)
        log_total = lse[h : h + 1, :]

        def step(i, dq):
            k = lst[i]
            keys = kv[k, :, HS * h : HS * (h + 1)]
            values = kv[k, :, KV + HS * h : KV + HS * (h + 1)]
            s = nt(keys, q) + block_bias(sched, qinfo, k)
            p = jnp.exp(s - log_total)
            ds = (p * (nt(values, do) - delta)).astype(bf16)
            dkv_ref[k, :, HS * h : HS * (h + 1)] = mm(ds, q).astype(bf16)
            dkv_ref[k, :, KV + HS * h : KV + HS * (h + 1)] = mm(p.astype(bf16), do).astype(bf16)
            return dq + tn(keys, ds)

        dq = lax.fori_loop(0, count, step, jnp.zeros((HS, R3), f32))
        rows = (dq * 0.125).T
        for g in range(GQ):
            j = GQ * h + g
            dq_scr[:, HS * j : HS * (j + 1)] = rows[BLK * g : BLK * (g + 1), :]
    cos, sin = cos_ref[...], sin_ref[...]
    for i in range(8):
        u = rope_back(dq_scr[:, 128 * i : 128 * (i + 1)], cos, sin).astype(bf16)
        if i < 7:
            dq_ref[:, 128 * i : 128 * (i + 1)] = u
        else:
            dq_ref[:, 128 * i :] = u[:, :HS]


def attend_back(scal, sched, qinfo, dy, db_own, db_got, m, gain, parts, q3, kv, o_t, lse, tables):
    n = kv.shape[0]
    return call(
        functools.partial(attend_back_body, n),
        "attend_back",
        2,
        [scal, sched, qinfo, dy, db_own, db_got, m, gain, *parts, q3, kv, o_t, lse, *tables],
        [
            shape((BLK, D), f32),
            shape((BLK, D), bf16),
            shape((1, D), f32),
            shape((BLK, D), bf16),
            shape((n, BLK, 2 * KV), bf16),
        ],
        [
            pltpu.SMEM((n,), i32),
            pltpu.VMEM((KVH, R3, HS), bf16),
            pltpu.VMEM((WA, BLK, SL), f32),
            pltpu.VMEM((BLK, D + 64), f32),
        ],
        flops=2 * BLK * D * D + 10 * BLK * D * 6 * BLK,
        limit=24 if n <= 8 else 60,
    )


def query_back_body(sc, dq, p0, p1, p2, p3, da):
    for k, p in enumerate((p0, p1, p2, p3)):
        da[sc[0] ^ k] = nt(dq[...], p[:, 2 * KV :])


def query_back(scal, dq, parts):
    return call(
        query_back_body,
        "query_back",
        1,
        [scal, dq, *parts],
        [shape((WA, BLK, SL), f32)],
        flops=2 * BLK * D * D,
    )[0]


def project_back_body(sc, own, go, back, cos_ref, sin_ref, da, p0, p1, p2, p3, x, dm, gain, *refs):
    dkv_ref, dx_ref, dxl_ref, gg, d4 = refs
    total = own[...].astype(f32) + go[...].astype(f32) + back[...].astype(f32)
    cos, sin = cos_ref[...], sin_ref[...]
    edge = head_only((cos, sin))
    for i in range(2):
        dkv_ref[:, 128 * i : 128 * (i + 1)] = rope_back(total[:, 128 * i : 128 * (i + 1)], cos, sin).astype(bf16)
    dkv_ref[:, 256:384] = rope_back(total[:, 256:384], *edge).astype(bf16)
    dkv_ref[:, 384:] = total[:, 384:].astype(bf16)
    for k, p in enumerate((p0, p1, p2, p3)):
        d4[sc[0] ^ k] = da[sc[0] ^ k] + nt(dkv_ref[...], p[:, : 2 * KV])
    grads = jnp.concatenate([d4[j] for j in range(WA)], axis=1)
    part, gain_grad = norm_back(grads, x[...], gain[...])
    gg[...] = gain_grad
    dx = dm[...] + part
    dx_ref[...] = dx
    dxl_ref[...] = dx.astype(bf16)


def project_back(scal, addends, tables, da, parts, x, dm, gain):
    return call(
        project_back_body,
        "project_back",
        1,
        [scal, *addends, *tables, da, *parts, x, dm, gain],
        [
            shape((BLK, 2 * KV), bf16),
            shape((BLK, D), f32),
            shape((BLK, D), bf16),
            shape((1, D), f32),
        ],
        [pltpu.VMEM((WA, BLK, SL), f32)],
        flops=2 * BLK * D * 2 * KV,
    )


def grad_rows_body(kind, n_low, has_prev, *refs):
    slices = refs[:WA]
    lows = refs[WA : WA + n_low]
    per = n_low // WA
    rest = refs[WA + n_low :]
    out = rest[-1]
    lo = 0
    for t in range(per):
        acc = None
        for m in range(WA):
            part = tn(slices[m][kind], lows[per * m + t][...])
            acc = part if acc is None else acc + part
        width = acc.shape[1]
        if has_prev:
            acc = acc + rest[0][:, lo : lo + width]
            out[:SL, lo : lo + width] = acc.astype(bf16)
        else:
            out[:, lo : lo + width] = acc
        lo += width
    if has_prev:
        out[SL:, :] = jnp.zeros((256 - SL, lo), bf16)


def grad_rows(kind, slices, lows, prev):
    flat = [x for group in lows for x in group]
    cols = sum(x.shape[1] for x in lows[0])
    has_prev = prev is not None
    return call(
        functools.partial(grad_rows_body, kind, len(flat), has_prev),
        "grad_rows",
        0,
        [*slices, *flat] + ([prev] if has_prev else []),
        [shape((256, cols), bf16) if has_prev else shape((SL, cols), f32)],
        flops=2 * WA * BLK * SL * cols,
    )[0]


def grad_gate_body(kind, has_prev, s0, s1, s2, s3, own, side, far, diag, *refs):
    out = refs[-1]
    slices = (s0, s1, s2, s3)
    for t in range(8):
        near, off = (own, far) if t < 4 else (side, diag)
        flip = 0 if t < 4 else 1
        lo = FFQ * (t % 4)
        acc = None
        for m in range(WA):
            src = near if m < 2 else off
            r = BLK * ((m % 2) ^ flip)
            part = tn(slices[m][kind], src[r : r + BLK, lo : lo + FFQ])
            acc = part if acc is None else acc + part
        if has_prev:
            acc = acc + refs[0][t]
        out[t] = acc.astype(out.dtype)


def grad_gate(kind, slices, pairs, prev):
    has_prev = prev is not None
    return call(
        functools.partial(grad_gate_body, kind, has_prev),
        "grad_gate",
        0,
        [*slices, *pairs] + ([prev] if has_prev else []),
        [shape((8, SL, FFQ), bf16 if has_prev else f32)],
        flops=2 * WA * BLK * SL * 8 * FFQ,
        limit=48,
    )[0]


def grad_down_body(has_prev, sc, z, z_far, l0, l1, l2, l3, *refs):
    out = refs[-1]
    acc = tn(z[sc[2], :BLK], l0[...]) + tn(z[sc[2], BLK:], l1[...])
    acc = acc + tn(z_far[:BLK], l2[...]) + tn(z_far[BLK:], l3[...])
    if has_prev:
        acc = acc + refs[0][...]
    out[...] = acc.astype(out.dtype)


def grad_down(scal, z, z_far, lows, prev):
    has_prev = prev is not None
    return call(
        functools.partial(grad_down_body, has_prev),
        "grad_down",
        1,
        [scal, z, z_far, *lows] + ([prev] if has_prev else []),
        [shape((FFQ, D), bf16 if has_prev else f32)],
        flops=2 * WA * BLK * FFQ * D,
        limit=32,
    )[0]


def finish_gate_body(n, sc, *refs):
    gate, up = refs[n], refs[n + 1]
    position, core = sc[3], sc[4]
    for k in range(n):
        p = (position - k + n) % n
        low = jnp.where(p < 4, core, 1 - core)
        lo = pl.multiple_of(FFQ * (2 * (p % 2) + low), 128)
        is_up = (p // 2) % 2

        @pl.when(is_up == 0)
        def _():
            gate[:, pl.ds(lo, FFQ)] = refs[k][...].astype(f32)

        @pl.when(is_up == 1)
        def _():
            up[:, pl.ds(lo, FFQ)] = refs[k][...].astype(f32)


def finish_gate(scal, gathered):
    return call(
        functools.partial(finish_gate_body, len(gathered)),
        "finish_gate",
        1,
        [scal, *gathered],
        [shape((SL, 4 * FFQ), f32)] * 2,
    )


def finish_rows_body(n, widths, sc, *refs):
    outs = refs[n:]
    for k in range(n):
        p = (sc[3] - k + n) % n
        rows = refs[k].shape[0]
        tail = SL - rows * (n - 1)
        first = pl.multiple_of(p * rows, 8)

        @pl.when(p < n - 1)
        def _():
            lo = 0
            for out, width in zip(outs, widths):
                out[pl.ds(first, rows), :] = refs[k][:, lo : lo + width].astype(f32)
                lo += width

        @pl.when(p == n - 1)
        def _():
            lo = 0
            for out, width in zip(outs, widths):
                out[rows * (n - 1) :, :] = refs[k][:tail, lo : lo + width].astype(f32)
                lo += width


def finish_rows(scal, gathered, widths):
    return call(
        functools.partial(finish_rows_body, len(gathered), tuple(widths)),
        "finish_rows",
        1,
        [scal, *gathered],
        [shape((SL, width), f32) for width in widths],
    )


def token_layout(segment_row, order_row, block_size):
    labels = jnp.arange(SEQS, dtype=i32)
    segment_sizes = jnp.sum((segment_row[None, :] == labels[:, None]).astype(i32), axis=1)
    segment_start = jnp.cumsum(segment_sizes) - segment_sizes
    return segment_start


def body(
    tokens,
    cotangent,
    segment_ids,
    block_order,
    gain_attn,
    w_query,
    key_projection,
    value_projection,
    w_out,
    gain_mlp,
    w_gate,
    w_up,
    w_down,
):
    n = block_order.shape[1]
    w = lax.axis_index("wa")
    r = lax.axis_index("ctx")
    core = w % 2
    row = w // 2
    position = ring_position(r, n)
    x_side = r % 2
    scal = jnp.stack([w, x_side, row, position, core]).astype(i32)

    qkv_own = jnp.concatenate([key_projection, value_projection, w_query], axis=1).astype(bf16)
    gains_own = jnp.stack([gain_attn, gain_mlp])
    qkv_across = swap(qkv_own, 2)
    qkv_side = swap(qkv_own, 1)
    qkv_parts = [qkv_own, qkv_side, qkv_across, swap(qkv_across, 1)]
    gains_parts = jnp.stack(everyone(gains_own.astype(bf16)))
    gains = jnp.concatenate(
        [lax.dynamic_index_in_dim(gains_parts, w ^ j, 0, keepdims=False) for j in range(WA)], axis=1
    ).astype(f32)
    gain_a, gain_m = gains[0:1], gains[1:2]

    blocks = ring_device((position - jnp.arange(n, dtype=i32)) % n, n)
    labels = jnp.arange(n, dtype=i32)
    order_row = block_order[0]
    anchors = jnp.sum(jnp.where(blocks[:, None] == labels[None, :], order_row[None, :], 0), axis=1)
    natural = anchors[0] * BLK + jnp.arange(BLK, dtype=i32)
    seg_labels = jnp.arange(SEQS, dtype=i32)
    sizes = jnp.sum((segment_ids[0][None, :] == seg_labels[:, None]).astype(i32), axis=1)
    before = (seg_labels[None, :] < seg_labels[:, None]).astype(i32)
    starts = jnp.sum(before * sizes[None, :], axis=1)
    start_of = jnp.max(jnp.where(starts[None, :] <= natural[:, None], starts[None, :], 0), axis=1)
    sched = jnp.concatenate([anchors, start_of[:1]]).astype(i32)
    qinfo = jnp.pad(
        jnp.stack([jnp.tile(natural, GQ), jnp.tile(start_of, GQ)]), ((0, 6), (0, 0))
    ).astype(i32)
    frequency = rope_base ** (-jnp.arange(HS // 2, dtype=f32) * 2.0 / HS)
    angles = (natural - start_of).astype(f32)[:, None] * frequency[None, :]
    tables = (jnp.tile(jnp.cos(angles), (1, 4)), jnp.tile(jnp.sin(angles), (1, 4)))

    out_parts = everyone(w_out.astype(bf16))
    gate_up = jnp.stack([w_gate, w_up]).astype(bf16).reshape(2, SL, 2, 2, FFQ).transpose(3, 0, 2, 1, 4)
    keep = lax.dynamic_index_in_dim(gate_up, core, 0, keepdims=False)
    core_part = swap(lax.dynamic_index_in_dim(gate_up, 1 - core, 0, keepdims=False), 1)
    give = jnp.stack(
        [
            lax.dynamic_index_in_dim(keep, x_side, 1, keepdims=False),
            lax.dynamic_index_in_dim(core_part, x_side, 1, keepdims=False),
        ],
        axis=1,
    )
    y_mine = swap(give, 2)
    y_other = side_swap(y_mine, n)
    down_own = w_down.astype(bf16)
    down_far = swap(down_own, 2)
    ff_parts = [keep, core_part, y_mine, y_other, down_own, down_far]

    xs = [tokens[0]]
    kept = []
    for repeat_index in range(REPEATS):
        x, a4, q3, kv = project(scal, xs, gain_a, tables, qkv_parts)
        every = jnp.stack(ring_gather(kv, n))
        ol4, o_t, lse, m, b, b4 = attend(scal, sched, qinfo, q3, every, x, gain_m, out_parts)
        z, gu, y_own, y_side = mlp(scal, b, swap(b, 1), ff_parts)
        xs = [m, y_own, swap(y_side, 1)]
        slices = own_slices([a4, ol4, b4], w)
        z_far = swap(lax.dynamic_index_in_dim(z, 1 - row, 0, keepdims=False), 2)
        kept.append((x, q3, every, o_t, lse, m, gu, z, z_far, slices))
    output = (xs[0] + xs[1] + xs[2]).astype(bf16)[None]

    dy = cotangent[0]
    low = cotangent[0]
    prev = [None] * 4
    gain_sums = []
    for x, q3, every, o_t, lse, m, gu, z, z_far, slices in reversed(kept):
        low_side = swap(low, 1)
        pair, db_own, db_side = mlp_back(scal, low, low_side, gu, ff_parts)
        db_got = swap(db_side, 1)
        low_far = swap(low, 2)
        lows = [low, low_side, low_far, swap(low_far, 1)]
        down_grad = grad_down(scal, z, z_far, lows, prev[0])
        pair_far = swap(pair, 2)
        pairs = [pair, swap(pair, 1), pair_far, swap(pair_far, 1)]
        gate_grad = grad_gate(2, slices, pairs, prev[1])
        dm, dml, gain_m_grad, dq, dkv = attend_back(
            scal, sched, qinfo, dy, db_own, db_got, m, gain_m, out_parts, q3, every, o_t, lse, tables
        )
        addends = ring_scatter(lambda k: dkv[k], n)
        da = query_back(scal, dq, qkv_parts)
        dkv0, dx, low, gain_a_grad = project_back(
            scal, addends, tables, da, qkv_parts, x, dm, gain_a
        )
        dy = dx
        out_grad = grad_rows(1, slices, [[t] for t in everyone(dml)], prev[2])
        dqs = everyone(dq)
        dkvs = everyone(dkv0)
        qkv_grad = grad_rows(0, slices, [[dkvs[i], dqs[i]] for i in range(WA)], prev[3])
        prev = [down_grad, gate_grad, out_grad, qkv_grad]
        gain_sums.append(jnp.concatenate([gain_a_grad, gain_m_grad], axis=0))
    input_grad = low[None]
    down_grad, gate_grad, out_grad, qkv_grad = prev

    gain_sum = lax.dynamic_slice_in_dim(all_sum(gain_sums[0] + gain_sums[1], n), w * SL, SL, 1)
    down_total = placed(
        ring_sum(down_grad.reshape(n, FFQ // n, D), n, position), n, position
    ).reshape(FFQ, D).astype(f32)
    gate_all = ring_sum(gate_grad.reshape(n, SL * 8 // n, FFQ), n, position)
    out_all = ring_sum(out_grad.reshape(n, 256 // n, D), n, position)
    qkv_all = ring_sum(qkv_grad.reshape(n, 256 // n, QKV), n, position)
    if n == 8:
        gate_total, up_total = finish_gate(scal, gate_all)
        (out_total,) = finish_rows(scal, out_all, [D])
        key_total, value_total, query_total = finish_rows(scal, qkv_all, [KV, KV, D])
    else:
        whole = placed(gate_all, n, position).reshape(2, 2, 2, SL, FFQ)
        low_half = jnp.where(core == 0, whole[0], whole[1])
        high_half = jnp.where(core == 0, whole[1], whole[0])
        gate_up_total = (
            jnp.stack([low_half, high_half], axis=2).transpose(0, 3, 1, 2, 4).reshape(2, SL, -1).astype(f32)
        )
        gate_total, up_total = gate_up_total[0], gate_up_total[1]
        out_total = placed(out_all, n, position).reshape(256, D)[:SL].astype(f32)
        qkv_total = placed(qkv_all, n, position).reshape(256, QKV)[:SL].astype(f32)
        key_total, value_total, query_total = (
            qkv_total[:, :KV],
            qkv_total[:, KV : 2 * KV],
            qkv_total[:, 2 * KV :],
        )
    return (
        output,
        input_grad,
        gain_sum[0],
        query_total,
        key_total,
        value_total,
        out_total,
        gain_sum[1],
        gate_total,
        up_total,
        down_total,
    )


def solution(mesh):
    rows = P("wa", None)
    flat = P("wa")
    act = P("wa", "ctx", None)
    return jax.shard_map(
        body,
        mesh=mesh,
        in_specs=(act, act, rows, rows, flat, rows, rows, rows, rows, flat, rows, rows, rows),
        out_specs=(act, act, flat, rows, rows, rows, rows, flat, rows, rows, rows),
        check_vma=False,
    )
```

```python
import functools

import jax
import jax.numpy as jnp
from jax import lax
from jax.experimental import pallas as pl
from jax.experimental.pallas import tpu as pltpu
from jax.sharding import PartitionSpec as P

QH = 15
KVH = 5
GQ = QH // KVH
HS = 64
SEQS = 8
REPEATS = 2
WA = 4
BLK = 128
D = 960
SL = D // WA
KV = KVH * HS
QKV = 2 * KV + D
FFQ = 640
R3 = GQ * BLK

epsilon = 1e-05
masked_score = -1e30
rope_base = 10000.0
bf16 = jnp.bfloat16
f32 = jnp.float32
i32 = jnp.int32
MB = 1 << 20


def swap(x, mask):
    return lax.ppermute(x, "wa", [(i, i ^ mask) for i in range(WA)])


def side_swap(x, n):
    return lax.ppermute(x, "ctx", [(i, i ^ 1) for i in range(n)])


def ring_order(n):
    return [i for i in range(0, n, 2)] + [i for i in range(n - 1, 0, -2)]


def ring_shift(x, n, step):
    order = ring_order(n)
    return lax.ppermute(x, "ctx", [(order[i], order[(i + step) % n]) for i in range(n)])


def ring_position(r, n):
    return jnp.where(r % 2 == 0, r // 2, n - 1 - r // 2) if n == 8 else r


def ring_device(p, n):
    return jnp.where(p < n // 2, 2 * p, 2 * (n - 1 - p) + 1) if n == 8 else p


def after(x, *others):
    return lax.optimization_barrier((x,) + others)[0]


def bar(*xs):
    return lax.optimization_barrier(xs)


def by_distance(x, n, position):
    return jnp.take(x, (position - jnp.arange(n, dtype=i32)) % n, axis=0)


def ring_gather(x, n, position):
    if n != 8:
        return by_distance(lax.all_gather(x, "ctx"), n, position)
    half = n // 2
    rows = x.shape[0] // 2
    ahead = [x]
    behind = [x]
    for _ in range(half - 1):
        ahead.append(ring_shift(ahead[-1], n, 1))
        behind.append(ring_shift(behind[-1], n, -1))
    far = jnp.concatenate(
        [ring_shift(ahead[-1][:rows], n, 1), ring_shift(behind[-1][rows:], n, -1)], axis=0
    )
    return ahead + [far] + behind[:0:-1]


def add_low(x, y):
    return (x.astype(f32) + y.astype(f32)).astype(bf16)


def ring_far(piece, n):
    far = piece(n // 2)
    rows = far.shape[0] // 2
    return ring_shift(far[:rows], n, 1), ring_shift(far[rows:], n, -1)


def ring_near(piece, n, k, go, back):
    ahead, behind = piece(n - k), piece(k)
    if go.shape != ahead.shape:
        rows = go.shape[0]
        go = jnp.concatenate([add_low(ahead[:rows], go), ahead[rows:]], axis=0)
        back = jnp.concatenate([behind[:rows], add_low(behind[rows:], back)], axis=0)
    else:
        go, back = add_low(ahead, go), add_low(behind, back)
    return ring_shift(go, n, 1), ring_shift(back, n, -1)


def ring_scatter(piece, n):
    go, back = ring_far(piece, n)
    for k in range(n // 2 - 1, 0, -1):
        go, back = ring_near(piece, n, k, go, back)
    return piece(0), go, back


def total_low(own, go, back):
    return (own.astype(f32) + go.astype(f32) + back.astype(f32)).astype(bf16)


def at_position(pieces, n, position):
    return lambda k: lax.dynamic_index_in_dim(pieces, (position - k) % n, 0, keepdims=False)


def ring_sum(pieces, n, position):
    if n != 8:
        mine = lax.psum_scatter(pieces, "ctx", scatter_dimension=0, tiled=False)
    else:
        mine = total_low(*ring_scatter(at_position(pieces, n, position), n))
    return ring_gather(mine, n, position)


def rows_home(mine, w):
    out = []
    for mask in range(WA):
        block = lax.dynamic_index_in_dim(mine, w ^ mask, 0, keepdims=False)
        out.append(swap(block, mask) if mask else block)
    return jnp.stack(out)


def placed(gathered, n, position):
    if n != 8:
        return by_distance(gathered, n, position)
    out = jnp.zeros((n,) + gathered[0].shape, bf16)
    for k in range(n):
        out = lax.dynamic_update_index_in_dim(out, gathered[k], (position - k) % n, 0)
    return out


def all_sum(x, n):
    for mask in (1, 2):
        x = x + swap(x, mask)
    step = 1
    while step < n:
        x = x + lax.ppermute(x, "ctx", [(i, i ^ step) for i in range(n)])
        step *= 2
    return x


def everyone(x):
    side = swap(x, 1)
    across = swap(x, 2)
    return [x, side, across, swap(across, 1)]


VMEM = pl.BlockSpec(memory_space=pltpu.VMEM)
SMEM = pl.BlockSpec(memory_space=pltpu.SMEM)


def call(body, name, n_scalar, ins, outs, scratch=(), us=2.0, limit=10, spec=VMEM):
    return pl.pallas_call(
        body,
        name=name,
        in_specs=[SMEM] * n_scalar + [spec] * (len(ins) - n_scalar),
        out_specs=[VMEM] * len(outs),
        out_shape=list(outs),
        scratch_shapes=list(scratch),
        cost_estimate=pl.CostEstimate(flops=int(us * 1.15e9), transcendentals=0, bytes_accessed=1 << 16),
        compiler_params=pltpu.CompilerParams(vmem_limit_bytes=limit * MB),
    )(*ins)


def shape(dims, dtype):
    return jax.ShapeDtypeStruct(dims, dtype)


def mm(a, b):
    return jnp.dot(a, b, preferred_element_type=f32)


def nt(a, b):
    return lax.dot_general(a, b, (((1,), (1,)), ((), ())), preferred_element_type=f32)


def tn(a, b):
    return lax.dot_general(a, b, (((0,), (0,)), ((), ())), preferred_element_type=f32)


def turn(u):
    lane = lax.broadcasted_iota(i32, u.shape, 1) % HS
    return jnp.where(lane < HS // 2, -pltpu.roll(u, 128 - HS // 2, 1), pltpu.roll(u, HS // 2, 1))


def turn_back(u):
    lane = lax.broadcasted_iota(i32, u.shape, 1) % HS
    return jnp.where(lane < HS // 2, pltpu.roll(u, 128 - HS // 2, 1), -pltpu.roll(u, HS // 2, 1))


def rope(u, cos, sin):
    return u * cos + turn(u) * sin


def rope_back(u, cos, sin):
    return u * cos + turn_back(u * sin)


def pack_qkv_body(wq, wk, wv, gains, out):
    out[:SL, :KV] = wk[...].astype(bf16)
    out[:SL, KV : 2 * KV] = wv[...].astype(bf16)
    out[:SL, 2 * KV :] = wq[...].astype(bf16)
    out[SL:, :] = jnp.zeros((8, QKV), bf16)
    out[SL:, :SL] = gains[...].astype(bf16)


def pack_rest_body(sc, w_out, w_gate, w_up, w_down, out_ref, keep, give, down):
    core = sc[4]
    out_ref[...] = w_out[...].astype(bf16)
    down[...] = w_down[...].astype(bf16)
    for gu, src in enumerate((w_gate, w_up)):
        for t in range(2):
            lo = pl.multiple_of(FFQ * (2 * t + core), 128)
            keep[gu, t] = src[:, pl.ds(lo, FFQ)].astype(bf16)
            lo = pl.multiple_of(FFQ * (2 * t + 1 - core), 128)
            give[gu, t] = src[:, pl.ds(lo, FFQ)].astype(bf16)


def pack_qkv(wq, wk, wv, gains):
    ins = [wq, wk, wv, gains]
    return call(pack_qkv_body, "pack_qkv", 0, ins, [shape((SL + 8, QKV), bf16)], us=1.5)[0]


def pack_rest(scal, w_out, w_gate, w_up, w_down):
    quarters = shape((2, 2, SL, FFQ), bf16)
    return call(
        pack_rest_body,
        "pack_rest",
        1,
        [scal, w_out, w_gate, w_up, w_down],
        [shape((SL, D), bf16), quarters, quarters, shape((FFQ, D), bf16)],
        limit=16,
        us=4,
    )


def head_only(tables):
    cos, sin = tables
    lane = lax.broadcasted_iota(i32, cos.shape, 1)
    return jnp.where(lane < HS, cos, 1.0), jnp.where(lane < HS, sin, 0.0)


def project_body(n_in, sc, *refs):
    xs = refs[:n_in]
    cos_ref, sin_ref, p0, p1, p2, p3 = refs[n_in : n_in + 6]
    x_ref, a4, q3, kv, acc_ref, x4 = refs[n_in + 6 :]
    x = xs[0][...].astype(f32)
    for r in xs[1:]:
        x = x + r[...]
    x_ref[...] = x
    ratio = lax.rsqrt(jnp.mean(x * x, axis=1, keepdims=True) + epsilon)
    x = x * ratio
    for j in range(WA):
        x4[j] = x[:, SL * j : SL * (j + 1)]
    acc = None
    for m, p in enumerate((p0, p1, p2, p3)):
        j = sc[0] ^ m
        a = (x4[j] * p[SL : SL + 1, :SL].astype(f32)).astype(bf16)
        a4[j] = a
        part = mm(a, p[:SL, :])
        acc = part if acc is None else acc + part
    acc_ref[:, :QKV] = acc
    cos, sin = cos_ref[...], sin_ref[...]
    edge = head_only((cos, sin))
    for i in range(2):
        kv[:, 128 * i : 128 * (i + 1)] = rope(acc_ref[:, 128 * i : 128 * (i + 1)], cos, sin).astype(bf16)
    kv[:, 256:384] = rope(acc_ref[:, 256:384], *edge).astype(bf16)
    kv[:, 384:640] = acc_ref[:, 384:640].astype(bf16)
    for i in range(8):
        lo = 2 * KV + 128 * i
        u = rope(acc_ref[:, lo : lo + 128], cos, sin).astype(bf16) * bf16(0.125)
        for j in range(2):
            h = 2 * i + j
            if h < QH:
                q3[h // GQ, BLK * (h % GQ) : BLK * (h % GQ + 1), :] = u[:, HS * j : HS * (j + 1)]


def project(scal, xs, tables, parts):
    return call(
        functools.partial(project_body, len(xs)),
        "project",
        1,
        [scal, *xs, *tables, *parts],
        [
            shape((BLK, D), f32),
            shape((WA, BLK, SL), bf16),
            shape((KVH, R3, HS), bf16),
            shape((BLK, 2 * KV), bf16),
        ],
        [pltpu.VMEM((BLK, QKV + 64), f32), pltpu.VMEM((WA, BLK, SL), f32)],
        us=2.5,
    )


def list_blocks(sched, lst, n):
    def step(k, count):
        first = sched[k] * BLK
        seen = (sched[k] <= sched[0]) & (first + BLK > sched[n])

        @pl.when(seen)
        def _():
            lst[count] = k

        return count + seen.astype(i32)

    return lax.fori_loop(0, n, step, jnp.int32(0))


def block_bias(sched, qinfo, k):
    key = sched[k] * BLK + lax.broadcasted_iota(i32, (BLK, R3), 0)
    ok = (key <= qinfo[0:1, :]) & (key >= qinfo[1:2, :])
    return jnp.where(ok, 0.0, masked_score).astype(f32)


def attend_body(n, sc, sched, qinfo, q3, kv, x, a4, gain, p0, p1, p2, p3, *refs):
    sl = refs[:WA]
    o_t, lse, m_ref, b_ref, lst, o_scr, ol4 = refs[WA:]
    count = list_blocks(sched, lst, n)
    o_t[...] = jnp.zeros(o_t.shape, f32)

    def step(i, state):
        k = lst[i]
        bias = block_bias(sched, qinfo, k)
        out = []
        for h in range(KVH):
            top, total = state[h]
            s = nt(kv[k, :, HS * h : HS * (h + 1)], q3[h]) + bias
            new = jnp.maximum(top, jnp.max(s, axis=0, keepdims=True))
            p = jnp.exp(s - new)
            fix = jnp.exp(top - new)
            values = kv[k, :, KV + HS * h : KV + HS * (h + 1)]
            o_t[h] = o_t[h] * fix + tn(values, p.astype(bf16))
            out.append((new, total * fix + jnp.sum(p, axis=0, keepdims=True)))
        return tuple(out)

    start = tuple(
        (jnp.full((1, R3), masked_score, f32), jnp.zeros((1, R3), f32)) for _ in range(KVH)
    )
    state = lax.fori_loop(0, count, step, start)
    for h in range(KVH):
        top, total = state[h]
        out = o_t[h] * (1.0 / total)
        o_t[h] = out
        lse[h : h + 1, :] = top + jnp.log(total)
        rows = out.T
        for g in range(GQ):
            j = GQ * h + g
            o_scr[:, HS * j : HS * (j + 1)] = rows[BLK * g : BLK * (g + 1), :]
    low = o_scr[...].astype(bf16)
    for j in range(WA):
        ol4[j] = low[:, SL * j : SL * (j + 1)]
    m = x[...]
    for k, p in enumerate((p0, p1, p2, p3)):
        j = sc[0] ^ k
        sl[k][0] = a4[j]
        sl[k][1] = ol4[j]
        m = m + mm(ol4[j], p[...])
    m_ref[...] = m
    ratio = lax.rsqrt(jnp.mean(m * m, axis=1, keepdims=True) + epsilon)
    b = (m * ratio * gain[...]).astype(bf16)
    b_ref[...] = b


def attend(scal, sched, qinfo, q3, kv, x, a4, gain, parts):
    n = kv.shape[0]
    return call(
        functools.partial(attend_body, n),
        "attend",
        2,
        [scal, sched, qinfo, q3, kv, x, a4, gain, *parts],
        [
            *[shape((2, BLK, SL), bf16)] * WA,
            shape((KVH, HS, R3), f32),
            shape((8, R3), f32),
            shape((BLK, D), f32),
            shape((BLK, D), bf16),
        ],
        [
            pltpu.SMEM((n,), i32),
            pltpu.VMEM((BLK, D), f32),
            pltpu.VMEM((WA, BLK, SL), bf16),
        ],
        limit=8,
        us=10,
    )


def mlp_body(sc, b_own, b_side, keep, core, gm, um, go, uo, d_own, d_far, *refs):
    z_keep, z_give, gu_ref, y_own, y_side, bs, z_ref = refs
    w = sc[0]
    for half, b in enumerate((b_own, b_side)):
        for j in range(WA):
            bs[j, BLK * half : BLK * (half + 1), :] = b[:, SL * j : SL * (j + 1)]
    for t, fars in ((sc[1], (gm, um)), (1 - sc[1], (go, uo))):
        lin = []
        for gu in range(2):
            acc = mm(bs[w], keep[gu, t]) + mm(bs[w ^ 1], core[gu, t])
            acc = acc + mm(bs[w ^ 2], fars[gu][0]) + mm(bs[w ^ 3], fars[gu][1])
            gu_ref[gu, t] = acc
            lin.append(acc)
        gate, up = lin
        z_ref[t] = (gate / (1.0 + jnp.exp(-gate)) * up).astype(bf16)
    row = sc[2]
    out = mm(z_ref[row], d_own[...]) + mm(z_ref[1 - row], d_far[...])
    y_own[...] = out[:BLK]
    y_side[...] = out[BLK:]
    z_keep[...] = z_ref[row]
    z_give[...] = z_ref[1 - row]


def mlp(scal, b_own, b_side, wts):
    return call(
        mlp_body,
        "mlp",
        1,
        [scal, b_own, b_side, *wts],
        [
            shape((2 * BLK, FFQ), bf16),
            shape((2 * BLK, FFQ), bf16),
            shape((2, 2, 2 * BLK, FFQ), f32),
            shape((BLK, D), f32),
            shape((BLK, D), f32),
        ],
        [pltpu.VMEM((WA, 2 * BLK, SL), bf16), pltpu.VMEM((2, 2 * BLK, FFQ), bf16)],
        limit=12,
        us=5.5,
    )


def mlp_back_body(sc, l_own, l_side, gu_ref, keep, core, gm, um, go, uo, d_own, d_far, *refs):
    keep_ref, give_ref, db_own, db_side, low, acc = refs
    w, row = sc[0], sc[2]
    low[:BLK] = l_own[...]
    low[BLK:] = l_side[...]
    for first, (t, fg, fu) in enumerate(((sc[1], gm, um), (1 - sc[1], go, uo))):
        dz = jnp.where(t == row, nt(low[...], d_own[...]), nt(low[...], d_far[...]))
        gate, up = gu_ref[0, t], gu_ref[1, t]
        sig = 1.0 / (1.0 + jnp.exp(-gate))
        dg = (dz * up * sig * (1.0 + gate * (1.0 - sig))).astype(bf16)
        du = (dz * gate * sig).astype(bf16)

        @pl.when(t == row)
        def _():
            keep_ref[0] = dg
            keep_ref[1] = du

        @pl.when(t != row)
        def _():
            give_ref[0] = dg
            give_ref[1] = du

        for j, p in ((w, keep.at[0, t]), (w ^ 1, core.at[0, t]), (w ^ 2, fg.at[0]), (w ^ 3, fg.at[1])):
            part = nt(dg, p[...])
            acc[j] = part if first == 0 else acc[j] + part
        for j, p in ((w, keep.at[1, t]), (w ^ 1, core.at[1, t]), (w ^ 2, fu.at[0]), (w ^ 3, fu.at[1])):
            acc[j] = acc[j] + nt(du, p[...])
    for j in range(WA):
        db_own[:, SL * j : SL * (j + 1)] = acc[j, :BLK, :]
        db_side[:, SL * j : SL * (j + 1)] = acc[j, BLK:, :]


def mlp_back(scal, l_own, l_side, gu, wts):
    return call(
        mlp_back_body,
        "mlp_back",
        1,
        [scal, l_own, l_side, gu, *wts],
        [
            shape((2, 2 * BLK, FFQ), bf16),
            shape((2, 2 * BLK, FFQ), bf16),
            shape((BLK, D), f32),
            shape((BLK, D), f32),
        ],
        [pltpu.VMEM((2 * BLK, D), bf16), pltpu.VMEM((WA, 2 * BLK, SL), f32)],
        limit=12,
        us=6.7,
    )


def norm_back(grads, hidden, gain):
    ratio = lax.rsqrt(jnp.mean(hidden * hidden, axis=1, keepdims=True) + epsilon)
    scaled = hidden * ratio
    gain_grad = jnp.sum(grads * scaled, axis=0, keepdims=True)
    inner = grads * gain
    out = ratio * (inner - scaled * jnp.mean(inner * scaled, axis=1, keepdims=True))
    return out, gain_grad


def attend_back_body(n, sc, sched, qinfo, dy, db_own, db_got, m, gain, p0, p1, p2, p3, q3, kv, o_t, lse, cos_ref, sin_ref, *refs):
    dm_ref, dml_ref, gg, dq_ref, dkv_ref, lst, do3, d_scr, dq_scr, dq_t = refs
    count = list_blocks(sched, lst, n)
    part, gain_grad = norm_back(db_own[...] + db_got[...], m[...], gain[...])
    gg[...] = gain_grad
    dm = dy[...].astype(f32) + part
    dm_ref[...] = dm
    dml = dm.astype(bf16)
    dml_ref[...] = dml
    for k, p in enumerate((p0, p1, p2, p3)):
        d_scr[sc[0] ^ k] = nt(dml, p[...]).astype(bf16).astype(f32)
    whole = jnp.concatenate([d_scr[j] for j in range(WA)], axis=1)
    for j in range(QH):
        do3[j // GQ, BLK * (j % GQ) : BLK * (j % GQ + 1), :] = whole[:, HS * j : HS * (j + 1)].astype(bf16)

    @pl.loop(1, n)
    def _(k):
        seen = (sched[k] <= sched[0]) & (sched[k] * BLK + BLK > sched[n])

        @pl.when(jnp.logical_not(seen))
        def _():
            dkv_ref[k] = jnp.zeros((BLK, 2 * KV), bf16)

    deltas = [
        jnp.sum(do3[h].astype(f32).T * o_t[h], axis=0, keepdims=True) for h in range(KVH)
    ]
    dq_t[...] = jnp.zeros(dq_t.shape, f32)

    @pl.loop(0, count)
    def _(i):
        k = lst[i]
        bias = block_bias(sched, qinfo, k)
        for h in range(KVH):
            keys = kv[k, :, HS * h : HS * (h + 1)]
            values = kv[k, :, KV + HS * h : KV + HS * (h + 1)]
            s = nt(keys, q3[h]) + bias
            p = jnp.exp(s - lse[h : h + 1, :])
            ds = (p * (nt(values, do3[h]) - deltas[h])).astype(bf16)
            dkv_ref[k, :, HS * h : HS * (h + 1)] = mm(ds, q3[h]).astype(bf16)
            dkv_ref[k, :, KV + HS * h : KV + HS * (h + 1)] = mm(p.astype(bf16), do3[h]).astype(bf16)
            dq_t[h] = dq_t[h] + tn(keys, ds)

    for h in range(KVH):
        rows = (dq_t[h] * 0.125).T
        for g in range(GQ):
            j = GQ * h + g
            dq_scr[:, HS * j : HS * (j + 1)] = rows[BLK * g : BLK * (g + 1), :]
    cos, sin = cos_ref[...], sin_ref[...]
    for i in range(8):
        u = rope_back(dq_scr[:, 128 * i : 128 * (i + 1)], cos, sin).astype(bf16)
        if i < 7:
            dq_ref[:, 128 * i : 128 * (i + 1)] = u
        else:
            dq_ref[:, 128 * i :] = u[:, :HS]


def attend_back(scal, sched, qinfo, dy, db_own, db_got, m, gain, parts, q3, kv, o_t, lse, tables):
    n = kv.shape[0]
    return call(
        functools.partial(attend_back_body, n),
        "attend_back",
        2,
        [scal, sched, qinfo, dy, db_own, db_got, m, gain, *parts, q3, kv, o_t, lse, *tables],
        [
            shape((BLK, D), f32),
            shape((BLK, D), bf16),
            shape((1, D), f32),
            shape((BLK, D), bf16),
            shape((n, BLK, 2 * KV), bf16),
        ],
        [
            pltpu.SMEM((n,), i32),
            pltpu.VMEM((KVH, R3, HS), bf16),
            pltpu.VMEM((WA, BLK, SL), f32),
            pltpu.VMEM((BLK, D + 64), f32),
            pltpu.VMEM((KVH, HS, R3), f32),
        ],
        limit=8,
        us=12,
    )


def query_back_body(sc, dq, p0, p1, p2, p3, da):
    for k, p in enumerate((p0, p1, p2, p3)):
        da[sc[0] ^ k] = nt(dq[...], p[:SL, 2 * KV :])


def query_back(scal, dq, parts):
    return call(
        query_back_body,
        "query_back",
        1,
        [scal, dq, *parts],
        [shape((WA, BLK, SL), f32)],
        us=2,
    )[0]


def project_back_body(sc, own, go, back, cos_ref, sin_ref, da, p0, p1, p2, p3, x, dm, gain, *refs):
    dkv_ref, dx_ref, dxl_ref, gg, d4 = refs
    total = own[...].astype(f32) + go[...].astype(f32) + back[...].astype(f32)
    cos, sin = cos_ref[...], sin_ref[...]
    edge = head_only((cos, sin))
    for i in range(2):
        dkv_ref[:, 128 * i : 128 * (i + 1)] = rope_back(total[:, 128 * i : 128 * (i + 1)], cos, sin).astype(bf16)
    dkv_ref[:, 256:384] = rope_back(total[:, 256:384], *edge).astype(bf16)
    dkv_ref[:, 384:] = total[:, 384:].astype(bf16)
    for k, p in enumerate((p0, p1, p2, p3)):
        d4[sc[0] ^ k] = da[sc[0] ^ k] + nt(dkv_ref[...], p[:SL, : 2 * KV])
    grads = jnp.concatenate([d4[j] for j in range(WA)], axis=1)
    part, gain_grad = norm_back(grads, x[...], gain[...])
    gg[...] = gain_grad
    dx = dm[...] + part
    dx_ref[...] = dx
    dxl_ref[...] = dx.astype(bf16)


def project_back(scal, addends, tables, da, parts, x, dm, gain):
    return call(
        project_back_body,
        "project_back",
        1,
        [scal, *addends, *tables, da, *parts, x, dm, gain],
        [
            shape((BLK, 2 * KV), bf16),
            shape((BLK, D), f32),
            shape((BLK, D), bf16),
            shape((1, D), f32),
        ],
        [pltpu.VMEM((WA, BLK, SL), f32)],
        us=2.5,
    )


def fetched(refs, bufs, sem):
    copies = [pltpu.make_async_copy(r, b, sem.at[i]) for i, (r, b) in enumerate(zip(refs, bufs))]
    for c in copies:
        c.start()
    for c in copies:
        c.wait()


def call_fetched(body, name, scal, ins, outs, us, limit, scratch=()):
    count = len(ins)

    def whole(sc, *refs):
        sources, results = refs[:count], refs[count : count + len(outs)]
        bufs = refs[count + len(outs) : 2 * count + len(outs)]
        sem, rest = refs[2 * count + len(outs)], refs[2 * count + len(outs) + 1 :]
        fetched(sources, bufs, sem)
        body(sc, *bufs, *results, *rest)

    bufs = [pltpu.VMEM(x.shape, x.dtype) for x in ins]
    return call(
        whole,
        name,
        1,
        [scal, *ins],
        outs,
        bufs + [pltpu.SemaphoreType.DMA((count,)), *scratch],
        us=us,
        limit=limit,
        spec=pl.BlockSpec(memory_space=pl.ANY),
    )


def grad_rows_body(has_prev, sc, *refs):
    out = refs[-1]
    slices = refs[:WA]
    lo = 0
    for t, kind in enumerate((0, 0, 1)):
        lows = refs[WA * (t + 1) : WA * (t + 2)]
        acc = None
        for sl, low in zip(slices, lows):
            part = tn(sl[kind], low[...])
            acc = part if acc is None else acc + part
        width = acc.shape[1]
        if has_prev:
            acc = acc + refs[4 * WA][:, lo : lo + width]
            out[:SL, lo : lo + width] = acc.astype(bf16)
        else:
            out[:, lo : lo + width] = acc
        lo += width
    if has_prev:
        out[SL:, :] = jnp.zeros((256 - SL, lo), bf16)


def grad_rows(scal, slices, dkvs, dqs, dms, prev):
    has_prev = prev is not None
    cols = QKV + D
    return call_fetched(
        functools.partial(grad_rows_body, has_prev),
        "grad_rows",
        scal,
        [*slices, *dkvs, *dqs, *dms] + ([prev] if has_prev else []),
        [shape((256, cols), bf16) if has_prev else shape((SL, cols), f32)],
        us=4,
        limit=20,
    )[0]


def grad_ff_body(has_prev, sc, b0, b1, b2, b3, keep, got, *refs):
    out, bt = refs[-2:]
    for m, b in enumerate((b0, b1, b2, b3)):
        bt[:, BLK * m : BLK * (m + 1)] = b[...].astype(f32).T.astype(bf16)
    for gu in range(2):
        for j in range(WA):
            lhs = bt[SL * j : SL * (j + 1), :]
            acc = mm(lhs[:, : 2 * BLK], keep[gu]) + mm(lhs[:, 2 * BLK :], got[gu])
            for i in range(4):
                rows = min(64, SL - 64 * i)
                part = acc[64 * i : 64 * i + rows]
                if has_prev:
                    part = part + refs[0][4 * gu + i, j, :rows]
                out[4 * gu + i, j, :rows] = part.astype(out.dtype)
                if rows < 64:
                    out[4 * gu + i, j, rows:] = jnp.zeros((64 - rows, FFQ), out.dtype)


def grad_ff(scal, bs, keep, got, prev):
    has_prev = prev is not None
    return call_fetched(
        functools.partial(grad_ff_body, has_prev),
        "grad_ff",
        scal,
        [*bs, keep, got] + ([prev] if has_prev else []),
        [shape((8, WA, 64, FFQ), bf16 if has_prev else f32)],
        us=5,
        limit=24,
        scratch=[pltpu.VMEM((D, WA * BLK), bf16)],
    )[0]


def grad_down_body(has_prev, sc, z, zg, l0, l1, l2, l3, *refs):
    out = refs[-1]
    acc = tn(z[:BLK], l0[...]) + tn(z[BLK:], l1[...])
    acc = acc + tn(zg[:BLK], l2[...]) + tn(zg[BLK:], l3[...])
    if has_prev:
        acc = acc + refs[0][...]
    out[...] = acc.astype(out.dtype)


def grad_down(scal, z, z_got, lows, prev):
    has_prev = prev is not None
    return call_fetched(
        functools.partial(grad_down_body, has_prev),
        "grad_down",
        scal,
        [z, z_got, *lows] + ([prev] if has_prev else []),
        [shape((FFQ, D), bf16 if has_prev else f32)],
        us=3,
        limit=16,
    )[0]


def finish_ff_body(n, sc, *refs):
    gate, up = refs[n:]
    position, w = sc[3], sc[0]
    for k in range(n):
        p = (position - k + n) % n
        first = pl.multiple_of(64 * (p % 4), 8)
        for gu, out in enumerate((gate, up)):
            for rows in (64, SL - 192):

                @pl.when((p // 4 == gu) & ((p % 4 < 3) == (rows == 64)))
                def _():
                    for m in range(WA):
                        lo = pl.multiple_of(FFQ * (w ^ m), 128)
                        out[pl.ds(first, rows), pl.ds(lo, FFQ)] = refs[k][m, :rows].astype(f32)


def finish_ff(scal, gathered):
    return call(
        functools.partial(finish_ff_body, len(gathered)),
        "finish_ff",
        1,
        [scal, *gathered],
        [shape((SL, 4 * FFQ), f32)] * 2,
        us=4,
        limit=12,
    )


def finish_down_body(n, sc, *refs):
    out = refs[n]
    for k in range(n):
        p = (sc[3] - k + n) % n
        rows = refs[k].shape[0]
        out[pl.ds(pl.multiple_of(p * rows, 8), rows), :] = refs[k][...].astype(f32)


def finish_down(scal, gathered):
    return call(
        functools.partial(finish_down_body, len(gathered)),
        "finish_down",
        1,
        [scal, *gathered],
        [shape((FFQ, D), f32)],
        us=2.5,
    )[0]


def finish_rows_body(n, widths, sc, *refs):
    outs = refs[n:]
    for k in range(n):
        p = (sc[3] - k + n) % n
        rows = refs[k].shape[0]
        tail = SL - rows * (n - 1)
        first = pl.multiple_of(p * rows, 8)

        @pl.when(p < n - 1)
        def _():
            lo = 0
            for out, width in zip(outs, widths):
                out[pl.ds(first, rows), :] = refs[k][:, lo : lo + width].astype(f32)
                lo += width

        @pl.when(p == n - 1)
        def _():
            lo = 0
            for out, width in zip(outs, widths):
                out[rows * (n - 1) :, :] = refs[k][:tail, lo : lo + width].astype(f32)
                lo += width


def finish_rows(scal, gathered, widths):
    return call(
        functools.partial(finish_rows_body, len(gathered), tuple(widths)),
        "finish_rows",
        1,
        [scal, *gathered],
        [shape((SL, width), f32) for width in widths],
        us=2.5,
    )


def body(
    tokens,
    cotangent,
    segment_ids,
    block_order,
    gain_attn,
    w_query,
    key_projection,
    value_projection,
    w_out,
    gain_mlp,
    w_gate,
    w_up,
    w_down,
):
    n = block_order.shape[1]
    w = lax.axis_index("wa")
    r = lax.axis_index("ctx")
    core = w % 2
    row = w // 2
    position = ring_position(r, n)
    x_side = r % 2
    scal = jnp.stack([w, x_side, row, position, core]).astype(i32)

    blocks = ring_device((position - jnp.arange(n, dtype=i32)) % n, n)
    labels = jnp.arange(n, dtype=i32)
    order_row = block_order[0]
    anchors = jnp.sum(jnp.where(blocks[:, None] == labels[None, :], order_row[None, :], 0), axis=1)
    natural = anchors[0] * BLK + jnp.arange(BLK, dtype=i32)
    seg_labels = jnp.arange(SEQS, dtype=i32)
    sizes = jnp.sum((segment_ids[0][None, :] == seg_labels[:, None]).astype(i32), axis=1)
    before = (seg_labels[None, :] < seg_labels[:, None]).astype(i32)
    starts = jnp.sum(before * sizes[None, :], axis=1)
    start_of = jnp.max(jnp.where(starts[None, :] <= natural[:, None], starts[None, :], 0), axis=1)
    sched = jnp.concatenate([anchors, start_of[:1]]).astype(i32)
    qinfo = jnp.pad(
        jnp.stack([jnp.tile(natural, GQ), jnp.tile(start_of, GQ)]), ((0, 6), (0, 0))
    ).astype(i32)
    frequency = rope_base ** (-jnp.arange(HS // 2, dtype=f32) * 2.0 / HS)
    angles = (natural - start_of).astype(f32)[:, None] * frequency[None, :]
    tables = (jnp.tile(jnp.cos(angles), (1, 4)), jnp.tile(jnp.sin(angles), (1, 4)))

    gains_own = jnp.pad(jnp.stack([gain_attn, gain_mlp]), ((0, 6), (0, 0)))
    qkv_own = pack_qkv(w_query, key_projection, value_projection, gains_own)
    qkv_across = swap(qkv_own, 2)
    qkv_side = swap(qkv_own, 1)
    out_own, keep, give, down_own = pack_rest(scal, after(w_out, qkv_own), w_gate, w_up, w_down)
    core_part = swap(give, 1)

    def y_half(gu):
        return jnp.stack(
            [
                lax.dynamic_index_in_dim(keep[gu], x_side, 0, keepdims=False),
                lax.dynamic_index_in_dim(core_part[gu], x_side, 0, keepdims=False),
            ]
        )

    gate_half, up_half = y_half(0), y_half(1)
    down_half = lax.dynamic_slice_in_dim(down_own, x_side * (FFQ // 2), FFQ // 2, 0)
    qkv_across, qkv_side, core_part, out_own, gate_half, up_half, down_half = bar(
        qkv_across, qkv_side, core_part, out_own, gate_half, up_half, down_half
    )
    qkv_parts = [qkv_own, qkv_side, qkv_across, swap(qkv_across, 1)]
    gains_parts = jnp.stack([p[SL : SL + 2, :SL] for p in qkv_parts])
    gains = jnp.concatenate(
        [lax.dynamic_index_in_dim(gains_parts, w ^ j, 0, keepdims=False) for j in range(WA)], axis=1
    ).astype(f32)
    gain_a, gain_m = gains[0:1], gains[1:2]

    def ring_keys(kv, extras):
        if n != 8:
            done = [e() for e in extras]
            return ring_gather(kv, n, position), done
        rows = BLK // 2
        ahead, behind, done = [kv], [kv], []
        for step in range(4):
            more = extras[step]()
            if step < 3:
                f, b = ring_shift(ahead[-1], n, 1), ring_shift(behind[-1], n, -1)
            else:
                f = ring_shift(ahead[-1][:rows], n, 1)
                b = ring_shift(behind[-1][rows:], n, -1)
            f, b, *more = bar(f, b, *more)
            ahead.append(f)
            behind.append(b)
            done.append(more)
        far = jnp.concatenate([ahead[4], behind[4]], axis=0)
        return jnp.stack(ahead[:4] + [far] + behind[3:0:-1]), done

    def nothing():
        return []

    out_across = swap(out_own, 2)
    gate_mine = swap(gate_half, 2)
    x, a4, q3, kv = project(scal, [tokens[0]], tables, qkv_parts)
    held = {}

    def step1():
        return [out_across]

    def step2():
        held["up_mine"] = swap(after(up_half, kv), 2)
        return [swap(out_across, 1), swap(out_own, 1), gate_mine]

    def step3():
        held["gate_other"] = side_swap(gate_mine, n)
        return []

    def step4():
        return [held["up_mine"], held["gate_other"]]

    every, more = ring_keys(kv, [step1, step2, step3, step4])
    out_across, (out_diag, out_side, gate_mine), (up_mine, gate_other) = more[0][0], more[1], more[3]
    out_parts = [out_own, out_side, out_across, out_diag]
    up_other = side_swap(up_mine, n)
    down_mine = swap(after(down_half, every), 2)
    *sl, o_t, lse, m, b = attend(scal, sched, qinfo, q3, every, x, a4, gain_m, out_parts)
    m, b, up_other, down_mine = bar(m, b, up_other, down_mine)
    b_side = swap(b, 1)
    down_other = side_swap(down_mine, n)
    down_far = jnp.concatenate(
        [
            jnp.where(x_side == 0, down_mine, down_other),
            jnp.where(x_side == 0, down_other, down_mine),
        ],
        axis=0,
    )
    ff_parts = [keep, core_part, gate_mine, up_mine, gate_other, up_other, down_own, down_far]
    b_far = swap(b, 2)
    z, z_give, gu, y_own, y_side = mlp(scal, b, b_side, ff_parts)
    y_own, y_side, b_far, z_give = bar(y_own, y_side, b_far, z_give)
    kept0 = [x, q3, every, o_t, lse, m, gu, z]

    y_got = swap(y_side, 1)
    z_got0 = swap(z_give, 2)
    x, a4, q3, kv = project(scal, [m, y_own, y_got], tables, qkv_parts)
    top = cotangent[0]
    b0, sl0 = b, sl

    def step1():
        return [z_got0, swap(b_far, 1)]

    def step2():
        return [swap(sl0[1], 1), swap(sl0[2], 2)]

    def step3():
        return [swap(sl0[3], 3), swap(after(top, kv), 2)]

    def step4():
        return [swap(top, 1)]

    every, more = ring_keys(kv, [step1, step2, step3, step4])
    (z_got0, b_diag), (s1, s2), (s3, top_far), (top_side,) = more
    kept0 += [z_got0, [b0, b_side, b_far, b_diag], [sl0[0], s1, s2, s3]]
    top_diag = swap(top_far, 1)
    *sl, o_t, lse, m, b = attend(scal, sched, qinfo, q3, every, x, a4, gain_m, out_parts)
    m, b, top_diag = bar(m, b, top_diag)
    b_side = swap(b, 1)
    b_far = swap(b, 2)
    z, z_give, gu, y_own, y_side = mlp(scal, b, b_side, ff_parts)
    y_own, y_side, b_far, z_give, z = bar(y_own, y_side, b_far, z_give, z)
    kept1 = [x, q3, every, o_t, lse, m, gu, z]

    x, q3, every, o_t, lse, m, gu, z = kept1
    y_got = swap(y_side, 1)
    z_got = swap(z_give, 2)
    b_diag = swap(b_far, 1)
    keep_d, give_d, db_own, db_side = mlp_back(scal, after(top, y_side), top_side, gu, ff_parts)
    db_own, db_side, give_d, z_got, b_diag, y_got = bar(
        db_own, db_side, give_d, z_got, b_diag, y_got
    )
    output = (m + y_own + y_got).astype(bf16)[None]
    db_got = swap(db_side, 1)
    got_d = swap(give_d, 2)
    dm, dml, gain_m_1, dq, dkv = attend_back(
        scal, sched, qinfo, top, db_own, db_got, m, gain_m, out_parts, q3, every, o_t, lse, tables
    )
    dkv, dq, dml, got_d = bar(dkv, dq, dml, got_d)

    def spread(dkv, extras):
        if n != 8:
            done = [e() for e in extras]
            total = lax.psum_scatter(
                by_distance(dkv, n, position), "ctx", scatter_dimension=0, tiled=False
            )
            return (total, jnp.zeros_like(total), jnp.zeros_like(total)), done
        done = []
        go = back = None
        for step in range(4):
            more = extras[step]()
            if step == 0:
                go, back = ring_far(lambda k: dkv[k], n)
            else:
                go, back = ring_near(lambda k: dkv[k], n, 4 - step, go, back)
            go, back, *more = bar(go, back, *more)
            done.append(more)
        return (dkv[0], go, back), done

    lows = [top, top_side, top_far, top_diag]

    def step1():
        return [swap(sl[1], 1), swap(sl[2], 2), grad_down(scal, z, z_got, lows, None)]

    def step2():
        return [swap(sl[3], 3), swap(dq, 2), query_back(scal, after(dq, dkv), qkv_parts)]

    def step3():
        bs = [b, b_side, b_far, b_diag]
        return [swap(after(dml, dq), 2), grad_ff(scal, bs, keep_d, got_d, None)]

    def step4():
        return [swap(dq, 1), swap(dml, 1)]


    addends, more = spread(dkv, [step1, step2, step3, step4])
    (s1, s2, down_1), (s3, dq_far, da), (dml_far, ff_1), (dq_side, dml_side) = more
    dq_diag = swap(dq_far, 1)
    dml_diag = swap(dml_far, 1)
    dkv0, dx, low, gain_a_1 = project_back(scal, addends, tables, da, qkv_parts, x, dm, gain_a)
    dx, low, dkv0, dq_diag, dml_diag = bar(dx, low, dkv0, dq_diag, dml_diag)
    slices_1 = [sl[0], s1, s2, s3]
    dqs_1 = [dq, dq_side, dq_far, dq_diag]
    dmls_1 = [dml, dml_side, dml_far, dml_diag]

    x, q3, every, o_t, lse, m, gu, z, z_got, bs, slices = kept0
    low_side = swap(low, 1)
    low_far = swap(low, 2)
    keep_d, give_d, db_own, db_side = mlp_back(scal, low, low_side, gu, ff_parts)
    db_own, db_side, give_d, low_far = bar(db_own, db_side, give_d, low_far)
    db_got = swap(db_side, 1)
    low_diag = swap(low_far, 1)
    dkv_side, dkv_far = swap(dkv0, 1), swap(dkv0, 2)
    down_grad = grad_down(scal, z, z_got, [low, low_side, low_far, low_diag], down_1)
    db_got, down_grad = bar(db_got, down_grad)
    down_piece = at_position(down_grad.reshape(n, FFQ // n, D), n, position)
    got_d = swap(give_d, 2)
    down_go = down_back = None
    if n == 8:
        down_go, down_back = ring_far(down_piece, n)
    dm, dml, gain_m_0, dq, dkv = attend_back(
        scal, sched, qinfo, dx, db_own, db_got, m, gain_m, out_parts, q3, every, o_t, lse, tables
    )
    dkv, dq, dml, got_d, dkv_side, dkv_far = bar(dkv, dq, dml, got_d, dkv_side, dkv_far)

    def ff_piece_of(ff):
        sub = n // 8
        pieces = ff.reshape(8, WA, sub, 64 // sub, FFQ).transpose(0, 2, 1, 3, 4)
        return pieces.reshape(n, WA, 64 // sub, FFQ)

    def down_step(k):
        nonlocal down_go, down_back
        if n != 8:
            return []
        down_go, down_back = ring_near(down_piece, n, k, down_go, down_back)
        return [down_go, down_back]

    def keep_down(pair):
        nonlocal down_go, down_back
        if n == 8:
            down_go, down_back = pair

    def step1():
        ff = grad_ff(scal, bs, keep_d, got_d, ff_1)
        return [ff, swap(dq, 2)] + down_step(3)

    def step2():
        return [swap(after(dml, dq), 2), query_back(scal, dq, qkv_parts)] + down_step(2)

    def step3():
        dkvs = [dkv0, dkv_side, dkv_far, swap(dkv_far, 1)]
        return [grad_rows(scal, slices_1, dkvs, dqs_1, dmls_1, None)] + down_step(1)

    def step4():
        return [swap(dq, 1), swap(dml, 1)]

    addends, more = spread(dkv, [step1, step2, step3, step4])
    (ff_grad, dq_far, *_), (dml_far, da, *_), (rows_1, *_), (dq_side, dml_side) = more
    dqs = [dq, dq_side, dq_far, swap(dq_far, 1)]
    dmls = [dml, dml_side, dml_far, swap(dml_far, 1)]
    dkv0, dx, low, gain_a_0 = project_back(scal, addends, tables, da, qkv_parts, x, dm, gain_a)
    input_grad = low[None]

    gain_sum = jnp.concatenate([gain_a_0 + gain_a_1, gain_m_0 + gain_m_1], axis=0)
    gain_sum = lax.dynamic_slice_in_dim(all_sum(gain_sum, n), w * SL, SL, 1)
    ff_pieces = ff_piece_of(ff_grad)
    if n == 8:
        down_all = ring_gather(total_low(down_piece(0), down_go, down_back), n, position)
        ff_mine = total_low(*ring_scatter(at_position(ff_pieces, n, position), n))
    else:
        down_all = ring_sum(down_grad.reshape(n, FFQ // n, D), n, position)
        ff_mine = lax.psum_scatter(ff_pieces, "ctx", scatter_dimension=0, tiled=False)
    ff_all = ring_gather(rows_home(ff_mine, w), n, position)
    rows_grad = grad_rows(scal, slices, everyone(dkv0), dqs, dmls, rows_1)
    rows_all = ring_sum(rows_grad.reshape(n, 256 // n, QKV + D), n, position)
    if n == 8:
        down_total = finish_down(scal, down_all)
        gate_total, up_total = finish_ff(scal, ff_all)
        key_total, value_total, query_total, out_total = finish_rows(scal, rows_all, [KV, KV, D, D])
    else:
        sub = n // 8
        whole = placed(ff_all, n, position).reshape(2, 4, sub, WA, 64 // sub, FFQ)
        whole = whole.transpose(0, 3, 1, 2, 4, 5).reshape(2, WA, 256, FFQ)[:, :, :SL]
        whole = jnp.take(whole, w ^ jnp.arange(WA, dtype=i32), axis=1).transpose(0, 2, 1, 3)
        gate_total, up_total = whole.reshape(2, SL, -1).astype(f32)
        down_total = placed(down_all, n, position).reshape(FFQ, D).astype(f32)
        rows_total = placed(rows_all, n, position).reshape(256, QKV + D)[:SL].astype(f32)
        key_total, value_total, query_total, out_total = (
            rows_total[:, :KV],
            rows_total[:, KV : 2 * KV],
            rows_total[:, 2 * KV : QKV],
            rows_total[:, QKV:],
        )
    return (
        output,
        input_grad,
        gain_sum[0],
        query_total,
        key_total,
        value_total,
        out_total,
        gain_sum[1],
        gate_total,
        up_total,
        down_total,
    )


def solution(mesh):
    rows = P("wa", None)
    flat = P("wa")
    act = P("wa", "ctx", None)
    return jax.shard_map(
        body,
        mesh=mesh,
        in_specs=(act, act, rows, rows, flat, rows, rows, rows, rows, flat, rows, rows, rows),
        out_specs=(act, act, flat, rows, rows, rows, rows, flat, rows, rows, rows),
        check_vma=False,
    )
```

```python
import functools

import jax
import jax.numpy as jnp
from jax import lax
from jax.experimental import pallas as pl
from jax.experimental.pallas import tpu as pltpu
from jax.sharding import PartitionSpec as P

QH = 15
KVH = 5
GQ = QH // KVH
HS = 64
SEQS = 8
REPEATS = 2
WA = 4
BLK = 128
D = 960
SL = D // WA
KV = KVH * HS
QKV = 2 * KV + D
FFQ = 640
R3 = GQ * BLK
QKVP = 1664

epsilon = 1e-05
masked_score = -1e30
rope_base = 10000.0
bf16 = jnp.bfloat16
f32 = jnp.float32
i32 = jnp.int32
MB = 1 << 20


def swap(x, mask):
    return lax.ppermute(x, "wa", [(i, i ^ mask) for i in range(WA)])


def side_swap(x, n):
    return lax.ppermute(x, "ctx", [(i, i ^ 1) for i in range(n)])


def ring_order(n):
    return [i for i in range(0, n, 2)] + [i for i in range(n - 1, 0, -2)]


def ring_shift(x, n, step):
    order = ring_order(n)
    return lax.ppermute(x, "ctx", [(order[i], order[(i + step) % n]) for i in range(n)])


def ring_position(r, n):
    return jnp.where(r % 2 == 0, r // 2, n - 1 - r // 2) if n == 8 else r


def ring_device(p, n):
    return jnp.where(p < n // 2, 2 * p, 2 * (n - 1 - p) + 1) if n == 8 else p


def after(x, *others):
    return lax.optimization_barrier((x,) + others)[0]


def bar(*xs):
    return lax.optimization_barrier(xs)


def by_distance(x, n, position):
    return jnp.take(x, (position - jnp.arange(n, dtype=i32)) % n, axis=0)


def ring_gather(x, n, position):
    if n != 8:
        return by_distance(lax.all_gather(x, "ctx"), n, position)
    half = n // 2
    rows = x.shape[0] // 2
    ahead = [x]
    behind = [x]
    for _ in range(half - 1):
        ahead.append(ring_shift(ahead[-1], n, 1))
        behind.append(ring_shift(behind[-1], n, -1))
    far = jnp.concatenate(
        [ring_shift(ahead[-1][:rows], n, 1), ring_shift(behind[-1][rows:], n, -1)], axis=0
    )
    return ahead + [far] + behind[:0:-1]


def add_low(x, y):
    return (x.astype(f32) + y.astype(f32)).astype(bf16)


def ring_far(piece, n):
    far = piece(n // 2)
    rows = far.shape[0] // 2
    return ring_shift(far[:rows], n, 1), ring_shift(far[rows:], n, -1)


def ring_near(piece, n, k, go, back):
    ahead, behind = piece(n - k), piece(k)
    if go.shape != ahead.shape:
        rows = go.shape[0]
        go = jnp.concatenate([add_low(ahead[:rows], go), ahead[rows:]], axis=0)
        back = jnp.concatenate([behind[:rows], add_low(behind[rows:], back)], axis=0)
    else:
        go, back = add_low(ahead, go), add_low(behind, back)
    return ring_shift(go, n, 1), ring_shift(back, n, -1)


def ring_scatter(piece, n):
    go, back = ring_far(piece, n)
    for k in range(n // 2 - 1, 0, -1):
        go, back = ring_near(piece, n, k, go, back)
    return piece(0), go, back


def total_low(own, go, back):
    return (own.astype(f32) + go.astype(f32) + back.astype(f32)).astype(bf16)


def at_position(pieces, n, position):
    return lambda k: lax.dynamic_index_in_dim(pieces, (position - k) % n, 0, keepdims=False)


def ring_sum(pieces, n, position):
    if n != 8:
        mine = lax.psum_scatter(pieces, "ctx", scatter_dimension=0, tiled=False)
    else:
        mine = total_low(*ring_scatter(at_position(pieces, n, position), n))
    return ring_gather(mine, n, position)


def rows_home(mine, w):
    out = []
    for mask in range(WA):
        block = lax.dynamic_index_in_dim(mine, w ^ mask, 0, keepdims=False)
        out.append(swap(block, mask) if mask else block)
    return jnp.stack(out)


def placed(gathered, n, position):
    if n != 8:
        return by_distance(gathered, n, position)
    out = jnp.zeros((n,) + gathered[0].shape, bf16)
    for k in range(n):
        out = lax.dynamic_update_index_in_dim(out, gathered[k], (position - k) % n, 0)
    return out


def everyone(x):
    side = swap(x, 1)
    across = swap(x, 2)
    return [x, side, across, swap(across, 1)]


VMEM = pl.BlockSpec(memory_space=pltpu.VMEM)
SMEM = pl.BlockSpec(memory_space=pltpu.SMEM)


HBM = pl.BlockSpec(memory_space=pltpu.HBM)


def call(body, name, n_scalar, ins, outs, scratch=(), us=2.0, limit=10, specs=None, out_specs=None):
    return pl.pallas_call(
        body,
        name=name,
        in_specs=[SMEM] * n_scalar + (specs or [VMEM] * (len(ins) - n_scalar)),
        out_specs=out_specs or [VMEM] * len(outs),
        out_shape=list(outs),
        scratch_shapes=list(scratch),
        cost_estimate=pl.CostEstimate(flops=int(us * 1.15e9), transcendentals=0, bytes_accessed=1 << 16),
        compiler_params=pltpu.CompilerParams(vmem_limit_bytes=limit * MB),
    )(*ins)


def fetched(refs, bufs, sem):
    copies = [pltpu.make_async_copy(r, b, sem.at[i]) for i, (r, b) in enumerate(zip(refs, bufs))]
    for c in copies:
        c.start()
    for c in copies:
        c.wait()


def call_fetched(body, name, scal, ins, outs, us, limit, scratch=(), far=None, far_out=False):
    count, n_out = len(ins), len(outs)
    far = [True] * count if far is None else far

    def whole(sc, *refs):
        sources, results = refs[:count], refs[count : count + n_out]
        bufs = refs[count + n_out : 2 * count + n_out]
        sem, rest = refs[2 * count + n_out], refs[2 * count + n_out + 1 :]
        fetched(sources, bufs, sem)
        if not far_out:
            body(sc, *bufs, *results, *rest)
            return
        body(sc, *bufs, *rest)
        fetched(rest[:n_out], results, sem)

    bufs = [pltpu.VMEM(x.shape, x.dtype) for x in ins]
    held = [pltpu.VMEM(x.shape, x.dtype) for x in outs] if far_out else []
    return call(
        whole,
        name,
        1,
        [scal, *ins],
        outs,
        bufs + [pltpu.SemaphoreType.DMA((max(count, n_out),)), *held, *scratch],
        us=us,
        limit=limit,
        specs=[HBM if f else pl.BlockSpec(memory_space=pl.ANY) for f in far],
        out_specs=[HBM] * n_out if far_out else None,
    )


def shape(dims, dtype):
    return jax.ShapeDtypeStruct(dims, dtype)


def mm(a, b):
    return jnp.dot(a, b, preferred_element_type=f32)


def nt(a, b):
    return lax.dot_general(a, b, (((1,), (1,)), ((), ())), preferred_element_type=f32)


def tn(a, b):
    return lax.dot_general(a, b, (((0,), (0,)), ((), ())), preferred_element_type=f32)


def turn(u):
    lane = lax.broadcasted_iota(i32, u.shape, 1) % HS
    return jnp.where(lane < HS // 2, -pltpu.roll(u, 128 - HS // 2, 1), pltpu.roll(u, HS // 2, 1))


def turn_back(u):
    lane = lax.broadcasted_iota(i32, u.shape, 1) % HS
    return jnp.where(lane < HS // 2, pltpu.roll(u, 128 - HS // 2, 1), -pltpu.roll(u, HS // 2, 1))


def rope(u, cos, sin):
    return u * cos + turn(u) * sin


def rope_back(u, cos, sin):
    return u * cos + turn_back(u * sin)


def pack_qkv_body(sc, wq, wk, wv, gains, out):
    out[:SL, :KV] = wk[...].T.astype(bf16)
    out[:SL, KV : 2 * KV] = wv[...].T.astype(bf16)
    out[:SL, 2 * KV : QKV] = wq[...].astype(bf16)
    out[:SL, QKV:] = jnp.zeros((SL, QKVP - QKV), bf16)
    out[SL:, :] = jnp.zeros((8, QKVP), bf16)
    out[SL:, :SL] = gains[...].astype(bf16)


def pack_qkv(scal, wq, wk, wv, gains):
    ins = [wq, wk.T, wv.T, gains]
    outs = [shape((SL + 8, QKVP), bf16)]
    return call_fetched(pack_qkv_body, "pack_qkv", scal, ins, outs, us=3, limit=8)[0]


def pack_rest_body(sc, w_out, w_gate, w_up, w_down, out_ref, keep, give, down):
    core = sc[4]
    out_ref[...] = w_out[...].astype(bf16)
    down[...] = w_down[...].T.astype(bf16)
    for gu, src in enumerate((w_gate, w_up)):
        for t in range(2):
            lo = pl.multiple_of(FFQ * (2 * t + core), 128)
            keep[gu, t] = src[:, pl.ds(lo, FFQ)].astype(bf16)
            lo = pl.multiple_of(FFQ * (2 * t + 1 - core), 128)
            give[gu, t] = src[:, pl.ds(lo, FFQ)].astype(bf16)


def pack_rest(scal, w_out, w_gate, w_up, w_down):
    quarters = shape((2, 2, SL, FFQ), bf16)
    outs = [shape((SL, D), bf16), quarters, quarters, shape((FFQ, D), bf16)]
    ins = [w_out, w_gate, w_up, w_down.T]
    return call_fetched(pack_rest_body, "pack_rest", scal, ins, outs, us=6, limit=24)


def head_only(tables):
    cos, sin = tables
    lane = lax.broadcasted_iota(i32, cos.shape, 1)
    return jnp.where(lane < HS, cos, 1.0), jnp.where(lane < HS, sin, 0.0)


def project_body(n_in, sc, *refs):
    xs = refs[:n_in]
    cos_ref, sin_ref, *parts = refs[n_in : n_in + 6]
    x_ref, a4, q3, kv, gains, acc_ref, x4, g4, buf, sem = refs[n_in + 6 :]
    copies = [pltpu.make_async_copy(p, buf.at[m], sem.at[m]) for m, p in enumerate(parts)]
    for c in copies:
        c.start()
    x = xs[0][...].astype(f32)
    for r in xs[1:]:
        x = x + r[...]
    x_ref[...] = x
    ratio = lax.rsqrt(jnp.mean(x * x, axis=1, keepdims=True) + epsilon)
    x = x * ratio
    for j in range(WA):
        x4[j] = x[:, SL * j : SL * (j + 1)]
    acc = None
    for m in range(WA):
        copies[m].wait()
        j = sc[0] ^ m
        gain = buf[m, SL:, :SL].astype(f32)
        g4[j] = gain
        a = (x4[j] * gain[:1]).astype(bf16)
        a4[j] = a
        part = mm(a, buf[m, :SL, :])
        acc = part if acc is None else acc + part
    gains[...] = jnp.concatenate([g4[j] for j in range(WA)], axis=1)
    acc_ref[...] = acc
    cos, sin = cos_ref[...], sin_ref[...]
    edge = head_only((cos, sin))
    for i in range(2):
        kv[:, 128 * i : 128 * (i + 1)] = rope(acc_ref[:, 128 * i : 128 * (i + 1)], cos, sin).astype(bf16)
    kv[:, 256:384] = rope(acc_ref[:, 256:384], *edge).astype(bf16)
    kv[:, 384:640] = acc_ref[:, 384:640].astype(bf16)
    for i in range(8):
        lo = 2 * KV + 128 * i
        u = rope(acc_ref[:, lo : lo + 128], cos, sin).astype(bf16) * bf16(0.125)
        for j in range(2):
            h = 2 * i + j
            if h < QH:
                q3[h // GQ, BLK * (h % GQ) : BLK * (h % GQ + 1), :] = u[:, HS * j : HS * (j + 1)]


def project(scal, xs, tables, parts):
    return call(
        functools.partial(project_body, len(xs)),
        "project",
        1,
        [scal, *xs, *tables, *parts],
        [
            shape((BLK, D), f32),
            shape((WA, BLK, SL), bf16),
            shape((KVH, R3, HS), bf16),
            shape((BLK, 2 * KV), bf16),
            shape((8, D), f32),
        ],
        [
            pltpu.VMEM((BLK, QKVP), f32),
            pltpu.VMEM((WA, BLK, SL), f32),
            pltpu.VMEM((WA, 8, SL), f32),
            pltpu.VMEM((WA, SL + 8, QKVP), bf16),
            pltpu.SemaphoreType.DMA((WA,)),
        ],
        us=3,
        limit=16,
        specs=[VMEM] * (len(xs) + 2) + [HBM] * WA,
    )


def list_blocks(sched, lst, n):
    def step(k, count):
        first = sched[k] * BLK
        seen = (sched[k] <= sched[0]) & (first + BLK > sched[n])

        @pl.when(seen)
        def _():
            lst[count] = k

        return count + seen.astype(i32)

    return lax.fori_loop(0, n, step, jnp.int32(0))


def block_bias(sched, qinfo, k):
    key = sched[k] * BLK + lax.broadcasted_iota(i32, (BLK, R3), 0)
    ok = (key <= qinfo[0:1, :]) & (key >= qinfo[1:2, :])
    return jnp.where(ok, 0.0, masked_score).astype(f32)


def attend_body(n, sc, sched, qinfo, q3, kv, x, a4, gain, p0, p1, p2, p3, *refs):
    sl = refs[:WA]
    o_t, lse, m_ref, b_ref, lst, o_scr, ol4 = refs[WA:]
    count = list_blocks(sched, lst, n)
    o_t[...] = jnp.zeros(o_t.shape, f32)

    def step(i, state):
        k = lst[i]
        bias = block_bias(sched, qinfo, k)
        out = []
        for h in range(KVH):
            top, total = state[h]
            s = nt(kv[k, :, HS * h : HS * (h + 1)], q3[h]) + bias
            new = jnp.maximum(top, jnp.max(s, axis=0, keepdims=True))
            p = jnp.exp(s - new)
            fix = jnp.exp(top - new)
            values = kv[k, :, KV + HS * h : KV + HS * (h + 1)]
            o_t[h] = o_t[h] * fix + tn(values, p.astype(bf16))
            out.append((new, total * fix + jnp.sum(p, axis=0, keepdims=True)))
        return tuple(out)

    start = tuple(
        (jnp.full((1, R3), masked_score, f32), jnp.zeros((1, R3), f32)) for _ in range(KVH)
    )
    state = lax.fori_loop(0, count, step, start)
    for h in range(KVH):
        top, total = state[h]
        out = o_t[h] * (1.0 / total)
        o_t[h] = out
        lse[h : h + 1, :] = top + jnp.log(total)
        rows = out.T
        for g in range(GQ):
            j = GQ * h + g
            o_scr[:, HS * j : HS * (j + 1)] = rows[BLK * g : BLK * (g + 1), :]
    low = o_scr[...].astype(bf16)
    for j in range(WA):
        ol4[j] = low[:, SL * j : SL * (j + 1)]
    m = x[...]
    for k, p in enumerate((p0, p1, p2, p3)):
        j = sc[0] ^ k
        sl[k][0] = a4[j]
        sl[k][1] = ol4[j]
        m = m + mm(ol4[j], p[...])
    m_ref[...] = m
    ratio = lax.rsqrt(jnp.mean(m * m, axis=1, keepdims=True) + epsilon)
    b = (m * ratio * gain[...]).astype(bf16)
    b_ref[...] = b


def attend(scal, sched, qinfo, q3, kv, x, a4, gain, parts):
    n = kv.shape[0]
    return call(
        functools.partial(attend_body, n),
        "attend",
        2,
        [scal, sched, qinfo, q3, kv, x, a4, gain, *parts],
        [
            *[shape((2, BLK, SL), bf16)] * WA,
            shape((KVH, HS, R3), f32),
            shape((8, R3), f32),
            shape((BLK, D), f32),
            shape((BLK, D), bf16),
        ],
        [
            pltpu.SMEM((n,), i32),
            pltpu.VMEM((BLK, D), f32),
            pltpu.VMEM((WA, BLK, SL), bf16),
        ],
        limit=8,
        us=10,
    )


def mlp_body(sc, b_own, b_side, keep, core, gm, um, go, uo, d_own, d_far, *refs):
    z_hbm, z_give, gu_hbm, y_own, y_side, bs, z_ref, gu_ref, sem = refs
    copies = []
    w = sc[0]
    for half, b in enumerate((b_own, b_side)):
        for j in range(WA):
            bs[j, BLK * half : BLK * (half + 1), :] = b[:, SL * j : SL * (j + 1)]
    for t, fars in ((sc[1], (gm, um)), (1 - sc[1], (go, uo))):
        lin = []
        for gu in range(2):
            acc = mm(bs[w], keep[gu, t]) + mm(bs[w ^ 1], core[gu, t])
            acc = acc + mm(bs[w ^ 2], fars[gu][0]) + mm(bs[w ^ 3], fars[gu][1])
            gu_ref[gu, t] = acc
            lin.append(acc)
        for gu in range(2):
            c = pltpu.make_async_copy(gu_ref.at[gu, t], gu_hbm.at[gu, t], sem.at[len(copies)])
            c.start()
            copies.append(c)
        gate, up = lin
        z_ref[t] = (gate / (1.0 + jnp.exp(-gate)) * up).astype(bf16)
    row = sc[2]
    copies.append(pltpu.make_async_copy(z_ref.at[row], z_hbm, sem.at[4]))
    copies[4].start()
    out = mm(z_ref[row], d_own[...]) + mm(z_ref[1 - row], d_far[...])
    y_own[...] = out[:BLK]
    y_side[...] = out[BLK:]
    z_give[...] = z_ref[1 - row]
    for c in copies:
        c.wait()


def mlp(scal, b_own, b_side, wts):
    return call(
        mlp_body,
        "mlp",
        1,
        [scal, b_own, b_side, *wts],
        [
            shape((2 * BLK, FFQ), bf16),
            shape((2 * BLK, FFQ), bf16),
            shape((2, 2, 2 * BLK, FFQ), f32),
            shape((BLK, D), f32),
            shape((BLK, D), f32),
        ],
        [
            pltpu.VMEM((WA, 2 * BLK, SL), bf16),
            pltpu.VMEM((2, 2 * BLK, FFQ), bf16),
            pltpu.VMEM((2, 2, 2 * BLK, FFQ), f32),
            pltpu.SemaphoreType.DMA((5,)),
        ],
        out_specs=[HBM, VMEM, HBM, VMEM, VMEM],
        limit=12,
        us=5.5,
    )


def mlp_back_body(sc, l_own, l_side, gu_hbm, keep, core, gm, um, go, uo, d_own, d_far, *refs):
    keep_ref, give_ref, db_own, db_side, low, acc, gu_ref, sem = refs
    copies = [
        [pltpu.make_async_copy(gu_hbm.at[gu, t], gu_ref.at[gu, t], sem.at[2 * i + gu]) for gu in range(2)]
        for i, t in enumerate((sc[1], 1 - sc[1]))
    ]
    for c in copies[0] + copies[1]:
        c.start()
    w, row = sc[0], sc[2]
    low[:BLK] = l_own[...]
    low[BLK:] = l_side[...]
    for first, (t, fg, fu) in enumerate(((sc[1], gm, um), (1 - sc[1], go, uo))):
        dz = jnp.where(t == row, nt(low[...], d_own[...]), nt(low[...], d_far[...]))
        for c in copies[first]:
            c.wait()
        gate, up = gu_ref[0, t], gu_ref[1, t]
        sig = 1.0 / (1.0 + jnp.exp(-gate))
        dg = (dz * up * sig * (1.0 + gate * (1.0 - sig))).astype(bf16)
        du = (dz * gate * sig).astype(bf16)

        @pl.when(t == row)
        def _():
            keep_ref[0] = dg
            keep_ref[1] = du

        @pl.when(t != row)
        def _():
            give_ref[0] = dg
            give_ref[1] = du

        for j, p in ((w, keep.at[0, t]), (w ^ 1, core.at[0, t]), (w ^ 2, fg.at[0]), (w ^ 3, fg.at[1])):
            part = nt(dg, p[...])
            acc[j] = part if first == 0 else acc[j] + part
        for j, p in ((w, keep.at[1, t]), (w ^ 1, core.at[1, t]), (w ^ 2, fu.at[0]), (w ^ 3, fu.at[1])):
            acc[j] = acc[j] + nt(du, p[...])
    for j in range(WA):
        db_own[:, SL * j : SL * (j + 1)] = acc[j, :BLK, :]
        db_side[:, SL * j : SL * (j + 1)] = acc[j, BLK:, :]


def mlp_back(scal, l_own, l_side, gu, wts):
    return call(
        mlp_back_body,
        "mlp_back",
        1,
        [scal, l_own, l_side, gu, *wts],
        [
            shape((2, 2 * BLK, FFQ), bf16),
            shape((2, 2 * BLK, FFQ), bf16),
            shape((BLK, D), f32),
            shape((BLK, D), f32),
        ],
        [
            pltpu.VMEM((2 * BLK, D), bf16),
            pltpu.VMEM((WA, 2 * BLK, SL), f32),
            pltpu.VMEM((2, 2, 2 * BLK, FFQ), f32),
            pltpu.SemaphoreType.DMA((4,)),
        ],
        specs=[VMEM, VMEM, HBM] + [VMEM] * 8,
        limit=12,
        us=6.7,
    )


def norm_back(grads, hidden, gain):
    ratio = lax.rsqrt(jnp.mean(hidden * hidden, axis=1, keepdims=True) + epsilon)
    scaled = hidden * ratio
    gain_grad = jnp.sum(grads * scaled, axis=0, keepdims=True)
    inner = grads * gain
    out = ratio * (inner - scaled * jnp.mean(inner * scaled, axis=1, keepdims=True))
    return out, gain_grad


def attend_back_body(n, sc, sched, qinfo, dy, db_own, db_got, m, gain, p0, p1, p2, p3, q3, kv, o_t, lse, cos_ref, sin_ref, *refs):
    dm_ref, dml_ref, gg, dq_ref, dkv_ref, lst, do3, d_scr, dq_scr, dq_t = refs
    count = list_blocks(sched, lst, n)
    part, gain_grad = norm_back(db_own[...] + db_got[...], m[...], gain[...])
    gg[...] = gain_grad
    dm = dy[...].astype(f32) + part
    dm_ref[...] = dm
    dml = dm.astype(bf16)
    dml_ref[...] = dml
    for k, p in enumerate((p0, p1, p2, p3)):
        d_scr[sc[0] ^ k] = nt(dml, p[...]).astype(bf16).astype(f32)
    whole = jnp.concatenate([d_scr[j] for j in range(WA)], axis=1)
    for j in range(QH):
        do3[j // GQ, BLK * (j % GQ) : BLK * (j % GQ + 1), :] = whole[:, HS * j : HS * (j + 1)].astype(bf16)

    @pl.loop(1, n)
    def _(k):
        seen = (sched[k] <= sched[0]) & (sched[k] * BLK + BLK > sched[n])

        @pl.when(jnp.logical_not(seen))
        def _():
            dkv_ref[k] = jnp.zeros((BLK, 2 * KV), bf16)

    deltas = [
        jnp.sum(do3[h].astype(f32).T * o_t[h], axis=0, keepdims=True) for h in range(KVH)
    ]
    dq_t[...] = jnp.zeros(dq_t.shape, f32)

    @pl.loop(0, count)
    def _(i):
        k = lst[i]
        bias = block_bias(sched, qinfo, k)
        for h in range(KVH):
            keys = kv[k, :, HS * h : HS * (h + 1)]
            values = kv[k, :, KV + HS * h : KV + HS * (h + 1)]
            s = nt(keys, q3[h]) + bias
            p = jnp.exp(s - lse[h : h + 1, :])
            ds = (p * (nt(values, do3[h]) - deltas[h])).astype(bf16)
            dkv_ref[k, :, HS * h : HS * (h + 1)] = mm(ds, q3[h]).astype(bf16)
            dkv_ref[k, :, KV + HS * h : KV + HS * (h + 1)] = mm(p.astype(bf16), do3[h]).astype(bf16)
            dq_t[h] = dq_t[h] + tn(keys, ds)

    for h in range(KVH):
        rows = (dq_t[h] * 0.125).T
        for g in range(GQ):
            j = GQ * h + g
            dq_scr[:, HS * j : HS * (j + 1)] = rows[BLK * g : BLK * (g + 1), :]
    cos, sin = cos_ref[...], sin_ref[...]
    for i in range(8):
        u = rope_back(dq_scr[:, 128 * i : 128 * (i + 1)], cos, sin).astype(bf16)
        if i < 7:
            dq_ref[:, 128 * i : 128 * (i + 1)] = u
        else:
            dq_ref[:, 128 * i :] = u[:, :HS]


def attend_back(scal, sched, qinfo, dy, db_own, db_got, m, gain, parts, q3, kv, o_t, lse, tables):
    n = kv.shape[0]
    return call(
        functools.partial(attend_back_body, n),
        "attend_back",
        2,
        [scal, sched, qinfo, dy, db_own, db_got, m, gain, *parts, q3, kv, o_t, lse, *tables],
        [
            shape((BLK, D), f32),
            shape((BLK, D), bf16),
            shape((1, D), f32),
            shape((BLK, D), bf16),
            shape((n, BLK, 2 * KV), bf16),
        ],
        [
            pltpu.SMEM((n,), i32),
            pltpu.VMEM((KVH, R3, HS), bf16),
            pltpu.VMEM((WA, BLK, SL), f32),
            pltpu.VMEM((BLK, D + 64), f32),
            pltpu.VMEM((KVH, HS, R3), f32),
        ],
        limit=8,
        us=12,
    )


def query_back_body(sc, dq, p0, p1, p2, p3, da, buf, sem):
    copies = [
        pltpu.make_async_copy(p, buf.at[m], sem.at[m]) for m, p in enumerate((p0, p1, p2, p3))
    ]
    for c in copies:
        c.start()
    for k, c in enumerate(copies):
        c.wait()
        da[sc[0] ^ k] = nt(dq[...], buf[k, :SL, 2 * KV : QKV])


def query_back(scal, dq, parts):
    return call(
        query_back_body,
        "query_back",
        1,
        [scal, dq, *parts],
        [shape((WA, BLK, SL), f32)],
        [pltpu.VMEM((WA, SL + 8, QKVP), bf16), pltpu.SemaphoreType.DMA((WA,))],
        specs=[VMEM] + [HBM] * WA,
        us=2,
    )[0]


def project_back_body(sc, own, go, back, cos_ref, sin_ref, da, x, dm, gain, gain_m, p0, p1, p2, p3, *refs):
    dkv_ref, dx_ref, dxl_ref, d4, buf, sem = refs
    copies = [
        pltpu.make_async_copy(p.at[:, pl.ds(0, 2 * KV)], buf.at[m], sem.at[m])
        for m, p in enumerate((p0, p1, p2, p3))
    ]
    for c in copies:
        c.start()
    total = own[...].astype(f32) + go[...].astype(f32) + back[...].astype(f32)
    cos, sin = cos_ref[...], sin_ref[...]
    edge = head_only((cos, sin))
    for i in range(2):
        dkv_ref[:BLK, 128 * i : 128 * (i + 1)] = rope_back(total[:, 128 * i : 128 * (i + 1)], cos, sin).astype(bf16)
    dkv_ref[:BLK, 256:384] = rope_back(total[:, 256:384], *edge).astype(bf16)
    dkv_ref[:BLK, 384:] = total[:, 384:].astype(bf16)
    for k, c in enumerate(copies):
        c.wait()
        d4[sc[0] ^ k] = da[sc[0] ^ k] + nt(dkv_ref[:BLK, :], buf[k, :SL, :])
    grads = jnp.concatenate([d4[j] for j in range(WA)], axis=1)
    part, gain_grad = norm_back(grads, x[...], gain[...])
    dkv_ref[BLK:, :] = jnp.zeros((8, 2 * KV), bf16)
    for i, g in enumerate((gain_grad, gain_m[...])):
        dkv_ref[BLK + 2 * i : BLK + 2 * i + 1, :] = g[:, : 2 * KV].astype(bf16)
        dkv_ref[BLK + 2 * i + 1 : BLK + 2 * i + 2, : D - 2 * KV] = g[:, 2 * KV :].astype(bf16)
    dx = dm[...] + part
    dx_ref[...] = dx
    dxl_ref[...] = dx.astype(bf16)


def project_back(scal, addends, tables, da, parts, x, dm, gain, gain_m_grad):
    return call(
        project_back_body,
        "project_back",
        1,
        [scal, *addends, *tables, da, x, dm, gain, gain_m_grad, *parts],
        [shape((BLK + 8, 2 * KV), bf16), shape((BLK, D), f32), shape((BLK, D), bf16)],
        [
            pltpu.VMEM((WA, BLK, SL), f32),
            pltpu.VMEM((WA, SL + 8, 2 * KV), bf16),
            pltpu.SemaphoreType.DMA((WA,)),
        ],
        us=2.5,
        specs=[VMEM] * 10 + [HBM] * WA,
    )


def grad_rows_body(has_prev, sc, *refs):
    out = refs[-1]
    slices = refs[:WA]
    lo = 0
    for t, kind in enumerate((0, 0, 1)):
        lows = refs[WA * (t + 1) : WA * (t + 2)]
        acc = None
        for sl, low in zip(slices, lows):
            part = tn(sl[kind], low[:BLK])
            acc = part if acc is None else acc + part
        width = acc.shape[1]
        if has_prev:
            acc = acc + refs[4 * WA][:SL, lo : lo + width]
            out[:SL, lo : lo + width] = acc.astype(bf16)
        else:
            out[:SL, lo : lo + width] = acc
        lo += width
    gains = sum(low[BLK:, :].astype(f32) for low in refs[WA : 2 * WA])
    rest = D - 2 * KV
    whole = jnp.concatenate(
        [
            jnp.concatenate([gains[2 * i : 2 * i + 1], gains[2 * i + 1 : 2 * i + 2, :rest]], axis=1)
            for i in range(2)
        ],
        axis=0,
    )
    if has_prev:
        whole = whole + refs[4 * WA][SL : SL + 2, :D]
    out[SL:, :] = jnp.zeros((256 - SL, lo), out.dtype)
    out[SL : SL + 2, :D] = whole.astype(out.dtype)


def grad_rows(scal, slices, dkvs, dqs, dms, prev, far=None):
    has_prev = prev is not None
    cols = QKV + D
    return call_fetched(
        functools.partial(grad_rows_body, has_prev),
        "grad_rows",
        scal,
        [*slices, *dkvs, *dqs, *dms] + ([prev] if has_prev else []),
        [shape((256, cols), bf16 if has_prev else f32)],
        us=4,
        limit=24,
        far=far,
        far_out=not has_prev,
    )[0]


def grad_ff_body(has_prev, sc, b0, b1, b2, b3, keep, got, *refs):
    out, bt = refs[-2:]
    for m, b in enumerate((b0, b1, b2, b3)):
        bt[:, BLK * m : BLK * (m + 1)] = b[...].astype(f32).T.astype(bf16)
    for gu in range(2):
        for j in range(WA):
            lhs = bt[SL * j : SL * (j + 1), :]
            acc = mm(lhs[:, : 2 * BLK], keep[gu]) + mm(lhs[:, 2 * BLK :], got[gu])
            for i in range(4):
                rows = min(64, SL - 64 * i)
                part = acc[64 * i : 64 * i + rows]
                if has_prev:
                    part = part + refs[0][4 * gu + i, j, :rows]
                out[4 * gu + i, j, :rows] = part.astype(out.dtype)
                if rows < 64:
                    out[4 * gu + i, j, rows:] = jnp.zeros((64 - rows, FFQ), out.dtype)


def grad_ff(scal, bs, keep, got, prev):
    has_prev = prev is not None
    return call_fetched(
        functools.partial(grad_ff_body, has_prev),
        "grad_ff",
        scal,
        [*bs, keep, got] + ([prev] if has_prev else []),
        [shape((8, WA, 64, FFQ), bf16 if has_prev else f32)],
        us=5,
        limit=32,
        scratch=[pltpu.VMEM((D, WA * BLK), bf16)],
        far=[False] * 6 + [True] * has_prev,
        far_out=not has_prev,
    )[0]


def grad_down_body(has_prev, sc, z, zg, l0, l1, l2, l3, *refs):
    out = refs[-1]
    acc = tn(z[:BLK], l0[...]) + tn(z[BLK:], l1[...])
    acc = acc + tn(zg[:BLK], l2[...]) + tn(zg[BLK:], l3[...])
    if has_prev:
        acc = acc + refs[0][...]
    out[...] = acc.astype(out.dtype)


def grad_down(scal, z, z_got, lows, prev):
    has_prev = prev is not None
    return call_fetched(
        functools.partial(grad_down_body, has_prev),
        "grad_down",
        scal,
        [z, z_got, *lows] + ([prev] if has_prev else []),
        [shape((FFQ, D), bf16 if has_prev else f32)],
        us=3,
        limit=20,
        far=[True, True] + [False] * 4 + [True] * has_prev,
        far_out=not has_prev,
    )[0]


def finish_ff_body(n, sc, *refs):
    gate, up = refs[n:]
    position, w = sc[3], sc[0]
    for k in range(n):
        p = (position - k + n) % n
        first = pl.multiple_of(64 * (p % 4), 8)
        for gu, out in enumerate((gate, up)):
            for rows in (64, SL - 192):

                @pl.when((p // 4 == gu) & ((p % 4 < 3) == (rows == 64)))
                def _():
                    for m in range(WA):
                        lo = pl.multiple_of(FFQ * (w ^ m), 128)
                        out[pl.ds(first, rows), pl.ds(lo, FFQ)] = refs[k][m, :rows].astype(f32)


def finish_ff(scal, gathered):
    return call_fetched(
        functools.partial(finish_ff_body, len(gathered)),
        "finish_ff",
        scal,
        list(gathered),
        [shape((SL, 4 * FFQ), f32)] * 2,
        us=4,
        limit=20,
        far=[False] * len(gathered),
    )


def finish_down_body(n, sc, *refs):
    out = refs[n]
    for k in range(n):
        p = (sc[3] - k + n) % n
        rows = refs[k].shape[0]
        out[pl.ds(pl.multiple_of(p * rows, 8), rows), :] = refs[k][...].astype(f32)


def finish_down(scal, gathered):
    return call_fetched(
        functools.partial(finish_down_body, len(gathered)),
        "finish_down",
        scal,
        list(gathered),
        [shape((FFQ, D), f32)],
        us=2.5,
        limit=20,
        far=[False] * len(gathered),
    )[0]


def finish_rows_body(n, widths, sc, *refs):
    *outs, gains = refs[n:]
    for k in range(n):
        p = (sc[3] - k + n) % n
        rows = refs[k].shape[0]
        tail = SL - rows * (n - 1)
        first = pl.multiple_of(p * rows, 8)

        @pl.when(p < n - 1)
        def _():
            lo = 0
            for out, width in zip(outs, widths):
                out[pl.ds(first, rows), :] = refs[k][:, lo : lo + width].astype(f32)
                lo += width

        @pl.when(p == n - 1)
        def _():
            lo = 0
            for out, width in zip(outs, widths):
                out[rows * (n - 1) :, :] = refs[k][:tail, lo : lo + width].astype(f32)
                lo += width
            gains[...] = refs[k][tail : tail + 8, :D].astype(f32)


def finish_rows(scal, gathered, widths):
    return call_fetched(
        functools.partial(finish_rows_body, len(gathered), tuple(widths)),
        "finish_rows",
        scal,
        list(gathered),
        [shape((SL, width), f32) for width in widths] + [shape((8, D), f32)],
        us=2.5,
        limit=20,
        far=[False] * len(gathered),
    )


def body(
    tokens,
    cotangent,
    segment_ids,
    block_order,
    gain_attn,
    w_query,
    key_projection,
    value_projection,
    w_out,
    gain_mlp,
    w_gate,
    w_up,
    w_down,
):
    n = block_order.shape[1]
    w = lax.axis_index("wa")
    r = lax.axis_index("ctx")
    core = w % 2
    row = w // 2
    position = ring_position(r, n)
    x_side = r % 2
    scal = jnp.stack([w, x_side, row, position, core]).astype(i32)

    blocks = ring_device((position - jnp.arange(n, dtype=i32)) % n, n)
    labels = jnp.arange(n, dtype=i32)
    order_row = block_order[0]
    anchors = jnp.sum(jnp.where(blocks[:, None] == labels[None, :], order_row[None, :], 0), axis=1)
    natural = anchors[0] * BLK + jnp.arange(BLK, dtype=i32)
    seg_labels = jnp.arange(SEQS, dtype=i32)
    sizes = jnp.sum((segment_ids[0][None, :] == seg_labels[:, None]).astype(i32), axis=1)
    before = (seg_labels[None, :] < seg_labels[:, None]).astype(i32)
    starts = jnp.sum(before * sizes[None, :], axis=1)
    start_of = jnp.max(jnp.where(starts[None, :] <= natural[:, None], starts[None, :], 0), axis=1)
    sched = jnp.concatenate([anchors, start_of[:1]]).astype(i32)
    qinfo = jnp.pad(
        jnp.stack([jnp.tile(natural, GQ), jnp.tile(start_of, GQ)]), ((0, 6), (0, 0))
    ).astype(i32)
    frequency = rope_base ** (-jnp.arange(HS // 2, dtype=f32) * 2.0 / HS)
    angles = (natural - start_of).astype(f32)[:, None] * frequency[None, :]
    tables = (jnp.tile(jnp.cos(angles), (1, 4)), jnp.tile(jnp.sin(angles), (1, 4)))

    gains_own = jnp.pad(jnp.stack([gain_attn, gain_mlp]), ((0, 6), (0, 0)))
    qkv_own = pack_qkv(scal, w_query, key_projection, value_projection, gains_own)
    qkv_across = swap(qkv_own, 2)
    qkv_side = swap(qkv_own, 1)
    out_own, keep, give, down_own = pack_rest(scal, after(w_out, qkv_own), w_gate, w_up, w_down)
    core_part = swap(give, 1)

    def y_half(gu):
        return jnp.stack(
            [
                lax.dynamic_index_in_dim(keep[gu], x_side, 0, keepdims=False),
                lax.dynamic_index_in_dim(core_part[gu], x_side, 0, keepdims=False),
            ]
        )

    gate_half, up_half = y_half(0), y_half(1)
    down_half = lax.dynamic_slice_in_dim(down_own, x_side * (FFQ // 2), FFQ // 2, 0)
    top = cotangent[0]
    first = tokens[0]
    cos, sin = tables
    (qkv_across, qkv_side, core_part, out_own, gate_half, up_half, down_half, top, first, cos, sin,
     sched, qinfo) = bar(
        qkv_across, qkv_side, core_part, out_own, gate_half, up_half, down_half, top, first, cos, sin,
        sched, qinfo)
    tables = (cos, sin)
    qkv_parts = [qkv_own, qkv_side, qkv_across, swap(qkv_across, 1)]

    def ring_keys(kv, extras, held):
        if n != 8:
            for e in extras:
                held.update(e(held))
            return ring_gather(kv, n, position)
        rows = BLK // 2
        ahead, behind = [kv], [kv]
        for step in range(4):
            more = extras[step](held)
            if step < 3:
                f, b = ring_shift(ahead[-1], n, 1), ring_shift(behind[-1], n, -1)
            else:
                f = ring_shift(ahead[-1][:rows], n, 1)
                b = ring_shift(behind[-1][rows:], n, -1)
            f, b, *values = bar(f, b, *more.values())
            ahead.append(f)
            behind.append(b)
            held.update(zip(more.keys(), values))
        far = jnp.concatenate([ahead[4], behind[4]], axis=0)
        return jnp.stack(ahead[:4] + [far] + behind[3:0:-1])

    def spread(dkv, extras, held):
        if n != 8:
            for e in extras:
                held.update(e(held))
            total = lax.psum_scatter(
                by_distance(dkv, n, position), "ctx", scatter_dimension=0, tiled=False
            )
            return (total, jnp.zeros_like(total), jnp.zeros_like(total))
        go = back = None
        for step in range(4):
            more = extras[step](held)
            if step == 0:
                go, back = ring_far(lambda k: dkv[k], n)
            else:
                go, back = ring_near(lambda k: dkv[k], n, 4 - step, go, back)
            go, back, *values = bar(go, back, *more.values())
            held.update(zip(more.keys(), values))
        return (dkv[0], go, back)

    gate_mine = swap(gate_half, 2)
    x, a4, q3, kv, gains = project(scal, [first], tables, qkv_parts)
    gain_a, gain_m = gains[0:1], gains[1:2]
    kv, out_own = bar(kv, out_own)
    held = dict(gate_mine=gate_mine)
    out_across = swap(out_own, 2)
    up_mine = swap(after(up_half, kv), 2)

    def gate_other(h):
        return side_swap(h["gate_mine"], n)

    extras = [
        lambda h: dict(out_side=swap(out_own, 1), gate_mine=h["gate_mine"]),
        lambda h: dict(out_across=out_across),
        lambda h: dict(out_diag=swap(h["out_across"], 1)),
        lambda h: dict(gate_other=gate_other(h), up_mine=up_mine),
    ]
    every = ring_keys(kv, extras, held)
    out_parts = [out_own, held["out_side"], held["out_across"], held["out_diag"]]
    up_other = side_swap(held["up_mine"], n)
    down_mine = swap(after(down_half, every), 2)
    *sl, o_t, lse, m, b = attend(scal, sched, qinfo, q3, every, x, a4, gain_m, out_parts)
    m, b, up_other, down_mine = bar(m, b, up_other, down_mine)
    b_side = swap(b, 1)
    down_other = side_swap(down_mine, n)
    down_far = jnp.concatenate(
        [
            jnp.where(x_side == 0, down_mine, down_other),
            jnp.where(x_side == 0, down_other, down_mine),
        ],
        axis=0,
    )
    ff_parts = [
        keep,
        core_part,
        held["gate_mine"],
        held["up_mine"],
        held["gate_other"],
        up_other,
        down_own,
        down_far,
    ]
    b_far = swap(b, 2)
    z, z_give, gu, y_own, y_side = mlp(scal, b, b_side, ff_parts)
    y_own, y_side, b_far, z_give = bar(y_own, y_side, b_far, z_give)
    kept0 = [x, q3, every, o_t, lse, m, gu, z]

    x, a4, q3, kv, _ = project(scal, [m, y_own, swap(y_side, 1)], tables, qkv_parts)
    kv, z_give, b_far = bar(kv, z_give, b_far)
    b0, b0_side, sl0 = b, b_side, sl
    held = {}
    extras = [
        lambda h: dict(z_got=swap(z_give, 2), b_diag=swap(b_far, 1)),
        lambda h: dict(s1=swap(sl0[1], 1), s2=swap(sl0[2], 2)),
        lambda h: dict(s3=swap(sl0[3], 3), top_side=swap(top, 1)),
        lambda h: dict(top_far=swap(top, 2)),
    ]
    every = ring_keys(kv, extras, held)
    kept0 += [
        held["z_got"],
        [b0, b0_side, b_far, held["b_diag"]],
        [sl0[0], held["s1"], held["s2"], held["s3"]],
    ]
    top_side, top_far = held["top_side"], held["top_far"]
    *sl, o_t, lse, m, b = attend(scal, sched, qinfo, q3, every, x, a4, gain_m, out_parts)
    m, b = bar(m, b)
    b_side = swap(b, 1)
    b_far = swap(b, 2)
    z, z_give, gu, y_own, y_side = mlp(scal, b, b_side, ff_parts)
    y_own, y_side, b_far, z_give, z, top = bar(y_own, y_side, b_far, z_give, z, top)

    y_got = swap(y_side, 1)
    z_got = swap(z_give, 2)
    keep_d, give_d, db_own, db_side = mlp_back(scal, top, top_side, gu, ff_parts)
    db_own, db_side, give_d, z_got, y_got = bar(db_own, db_side, give_d, z_got, y_got)
    output = (m + y_own + y_got).astype(bf16)[None]
    db_got = swap(db_side, 1)
    got_d = swap(give_d, 2)
    b_diag = swap(b_far, 1)
    top_diag = swap(top_far, 1)
    dm, dml, gain_m_1, dq, dkv = attend_back(
        scal, sched, qinfo, top, db_own, db_got, m, gain_m, out_parts, q3, every, o_t, lse, tables
    )
    dkv, dq, dml, b_diag, top_diag = bar(dkv, dq, dml, b_diag, top_diag)
    lows = [top, top_side, top_far, top_diag]
    bs = [b, b_side, b_far, b_diag]
    sl1, keep_d1, z1 = sl, keep_d, z
    held = {}
    extras = [
        lambda h: dict(got_d=got_d, down_1=grad_down(scal, z1, z_got, lows, None)),
        lambda h: dict(
            s1=swap(sl1[1], 1), s2=swap(sl1[2], 2), da=query_back(scal, dq, qkv_parts)
        ),
        lambda h: dict(
            s3=swap(sl1[3], 3), dq_far=swap(dq, 2), ff_1=grad_ff(scal, bs, keep_d1, h["got_d"], None)
        ),
        lambda h: dict(dq_side=swap(dq, 1), dml_side=swap(dml, 1), dml_far=swap(dml, 2)),
    ]
    addends = spread(dkv, extras, held)
    down_1, ff_1 = held["down_1"], held["ff_1"]
    dq_diag, dml_diag = swap(held["dq_far"], 1), swap(held["dml_far"], 1)
    dkv0, dx, low = project_back(
        scal, addends, tables, held["da"], qkv_parts, x, dm, gain_a, gain_m_1
    )
    dx, low, dkv0, dq_diag, dml_diag = bar(dx, low, dkv0, dq_diag, dml_diag)
    slices_1 = [sl[0], held["s1"], held["s2"], held["s3"]]
    dqs_1 = [dq, held["dq_side"], held["dq_far"], dq_diag]
    dmls_1 = [dml, held["dml_side"], held["dml_far"], dml_diag]

    x, q3, every, o_t, lse, m, gu, z, z_got, bs0, slices = kept0
    low_side = swap(low, 1)
    low_far = swap(low, 2)
    keep_d, give_d, db_own, db_side = mlp_back(scal, low, low_side, gu, ff_parts)
    db_own, db_side, give_d, low_far = bar(db_own, db_side, give_d, low_far)
    db_got = swap(db_side, 1)
    low_diag = swap(low_far, 1)
    dkv_side, dkv_far = swap(dkv0, 1), swap(dkv0, 2)
    down_grad = grad_down(scal, z, z_got, [low, low_side, low_far, low_diag], down_1)
    db_got, down_grad = bar(db_got, down_grad)
    down_piece = at_position(down_grad.reshape(n, FFQ // n, D), n, position)
    got_d = swap(give_d, 2)
    held = {}
    if n == 8:
        held["down"] = ring_far(down_piece, n)
    dm, dml, gain_m_0, dq, dkv = attend_back(
        scal, sched, qinfo, dx, db_own, db_got, m, gain_m, out_parts, q3, every, o_t, lse, tables
    )
    dkv, dq, dml, got_d, dkv_side, dkv_far = bar(dkv, dq, dml, got_d, dkv_side, dkv_far)
    dkvs_1 = [dkv0, dkv_side, dkv_far]

    def ff_piece_of(ff):
        sub = n // 8
        pieces = ff.reshape(8, WA, sub, 64 // sub, FFQ).transpose(0, 2, 1, 3, 4)
        return pieces.reshape(n, WA, 64 // sub, FFQ)

    def down_step(k, h):
        if n != 8:
            return {}
        go, back = h.get("down_go"), h.get("down_back")
        if go is None:
            go, back = h["down"]
        go, back = ring_near(down_piece, n, k, go, back)
        return dict(down_go=go, down_back=back)

    keep_d0, dq0, dml0 = keep_d, dq, dml
    extras = [
        lambda h: dict(
            dq_far=swap(dq0, 2), ff=grad_ff(scal, bs0, keep_d0, got_d, ff_1), **down_step(3, h)
        ),
        lambda h: dict(dml_far=swap(dml0, 2), da=query_back(scal, dq0, qkv_parts), **down_step(2, h)),
        lambda h: dict(dkv_diag=swap(dkv_far, 1), **down_step(1, h)),
        lambda h: dict(dq_side=swap(dq0, 1), dml_side=swap(dml0, 1)),
    ]
    addends = spread(dkv, extras, held)
    dkv0, dx, low = project_back(
        scal, addends, tables, held["da"], qkv_parts, x, dm, gain_a, gain_m_0
    )
    input_grad = low[None]

    ff_pieces = ff_piece_of(held["ff"])
    if n == 8:
        down_mine = total_low(down_piece(0), held["down_go"], held["down_back"])
        down_all = ring_gather(down_mine, n, position)
        ff_mine = total_low(*ring_scatter(at_position(ff_pieces, n, position), n))
    else:
        down_all = ring_sum(down_grad.reshape(n, FFQ // n, D), n, position)
        ff_mine = lax.psum_scatter(ff_pieces, "ctx", scatter_dimension=0, tiled=False)
    ff_all = ring_gather(rows_home(ff_mine, w), n, position)
    rows_1 = grad_rows(scal, slices_1, dkvs_1 + [held["dkv_diag"]], dqs_1, dmls_1, None)
    dqs = [dq, held["dq_side"], held["dq_far"], swap(held["dq_far"], 1)]
    dmls = [dml, held["dml_side"], held["dml_far"], swap(held["dml_far"], 1)]
    rows_grad = grad_rows(scal, slices, everyone(dkv0), dqs, dmls, rows_1)
    rows_all = ring_sum(rows_grad.reshape(n, 256 // n, QKV + D), n, position)
    if n == 8:
        down_total = finish_down(scal, down_all)
        gate_total, up_total = finish_ff(scal, ff_all)
        key_total, value_total, query_total, out_total, gain_rows = finish_rows(
            scal, rows_all, [KV, KV, D, D]
        )
    else:
        sub = n // 8
        whole = placed(ff_all, n, position).reshape(2, 4, sub, WA, 64 // sub, FFQ)
        whole = whole.transpose(0, 3, 1, 2, 4, 5).reshape(2, WA, 256, FFQ)[:, :, :SL]
        whole = jnp.take(whole, w ^ jnp.arange(WA, dtype=i32), axis=1).transpose(0, 2, 1, 3)
        gate_total, up_total = whole.reshape(2, SL, -1).astype(f32)
        down_total = placed(down_all, n, position).reshape(FFQ, D).astype(f32)
        rows_total = placed(rows_all, n, position).reshape(256, QKV + D).astype(f32)
        gain_rows = rows_total[SL:, :D]
        rows_total = rows_total[:SL]
        key_total, value_total, query_total, out_total = (
            rows_total[:, :KV],
            rows_total[:, KV : 2 * KV],
            rows_total[:, 2 * KV : QKV],
            rows_total[:, QKV:],
        )
    gain_rows = lax.dynamic_slice_in_dim(gain_rows[:2], w * SL, SL, 1)
    return (
        output,
        input_grad,
        gain_rows[0],
        query_total,
        key_total,
        value_total,
        out_total,
        gain_rows[1],
        gate_total,
        up_total,
        down_total,
    )


def solution(mesh):
    rows = P("wa", None)
    flat = P("wa")
    act = P("wa", "ctx", None)
    return jax.shard_map(
        body,
        mesh=mesh,
        in_specs=(act, act, rows, rows, flat, rows, rows, rows, rows, flat, rows, rows, rows),
        out_specs=(act, act, flat, rows, rows, rows, rows, flat, rows, rows, rows),
        check_vma=False,
    )
```

```python
import functools

import jax
import jax.numpy as jnp
from jax import lax
from jax.experimental import pallas as pl
from jax.experimental.pallas import tpu as pltpu
from jax.sharding import PartitionSpec as P

QH = 15
KVH = 5
GQ = QH // KVH
HS = 64
SEQS = 8
REPEATS = 2
WA = 4
BLK = 128
D = 960
SL = D // WA
KV = KVH * HS
QKV = 2 * KV + D
FFQ = 640
R3 = GQ * BLK
QKVP = 1664

epsilon = 1e-05
masked_score = -1e30
rope_base = 10000.0
bf16 = jnp.bfloat16
f32 = jnp.float32
i32 = jnp.int32
MB = 1 << 20


def swap(x, mask):
    return lax.ppermute(x, "wa", [(i, i ^ mask) for i in range(WA)])


def side_swap(x, n):
    return lax.ppermute(x, "ctx", [(i, i ^ 1) for i in range(n)])


def ring_order(n):
    return [i for i in range(0, n, 2)] + [i for i in range(n - 1, 0, -2)]


def ring_shift(x, n, step):
    order = ring_order(n)
    return lax.ppermute(x, "ctx", [(order[i], order[(i + step) % n]) for i in range(n)])


def ring_position(r, n):
    return jnp.where(r % 2 == 0, r // 2, n - 1 - r // 2) if n == 8 else r


def ring_device(p, n):
    return jnp.where(p < n // 2, 2 * p, 2 * (n - 1 - p) + 1) if n == 8 else p


def after(x, *others):
    return lax.optimization_barrier((x,) + others)[0]


def bar(*xs):
    return lax.optimization_barrier(xs)


def by_distance(x, n, position):
    return jnp.take(x, (position - jnp.arange(n, dtype=i32)) % n, axis=0)


def ring_gather(x, n, position):
    if n != 8:
        return by_distance(lax.all_gather(x, "ctx"), n, position)
    half = n // 2
    rows = x.shape[0] // 2
    ahead = [x]
    behind = [x]
    for _ in range(half - 1):
        ahead.append(ring_shift(ahead[-1], n, 1))
        behind.append(ring_shift(behind[-1], n, -1))
    far = jnp.concatenate(
        [ring_shift(ahead[-1][:rows], n, 1), ring_shift(behind[-1][rows:], n, -1)], axis=0
    )
    return ahead + [far] + behind[:0:-1]


def add_low(x, y):
    return (x.astype(f32) + y.astype(f32)).astype(bf16)


def ring_far(piece, n):
    far = piece(n // 2)
    rows = far.shape[0] // 2
    return ring_shift(far[:rows], n, 1), ring_shift(far[rows:], n, -1)


def ring_near(piece, n, k, go, back):
    ahead, behind = piece(n - k), piece(k)
    if go.shape != ahead.shape:
        rows = go.shape[0]
        go = jnp.concatenate([add_low(ahead[:rows], go), ahead[rows:]], axis=0)
        back = jnp.concatenate([behind[:rows], add_low(behind[rows:], back)], axis=0)
    else:
        go, back = add_low(ahead, go), add_low(behind, back)
    return ring_shift(go, n, 1), ring_shift(back, n, -1)


def ring_scatter(piece, n):
    go, back = ring_far(piece, n)
    for k in range(n // 2 - 1, 0, -1):
        go, back = ring_near(piece, n, k, go, back)
    return piece(0), go, back


def total_low(own, go, back):
    return (own.astype(f32) + go.astype(f32) + back.astype(f32)).astype(bf16)


def at_position(pieces, n, position):
    return lambda k: lax.dynamic_index_in_dim(pieces, (position - k) % n, 0, keepdims=False)


def ring_sum(pieces, n, position):
    if n != 8:
        mine = lax.psum_scatter(pieces, "ctx", scatter_dimension=0, tiled=False)
    else:
        mine = total_low(*ring_scatter(at_position(pieces, n, position), n))
    return ring_gather(mine, n, position)


def rows_home(mine, w):
    out = []
    for mask in range(WA):
        block = lax.dynamic_index_in_dim(mine, w ^ mask, 0, keepdims=False)
        out.append(swap(block, mask) if mask else block)
    return jnp.stack(out)


def placed(gathered, n, position):
    if n != 8:
        return by_distance(gathered, n, position)
    out = jnp.zeros((n,) + gathered[0].shape, bf16)
    for k in range(n):
        out = lax.dynamic_update_index_in_dim(out, gathered[k], (position - k) % n, 0)
    return out


def everyone(x):
    side = swap(x, 1)
    across = swap(x, 2)
    return [x, side, across, swap(across, 1)]


VMEM = pl.BlockSpec(memory_space=pltpu.VMEM)
SMEM = pl.BlockSpec(memory_space=pltpu.SMEM)


ANY = pl.BlockSpec(memory_space=pl.ANY)
HBM = pl.BlockSpec(memory_space=pltpu.HBM)


def call(body, name, n_scalar, ins, outs, scratch=(), us=2.0, limit=10, specs=None, out_specs=None):
    specs = specs or [VMEM] * (len(ins) - n_scalar)
    ins = list(ins[:n_scalar]) + [
        pltpu.with_memory_space_constraint(x, pltpu.HBM) if spec is HBM else x
        for x, spec in zip(ins[n_scalar:], specs)
    ]
    return pl.pallas_call(
        body,
        name=name,
        in_specs=[SMEM] * n_scalar + specs,
        out_specs=out_specs or [VMEM] * len(outs),
        out_shape=list(outs),
        scratch_shapes=list(scratch),
        cost_estimate=pl.CostEstimate(flops=int(us * 1.15e9), transcendentals=0, bytes_accessed=1 << 16),
        compiler_params=pltpu.CompilerParams(vmem_limit_bytes=limit * MB),
    )(*ins)


def fetched(refs, bufs, sem):
    copies = [pltpu.make_async_copy(r, b, sem.at[i]) for i, (r, b) in enumerate(zip(refs, bufs))]
    for c in copies:
        c.start()
    for c in copies:
        c.wait()


def call_fetched(body, name, scal, ins, outs, us, limit, scratch=(), far=None, far_out=False):
    count, n_out = len(ins), len(outs)
    far = far or [False] * count

    def whole(sc, *refs):
        sources, results = refs[:count], refs[count : count + n_out]
        bufs = refs[count + n_out : 2 * count + n_out]
        sem, rest = refs[2 * count + n_out], refs[2 * count + n_out + 1 :]
        fetched(sources, bufs, sem)
        if not far_out:
            body(sc, *bufs, *results, *rest)
            return
        body(sc, *bufs, *rest)
        fetched(rest[:n_out], results, sem)

    bufs = [pltpu.VMEM(x.shape, x.dtype) for x in ins]
    held = [pltpu.VMEM(x.shape, x.dtype) for x in outs] if far_out else []
    return call(
        whole,
        name,
        1,
        [scal, *ins],
        outs,
        bufs + [pltpu.SemaphoreType.DMA((max(count, n_out),)), *held, *scratch],
        us=us,
        limit=limit,
        specs=[HBM if f else ANY for f in far],
        out_specs=[ANY] * n_out if far_out else None,
    )


def shape(dims, dtype):
    return jax.ShapeDtypeStruct(dims, dtype)


def mm(a, b):
    return jnp.dot(a, b, preferred_element_type=f32)


def nt(a, b):
    return lax.dot_general(a, b, (((1,), (1,)), ((), ())), preferred_element_type=f32)


def tn(a, b):
    return lax.dot_general(a, b, (((0,), (0,)), ((), ())), preferred_element_type=f32)


def turn(u):
    lane = lax.broadcasted_iota(i32, u.shape, 1) % HS
    return jnp.where(lane < HS // 2, -pltpu.roll(u, 128 - HS // 2, 1), pltpu.roll(u, HS // 2, 1))


def turn_back(u):
    lane = lax.broadcasted_iota(i32, u.shape, 1) % HS
    return jnp.where(lane < HS // 2, pltpu.roll(u, 128 - HS // 2, 1), -pltpu.roll(u, HS // 2, 1))


def rope(u, cos, sin):
    return u * cos + turn(u) * sin


def rope_back(u, cos, sin):
    return u * cos + turn_back(u * sin)


def pack_qkv_body(sc, wq, wk, wv, gains, out):
    out[:SL, :KV] = wk[...].T.astype(bf16)
    out[:SL, KV : 2 * KV] = wv[...].T.astype(bf16)
    out[:SL, 2 * KV : QKV] = wq[...].astype(bf16)
    out[:SL, QKV:] = jnp.zeros((SL, QKVP - QKV), bf16)
    out[SL:, :] = jnp.zeros((8, QKVP), bf16)
    out[SL:, :SL] = gains[...].astype(bf16)


def pack_qkv(scal, wq, wk, wv, gains):
    ins = [wq, wk.T, wv.T, gains]
    outs = [shape((SL + 8, QKVP), bf16)]
    return call_fetched(pack_qkv_body, "pack_qkv", scal, ins, outs, us=3, limit=8, far=[True] * 3 + [False])[0]


def pack_rest_body(sc, w_out, w_gate, w_up, w_down, out_ref, keep, give, down):
    core = sc[4]
    out_ref[...] = w_out[...].astype(bf16)
    down[...] = w_down[...].T.astype(bf16)
    for gu, src in enumerate((w_gate, w_up)):
        for t in range(2):
            lo = pl.multiple_of(FFQ * (2 * t + core), 128)
            keep[gu, t] = src[:, pl.ds(lo, FFQ)].astype(bf16)
            lo = pl.multiple_of(FFQ * (2 * t + 1 - core), 128)
            give[gu, t] = src[:, pl.ds(lo, FFQ)].astype(bf16)


def pack_rest(scal, w_out, w_gate, w_up, w_down):
    quarters = shape((2, 2, SL, FFQ), bf16)
    outs = [shape((SL, D), bf16), quarters, quarters, shape((FFQ, D), bf16)]
    ins = [w_out, w_gate, w_up, w_down.T]
    return call_fetched(pack_rest_body, "pack_rest", scal, ins, outs, us=6, limit=24, far=[True] * 4)


def head_only(tables):
    cos, sin = tables
    lane = lax.broadcasted_iota(i32, cos.shape, 1)
    return jnp.where(lane < HS, cos, 1.0), jnp.where(lane < HS, sin, 0.0)


def project_body(n_in, sc, *refs):
    xs = refs[:n_in]
    cos_ref, sin_ref, *parts = refs[n_in : n_in + 6]
    x_ref, a4, q3, kv, gains, acc_ref, x4, g4, buf, sem = refs[n_in + 6 :]
    copies = [pltpu.make_async_copy(p, buf.at[m], sem.at[m]) for m, p in enumerate(parts)]
    for c in copies:
        c.start()
    x = xs[0][...].astype(f32)
    for r in xs[1:]:
        x = x + r[...]
    x_ref[...] = x
    ratio = lax.rsqrt(jnp.mean(x * x, axis=1, keepdims=True) + epsilon)
    x = x * ratio
    for j in range(WA):
        x4[j] = x[:, SL * j : SL * (j + 1)]
    acc = None
    for m in range(WA):
        copies[m].wait()
        j = sc[0] ^ m
        gain = buf[m, SL:, :SL].astype(f32)
        g4[j] = gain
        a = (x4[j] * gain[:1]).astype(bf16)
        a4[j] = a
        part = mm(a, buf[m, :SL, :])
        acc = part if acc is None else acc + part
    gains[...] = jnp.concatenate([g4[j] for j in range(WA)], axis=1)
    acc_ref[...] = acc
    cos, sin = cos_ref[...], sin_ref[...]
    edge = head_only((cos, sin))
    for i in range(2):
        kv[:, 128 * i : 128 * (i + 1)] = rope(acc_ref[:, 128 * i : 128 * (i + 1)], cos, sin).astype(bf16)
    kv[:, 256:384] = rope(acc_ref[:, 256:384], *edge).astype(bf16)
    kv[:, 384:640] = acc_ref[:, 384:640].astype(bf16)
    for i in range(8):
        lo = 2 * KV + 128 * i
        u = rope(acc_ref[:, lo : lo + 128], cos, sin).astype(bf16) * bf16(0.125)
        for j in range(2):
            h = 2 * i + j
            if h < QH:
                q3[h // GQ, BLK * (h % GQ) : BLK * (h % GQ + 1), :] = u[:, HS * j : HS * (j + 1)]


def project(scal, xs, tables, parts):
    return call(
        functools.partial(project_body, len(xs)),
        "project",
        1,
        [scal, *xs, *tables, *parts],
        [
            shape((BLK, D), f32),
            shape((WA, BLK, SL), bf16),
            shape((KVH, R3, HS), bf16),
            shape((BLK, 2 * KV), bf16),
            shape((8, D), f32),
        ],
        [
            pltpu.VMEM((BLK, QKVP), f32),
            pltpu.VMEM((WA, BLK, SL), f32),
            pltpu.VMEM((WA, 8, SL), f32),
            pltpu.VMEM((WA, SL + 8, QKVP), bf16),
            pltpu.SemaphoreType.DMA((WA,)),
        ],
        us=3,
        limit=10,
        specs=[VMEM] * (len(xs) + 2) + [ANY] * WA,
    )


def list_blocks(sched, lst, n):
    def step(k, count):
        first = sched[k] * BLK
        seen = (sched[k] <= sched[0]) & (first + BLK > sched[n])

        @pl.when(seen)
        def _():
            lst[count] = k

        return count + seen.astype(i32)

    return lax.fori_loop(0, n, step, jnp.int32(0))


def block_bias(sched, qinfo, k):
    key = sched[k] * BLK + lax.broadcasted_iota(i32, (BLK, R3), 0)
    ok = (key <= qinfo[0:1, :]) & (key >= qinfo[1:2, :])
    return jnp.where(ok, 0.0, masked_score).astype(f32)


def attend_body(n, sc, sched, qinfo, q3, kv, x, a4, gain, p0, p1, p2, p3, *refs):
    sl = refs[:WA]
    o_t, lse, m_ref, b_ref, lst, o_scr, ol4 = refs[WA:]
    count = list_blocks(sched, lst, n)
    o_t[...] = jnp.zeros(o_t.shape, f32)

    def step(i, state):
        k = lst[i]
        bias = block_bias(sched, qinfo, k)
        out = []
        for h in range(KVH):
            top, total = state[h]
            s = nt(kv[k, :, HS * h : HS * (h + 1)], q3[h]) + bias
            new = jnp.maximum(top, jnp.max(s, axis=0, keepdims=True))
            p = jnp.exp(s - new)
            fix = jnp.exp(top - new)
            values = kv[k, :, KV + HS * h : KV + HS * (h + 1)]
            o_t[h] = o_t[h] * fix + tn(values, p.astype(bf16))
            out.append((new, total * fix + jnp.sum(p, axis=0, keepdims=True)))
        return tuple(out)

    start = tuple(
        (jnp.full((1, R3), masked_score, f32), jnp.zeros((1, R3), f32)) for _ in range(KVH)
    )
    state = lax.fori_loop(0, count, step, start)
    for h in range(KVH):
        top, total = state[h]
        out = o_t[h] * (1.0 / total)
        o_t[h] = out
        lse[h : h + 1, :] = top + jnp.log(total)
        rows = out.T
        for g in range(GQ):
            j = GQ * h + g
            o_scr[:, HS * j : HS * (j + 1)] = rows[BLK * g : BLK * (g + 1), :]
    low = o_scr[...].astype(bf16)
    for j in range(WA):
        ol4[j] = low[:, SL * j : SL * (j + 1)]
    m = x[...]
    for k, p in enumerate((p0, p1, p2, p3)):
        j = sc[0] ^ k
        sl[k][0] = a4[j]
        sl[k][1] = ol4[j]
        m = m + mm(ol4[j], p[...])
    m_ref[...] = m
    ratio = lax.rsqrt(jnp.mean(m * m, axis=1, keepdims=True) + epsilon)
    b = (m * ratio * gain[...]).astype(bf16)
    b_ref[...] = b


def attend(scal, sched, qinfo, q3, kv, x, a4, gain, parts):
    n = kv.shape[0]
    return call(
        functools.partial(attend_body, n),
        "attend",
        2,
        [scal, sched, qinfo, q3, kv, x, a4, gain, *parts],
        [
            *[shape((2, BLK, SL), bf16)] * WA,
            shape((KVH, HS, R3), f32),
            shape((8, R3), f32),
            shape((BLK, D), f32),
            shape((BLK, D), bf16),
        ],
        [
            pltpu.SMEM((n,), i32),
            pltpu.VMEM((BLK, D), f32),
            pltpu.VMEM((WA, BLK, SL), bf16),
        ],
        limit=8,
        us=10,
    )


def mlp_body(sc, b_own, b_side, keep, core, gm, um, go, uo, d_own, d_far, *refs):
    z_hbm, z_give, gu_hbm, y_own, y_side, bs, z_ref, gu_ref, sem = refs
    copies = []
    w = sc[0]
    for half, b in enumerate((b_own, b_side)):
        for j in range(WA):
            bs[j, BLK * half : BLK * (half + 1), :] = b[:, SL * j : SL * (j + 1)]
    for t, fars in ((sc[1], (gm, um)), (1 - sc[1], (go, uo))):
        lin = []
        for gu in range(2):
            acc = mm(bs[w], keep[gu, t]) + mm(bs[w ^ 1], core[gu, t])
            acc = acc + mm(bs[w ^ 2], fars[gu][0]) + mm(bs[w ^ 3], fars[gu][1])
            gu_ref[gu, t] = acc
            lin.append(acc)
        for gu in range(2):
            c = pltpu.make_async_copy(gu_ref.at[gu, t], gu_hbm.at[gu, t], sem.at[len(copies)])
            c.start()
            copies.append(c)
        gate, up = lin
        z_ref[t] = (gate / (1.0 + jnp.exp(-gate)) * up).astype(bf16)
    row = sc[2]
    copies.append(pltpu.make_async_copy(z_ref.at[row], z_hbm, sem.at[4]))
    copies[4].start()
    out = mm(z_ref[row], d_own[...]) + mm(z_ref[1 - row], d_far[...])
    y_own[...] = out[:BLK]
    y_side[...] = out[BLK:]
    z_give[...] = z_ref[1 - row]
    for c in copies:
        c.wait()


def mlp(scal, b_own, b_side, wts):
    return call(
        mlp_body,
        "mlp",
        1,
        [scal, b_own, b_side, *wts],
        [
            shape((2 * BLK, FFQ), bf16),
            shape((2 * BLK, FFQ), bf16),
            shape((2, 2, 2 * BLK, FFQ), f32),
            shape((BLK, D), f32),
            shape((BLK, D), f32),
        ],
        [
            pltpu.VMEM((WA, 2 * BLK, SL), bf16),
            pltpu.VMEM((2, 2 * BLK, FFQ), bf16),
            pltpu.VMEM((2, 2, 2 * BLK, FFQ), f32),
            pltpu.SemaphoreType.DMA((5,)),
        ],
        out_specs=[ANY, VMEM, ANY, VMEM, VMEM],
        limit=12,
        us=5.5,
    )


def mlp_back_body(sc, l_own, l_side, gu_hbm, keep, core, gm, um, go, uo, d_own, d_far, *refs):
    keep_ref, give_ref, db_own, db_side, low, acc, gu_ref, sem = refs
    copies = [
        [pltpu.make_async_copy(gu_hbm.at[gu, t], gu_ref.at[gu, t], sem.at[2 * i + gu]) for gu in range(2)]
        for i, t in enumerate((sc[1], 1 - sc[1]))
    ]
    for c in copies[0] + copies[1]:
        c.start()
    w, row = sc[0], sc[2]
    low[:BLK] = l_own[...]
    low[BLK:] = l_side[...]
    for first, (t, fg, fu) in enumerate(((sc[1], gm, um), (1 - sc[1], go, uo))):
        dz = jnp.where(t == row, nt(low[...], d_own[...]), nt(low[...], d_far[...]))
        for c in copies[first]:
            c.wait()
        gate, up = gu_ref[0, t], gu_ref[1, t]
        sig = 1.0 / (1.0 + jnp.exp(-gate))
        dg = (dz * up * sig * (1.0 + gate * (1.0 - sig))).astype(bf16)
        du = (dz * gate * sig).astype(bf16)

        @pl.when(t == row)
        def _():
            keep_ref[0] = dg
            keep_ref[1] = du

        @pl.when(t != row)
        def _():
            give_ref[0] = dg
            give_ref[1] = du

        for j, p in ((w, keep.at[0, t]), (w ^ 1, core.at[0, t]), (w ^ 2, fg.at[0]), (w ^ 3, fg.at[1])):
            part = nt(dg, p[...])
            acc[j] = part if first == 0 else acc[j] + part
        for j, p in ((w, keep.at[1, t]), (w ^ 1, core.at[1, t]), (w ^ 2, fu.at[0]), (w ^ 3, fu.at[1])):
            acc[j] = acc[j] + nt(du, p[...])
    for j in range(WA):
        db_own[:, SL * j : SL * (j + 1)] = acc[j, :BLK, :]
        db_side[:, SL * j : SL * (j + 1)] = acc[j, BLK:, :]


def mlp_back(scal, l_own, l_side, gu, wts):
    return call(
        mlp_back_body,
        "mlp_back",
        1,
        [scal, l_own, l_side, gu, *wts],
        [
            shape((2, 2 * BLK, FFQ), bf16),
            shape((2, 2 * BLK, FFQ), bf16),
            shape((BLK, D), f32),
            shape((BLK, D), f32),
        ],
        [
            pltpu.VMEM((2 * BLK, D), bf16),
            pltpu.VMEM((WA, 2 * BLK, SL), f32),
            pltpu.VMEM((2, 2, 2 * BLK, FFQ), f32),
            pltpu.SemaphoreType.DMA((4,)),
        ],
        specs=[VMEM, VMEM, ANY] + [VMEM] * 8,
        limit=12,
        us=6.7,
    )


def norm_back(grads, hidden, gain):
    ratio = lax.rsqrt(jnp.mean(hidden * hidden, axis=1, keepdims=True) + epsilon)
    scaled = hidden * ratio
    gain_grad = jnp.sum(grads * scaled, axis=0, keepdims=True)
    inner = grads * gain
    out = ratio * (inner - scaled * jnp.mean(inner * scaled, axis=1, keepdims=True))
    return out, gain_grad


def attend_back_body(n, far, sc, sched, qinfo, dy, db_own, db_got, gain, lse, cos_ref, sin_ref, *refs):
    (m, *parts, q3, kv, o_t), refs = refs[:8], refs[8:]
    dm_ref, dml_ref, gg, dq_ref, dkv_ref, lst, do3, d_scr, dq_scr, dq_t = refs[:10]
    waits = []
    if far:
        bufs, sem = refs[10:18], refs[18]
        copies = [
            pltpu.make_async_copy(a, b, sem.at[i])
            for i, (a, b) in enumerate(zip((m, *parts, q3, kv, o_t), bufs))
        ]
        for c in copies:
            c.start()
        m, *parts, q3, kv, o_t = bufs
        copies[0].wait()
        waits = copies[1:]
    count = list_blocks(sched, lst, n)
    part, gain_grad = norm_back(db_own[...] + db_got[...], m[...], gain[...])
    gg[...] = gain_grad
    dm = dy[...].astype(f32) + part
    dm_ref[...] = dm
    dml = dm.astype(bf16)
    dml_ref[...] = dml
    for c in waits:
        c.wait()
    for k, p in enumerate(parts):
        d_scr[sc[0] ^ k] = nt(dml, p[...]).astype(bf16).astype(f32)
    whole = jnp.concatenate([d_scr[j] for j in range(WA)], axis=1)
    for j in range(QH):
        do3[j // GQ, BLK * (j % GQ) : BLK * (j % GQ + 1), :] = whole[:, HS * j : HS * (j + 1)].astype(bf16)

    @pl.loop(1, n)
    def _(k):
        seen = (sched[k] <= sched[0]) & (sched[k] * BLK + BLK > sched[n])

        @pl.when(jnp.logical_not(seen))
        def _():
            dkv_ref[k] = jnp.zeros((BLK, 2 * KV), bf16)

    deltas = [
        jnp.sum(do3[h].astype(f32).T * o_t[h], axis=0, keepdims=True) for h in range(KVH)
    ]
    dq_t[...] = jnp.zeros(dq_t.shape, f32)

    @pl.loop(0, count)
    def _(i):
        k = lst[i]
        bias = block_bias(sched, qinfo, k)
        for h in range(KVH):
            keys = kv[k, :, HS * h : HS * (h + 1)]
            values = kv[k, :, KV + HS * h : KV + HS * (h + 1)]
            s = nt(keys, q3[h]) + bias
            p = jnp.exp(s - lse[h : h + 1, :])
            ds = (p * (nt(values, do3[h]) - deltas[h])).astype(bf16)
            dkv_ref[k, :, HS * h : HS * (h + 1)] = mm(ds, q3[h]).astype(bf16)
            dkv_ref[k, :, KV + HS * h : KV + HS * (h + 1)] = mm(p.astype(bf16), do3[h]).astype(bf16)
            dq_t[h] = dq_t[h] + tn(keys, ds)

    for h in range(KVH):
        rows = (dq_t[h] * 0.125).T
        for g in range(GQ):
            j = GQ * h + g
            dq_scr[:, HS * j : HS * (j + 1)] = rows[BLK * g : BLK * (g + 1), :]
    cos, sin = cos_ref[...], sin_ref[...]
    for i in range(8):
        u = rope_back(dq_scr[:, 128 * i : 128 * (i + 1)], cos, sin).astype(bf16)
        if i < 7:
            dq_ref[:, 128 * i : 128 * (i + 1)] = u
        else:
            dq_ref[:, 128 * i :] = u[:, :HS]


def attend_back(far, scal, sched, qinfo, dy, db_own, db_got, m, gain, parts, q3, kv, o_t, lse, tables):
    n = kv.shape[0]
    kept = [m, *parts, q3, kv, o_t]
    bufs = [pltpu.VMEM(x.shape, x.dtype) for x in kept] + [pltpu.SemaphoreType.DMA((8,))]
    return call(
        functools.partial(attend_back_body, n, far),
        "attend_back",
        2,
        [scal, sched, qinfo, dy, db_own, db_got, gain, lse, *tables, *kept],
        [
            shape((BLK, D), f32),
            shape((BLK, D), bf16),
            shape((1, D), f32),
            shape((BLK, D), bf16),
            shape((n, BLK, 2 * KV), bf16),
        ],
        [
            pltpu.SMEM((n,), i32),
            pltpu.VMEM((KVH, R3, HS), bf16),
            pltpu.VMEM((WA, BLK, SL), f32),
            pltpu.VMEM((BLK, D + 64), f32),
            pltpu.VMEM((KVH, HS, R3), f32),
            *(bufs if far else []),
        ],
        specs=[VMEM] * 8 + [HBM if far else VMEM] * 8,
        limit=(16 if n == 8 else 40) if far else 8,
        us=12,
    )


def query_back_body(sc, dq, p0, p1, p2, p3, da, buf, sem):
    copies = [
        pltpu.make_async_copy(p, buf.at[m], sem.at[m]) for m, p in enumerate((p0, p1, p2, p3))
    ]
    for c in copies:
        c.start()
    for k, c in enumerate(copies):
        c.wait()
        da[sc[0] ^ k] = nt(dq[...], buf[k, :SL, 2 * KV : QKV])


def query_back(scal, dq, parts):
    return call(
        query_back_body,
        "query_back",
        1,
        [scal, dq, *parts],
        [shape((WA, BLK, SL), f32)],
        [pltpu.VMEM((WA, SL + 8, QKVP), bf16), pltpu.SemaphoreType.DMA((WA,))],
        specs=[VMEM] + [ANY] * WA,
        us=2,
    )[0]


def project_back_body(sc, own, go, back, cos_ref, sin_ref, da, x, dm, gain, gain_m, p0, p1, p2, p3, *refs):
    dkv_ref, dx_ref, dxl_ref, d4, buf, sem = refs
    copies = [
        pltpu.make_async_copy(p.at[:, pl.ds(0, 2 * KV)], buf.at[m], sem.at[m])
        for m, p in enumerate((p0, p1, p2, p3))
    ]
    for c in copies:
        c.start()
    total = own[...].astype(f32) + go[...].astype(f32) + back[...].astype(f32)
    cos, sin = cos_ref[...], sin_ref[...]
    edge = head_only((cos, sin))
    for i in range(2):
        dkv_ref[:BLK, 128 * i : 128 * (i + 1)] = rope_back(total[:, 128 * i : 128 * (i + 1)], cos, sin).astype(bf16)
    dkv_ref[:BLK, 256:384] = rope_back(total[:, 256:384], *edge).astype(bf16)
    dkv_ref[:BLK, 384:] = total[:, 384:].astype(bf16)
    for k, c in enumerate(copies):
        c.wait()
        d4[sc[0] ^ k] = da[sc[0] ^ k] + nt(dkv_ref[:BLK, :], buf[k, :SL, :])
    grads = jnp.concatenate([d4[j] for j in range(WA)], axis=1)
    part, gain_grad = norm_back(grads, x[...], gain[...])
    dkv_ref[BLK:, :] = jnp.zeros((8, 2 * KV), bf16)
    for i, g in enumerate((gain_grad, gain_m[...])):
        dkv_ref[BLK + 2 * i : BLK + 2 * i + 1, :] = g[:, : 2 * KV].astype(bf16)
        dkv_ref[BLK + 2 * i + 1 : BLK + 2 * i + 2, : D - 2 * KV] = g[:, 2 * KV :].astype(bf16)
    dx = dm[...] + part
    dx_ref[...] = dx
    dxl_ref[...] = dx.astype(bf16)


def project_back(scal, addends, tables, da, parts, x, dm, gain, gain_m_grad):
    return call(
        project_back_body,
        "project_back",
        1,
        [scal, *addends, *tables, da, x, dm, gain, gain_m_grad, *parts],
        [shape((BLK + 8, 2 * KV), bf16), shape((BLK, D), f32), shape((BLK, D), bf16)],
        [
            pltpu.VMEM((WA, BLK, SL), f32),
            pltpu.VMEM((WA, SL + 8, 2 * KV), bf16),
            pltpu.SemaphoreType.DMA((WA,)),
        ],
        us=2.5,
        specs=[VMEM] * 10 + [ANY] * WA,
    )


def grad_rows_body(has_prev, sc, *refs):
    out = refs[-1]
    slices = refs[:WA]
    lo = 0
    for kind, lows in ((0, refs[WA : 2 * WA]), (0, refs[2 * WA : 3 * WA]), (1, refs[3 * WA : 4 * WA])):
        acc = None
        for sl, low in zip(slices, lows):
            part = tn(sl[kind], low[:BLK])
            acc = part if acc is None else acc + part
        width = acc.shape[1]
        if has_prev:
            acc = acc + refs[4 * WA][:SL, lo : lo + width]
            out[:SL, lo : lo + width] = acc.astype(bf16)
        else:
            out[:SL, lo : lo + width] = acc
        lo += width
    gains = sum(low[BLK:, :].astype(f32) for low in refs[WA : 2 * WA])
    rest = D - 2 * KV
    whole = jnp.concatenate(
        [
            jnp.concatenate([gains[2 * i : 2 * i + 1], gains[2 * i + 1 : 2 * i + 2, :rest]], axis=1)
            for i in range(2)
        ],
        axis=0,
    )
    if has_prev:
        whole = whole + refs[4 * WA][SL : SL + 2, :D]
    out[SL:, :] = jnp.zeros((256 - SL, lo), out.dtype)
    out[SL : SL + 2, :D] = whole.astype(out.dtype)


def grad_rows(scal, slices, dkvs, dqs, dmls, prev):
    has_prev = prev is not None
    cols = QKV + D
    return call_fetched(
        functools.partial(grad_rows_body, has_prev),
        "grad_rows",
        scal,
        [*slices, *dkvs, *dqs, *dmls] + ([prev] if has_prev else []),
        [shape((256, cols), bf16 if has_prev else f32)],
        us=4,
        limit=12,
        far=[True] * WA + [not has_prev] * (3 * WA) + [True] * has_prev,
        far_out=not has_prev,
    )[0]


def grad_ffd_body(has_prev, sc, b0, b1, b2, b3, keep, got, z, zg, l0, l1, l2, l3, *refs):
    out, bt = refs[-2:]

    def put(piece, block, lo, part):
        rows, cols = part.shape
        if has_prev:
            part = part + refs[0][piece, block, lo : lo + rows, :cols]
        out[piece, block, lo : lo + rows, :] = part.astype(out.dtype)

    for m, b in enumerate((b0, b1, b2, b3)):
        bt[:, BLK * m : BLK * (m + 1)] = b[...].astype(f32).T.astype(bf16)
    for gu in range(2):
        for j in range(WA):
            lhs = bt[SL * j : SL * (j + 1), :]
            acc = mm(lhs[:, : 2 * BLK], keep[gu]) + mm(lhs[:, 2 * BLK :], got[gu])
            for i in range(4):
                rows = min(64, SL - 64 * i)
                put(4 * gu + i, j, 0, acc[64 * i : 64 * i + rows])
                if rows < 64:
                    out[4 * gu + i, j, rows:] = jnp.zeros((64 - rows, FFQ), out.dtype)
    acc = tn(z[:BLK], l0[...]) + tn(z[BLK:], l1[...])
    acc = acc + tn(zg[:BLK], l2[...]) + tn(zg[BLK:], l3[...])
    for p in range(8):
        d = acc[80 * p : 80 * (p + 1)]
        put(p, 4, 0, d[:64, :FFQ])
        put(p, 5, 0, d[64:, :FFQ])
        put(p, 5, 16, jnp.concatenate([d[:40, FFQ:], d[40:, FFQ:]], axis=1))
        out[p, 5, 56:] = jnp.zeros((8, FFQ), out.dtype)


def grad_ffd(scal, bs, keep, got, z, z_got, lows, prev):
    has_prev = prev is not None
    return call_fetched(
        functools.partial(grad_ffd_body, has_prev),
        "grad_ffd",
        scal,
        [*bs, keep, got, z, z_got, *lows] + ([prev] if has_prev else []),
        [shape((8, WA + 2, 64, FFQ), bf16 if has_prev else f32)],
        us=7,
        limit=24,
        scratch=[pltpu.VMEM((D, WA * BLK), bf16)],
        far=[has_prev] * 4 + [False, False] + [has_prev] * 2 + [False] * WA + [True] * has_prev,
        far_out=not has_prev,
    )[0]


def finish_ff_body(n, sc, *refs):
    gate, up, down, whole = refs[n:]
    position, w = sc[3], sc[0]
    for k in range(n):
        p = (position - k + n) % n
        first = pl.multiple_of(64 * (p % 4), 8)
        for gu, out in enumerate((gate, up)):
            for rows in (64, SL - 192):

                @pl.when((p // 4 == gu) & ((p % 4 < 3) == (rows == 64)))
                def _():
                    for m in range(WA):
                        lo = pl.multiple_of(FFQ * (w ^ m), 128)
                        out[pl.ds(first, rows), pl.ds(lo, FFQ)] = refs[k][m, :rows].astype(f32)

        at = pl.multiple_of(80 * p, 8)
        whole[pl.ds(at, 64), :FFQ] = refs[k][4].astype(f32)
        whole[pl.ds(at + 64, 16), :FFQ] = refs[k][5, :16].astype(f32)
        for i in range(2):
            part = refs[k][5, 16:56, 320 * i : 320 * (i + 1)]
            whole[pl.ds(at + 40 * i, 40), FFQ:] = part.astype(f32)
    down[...] = whole[...].T


def finish_ff(scal, gathered):
    gate, up, down = call_fetched(
        functools.partial(finish_ff_body, len(gathered)),
        "finish_ff",
        scal,
        list(gathered),
        [shape((SL, 4 * FFQ), f32), shape((SL, 4 * FFQ), f32), shape((D, FFQ), f32)],
        us=6,
        limit=32,
        far=[True] * len(gathered),
        scratch=[pltpu.VMEM((FFQ, D), f32)],
    )
    return gate, up, down.T


def finish_rows_body(n, sc, *refs):
    keys, values, query, rows_out, gains, whole = refs[n:]
    for k in range(n):
        p = (sc[3] - k + n) % n
        rows = refs[k].shape[0]
        tail = SL - rows * (n - 1)
        first = pl.multiple_of(p * rows, 8)
        whole[pl.ds(first, rows), :] = refs[k][:, : 2 * KV].astype(f32)

        @pl.when(p < n - 1)
        def _():
            query[pl.ds(first, rows), :] = refs[k][:, 2 * KV : QKV].astype(f32)
            rows_out[pl.ds(first, rows), :] = refs[k][:, QKV:].astype(f32)

        @pl.when(p == n - 1)
        def _():
            query[rows * (n - 1) :, :] = refs[k][:tail, 2 * KV : QKV].astype(f32)
            rows_out[rows * (n - 1) :, :] = refs[k][:tail, QKV:].astype(f32)
            gains[...] = refs[k][tail : tail + 8, :D].astype(f32)

    keys[...] = whole[:SL, :KV].T
    values[...] = whole[:SL, KV:].T


def finish_rows(scal, gathered):
    wide = shape((SL, D), f32)
    keys, values, query, rows_out, gains = call_fetched(
        functools.partial(finish_rows_body, len(gathered)),
        "finish_rows",
        scal,
        list(gathered),
        [shape((KV, SL), f32), shape((KV, SL), f32), wide, wide, shape((8, D), f32)],
        us=4,
        limit=20,
        far=[True] * len(gathered),
        scratch=[pltpu.VMEM((256, 2 * KV), f32)],
    )
    return keys.T, values.T, query, rows_out, gains


def body(
    tokens,
    cotangent,
    segment_ids,
    block_order,
    gain_attn,
    w_query,
    key_projection,
    value_projection,
    w_out,
    gain_mlp,
    w_gate,
    w_up,
    w_down,
):
    n = block_order.shape[1]
    w = lax.axis_index("wa")
    r = lax.axis_index("ctx")
    core = w % 2
    row = w // 2
    position = ring_position(r, n)
    x_side = r % 2
    scal = jnp.stack([w, x_side, row, position, core]).astype(i32)

    blocks = ring_device((position - jnp.arange(n, dtype=i32)) % n, n)
    labels = jnp.arange(n, dtype=i32)
    order_row = block_order[0]
    anchors = jnp.sum(jnp.where(blocks[:, None] == labels[None, :], order_row[None, :], 0), axis=1)
    natural = anchors[0] * BLK + jnp.arange(BLK, dtype=i32)
    seg_labels = jnp.arange(SEQS, dtype=i32)
    sizes = jnp.sum((segment_ids[0][None, :] == seg_labels[:, None]).astype(i32), axis=1)
    before = (seg_labels[None, :] < seg_labels[:, None]).astype(i32)
    starts = jnp.sum(before * sizes[None, :], axis=1)
    start_of = jnp.max(jnp.where(starts[None, :] <= natural[:, None], starts[None, :], 0), axis=1)
    sched = jnp.concatenate([anchors, start_of[:1]]).astype(i32)
    qinfo = jnp.pad(
        jnp.stack([jnp.tile(natural, GQ), jnp.tile(start_of, GQ)]), ((0, 6), (0, 0))
    ).astype(i32)
    frequency = rope_base ** (-jnp.arange(HS // 2, dtype=f32) * 2.0 / HS)
    angles = (natural - start_of).astype(f32)[:, None] * frequency[None, :]
    tables = (jnp.tile(jnp.cos(angles), (1, 4)), jnp.tile(jnp.sin(angles), (1, 4)))

    gains_own = jnp.pad(jnp.stack([gain_attn, gain_mlp]), ((0, 6), (0, 0)))
    qkv_own = pack_qkv(scal, w_query, key_projection, value_projection, gains_own)
    qkv_across = swap(qkv_own, 2)
    qkv_side = swap(qkv_own, 1)
    out_own, keep, give, down_own = pack_rest(scal, after(w_out, qkv_own), w_gate, w_up, w_down)
    core_part = swap(give, 1)

    def y_half(gu):
        return jnp.stack(
            [
                lax.dynamic_index_in_dim(keep[gu], x_side, 0, keepdims=False),
                lax.dynamic_index_in_dim(core_part[gu], x_side, 0, keepdims=False),
            ]
        )

    gate_half, up_half = y_half(0), y_half(1)
    down_half = lax.dynamic_slice_in_dim(down_own, x_side * (FFQ // 2), FFQ // 2, 0)
    top = cotangent[0]
    first = tokens[0]
    cos, sin = tables
    (qkv_across, qkv_side, core_part, out_own, gate_half, up_half, down_half, top, first, cos, sin,
     sched, qinfo) = bar(
        qkv_across, qkv_side, core_part, out_own, gate_half, up_half, down_half, top, first, cos, sin,
        sched, qinfo)
    tables = (cos, sin)
    qkv_parts = [qkv_own, qkv_side, qkv_across, swap(qkv_across, 1)]

    def ring_keys(kv, extras, held):
        if n != 8:
            for e in extras:
                held.update(e(held))
            return ring_gather(kv, n, position)
        rows = BLK // 2
        ahead, behind = [kv], [kv]
        for step in range(4):
            more = extras[step](held)
            if step < 3:
                f, b = ring_shift(ahead[-1], n, 1), ring_shift(behind[-1], n, -1)
            else:
                f = ring_shift(ahead[-1][:rows], n, 1)
                b = ring_shift(behind[-1][rows:], n, -1)
            f, b, *values = bar(f, b, *more.values())
            ahead.append(f)
            behind.append(b)
            held.update(zip(more.keys(), values))
        far = jnp.concatenate([ahead[4], behind[4]], axis=0)
        return jnp.stack(ahead[:4] + [far] + behind[3:0:-1])

    def spread(dkv, extras, held):
        if n != 8:
            for e in extras:
                held.update(e(held))
            total = lax.psum_scatter(
                by_distance(dkv, n, position), "ctx", scatter_dimension=0, tiled=False
            )
            return (total, jnp.zeros_like(total), jnp.zeros_like(total))
        go = back = None
        for step in range(4):
            more = extras[step](held)
            if step == 0:
                go, back = ring_far(lambda k: dkv[k], n)
            else:
                go, back = ring_near(lambda k: dkv[k], n, 4 - step, go, back)
            go, back, *values = bar(go, back, *more.values())
            held.update(zip(more.keys(), values))
        return (dkv[0], go, back)

    gate_mine = swap(gate_half, 2)
    x, a4, q3, kv, gains = project(scal, [first], tables, qkv_parts)
    gain_a, gain_m = gains[0:1], gains[1:2]
    kv, out_own = bar(kv, out_own)
    held = dict(gate_mine=gate_mine)
    out_across = swap(out_own, 2)
    up_mine = swap(after(up_half, kv), 2)

    def gate_other(h):
        return side_swap(h["gate_mine"], n)

    extras = [
        lambda h: dict(out_side=swap(out_own, 1), gate_mine=h["gate_mine"]),
        lambda h: dict(out_across=out_across),
        lambda h: dict(out_diag=swap(h["out_across"], 1)),
        lambda h: dict(gate_other=gate_other(h), up_mine=up_mine),
    ]
    every = ring_keys(kv, extras, held)
    out_parts = [out_own, held["out_side"], held["out_across"], held["out_diag"]]
    up_other = side_swap(held["up_mine"], n)
    down_mine = swap(after(down_half, every), 2)
    *sl, o_t, lse, m, b = attend(scal, sched, qinfo, q3, every, x, a4, gain_m, out_parts)
    m, b, up_other, down_mine = bar(m, b, up_other, down_mine)
    b_side = swap(b, 1)
    down_other = side_swap(down_mine, n)
    down_far = jnp.concatenate(
        [
            jnp.where(x_side == 0, down_mine, down_other),
            jnp.where(x_side == 0, down_other, down_mine),
        ],
        axis=0,
    )
    ff_parts = [
        keep,
        core_part,
        held["gate_mine"],
        held["up_mine"],
        held["gate_other"],
        up_other,
        down_own,
        down_far,
    ]
    b_far = swap(b, 2)
    z, z_give, gu, y_own, y_side = mlp(scal, b, b_side, ff_parts)
    y_own, y_side, b_far, z_give = bar(y_own, y_side, b_far, z_give)
    kept0 = [x, q3, every, o_t, lse, m, gu, z]

    x, a4, q3, kv, _ = project(scal, [m, y_own, swap(y_side, 1)], tables, qkv_parts)
    kv, z_give, b_far = bar(kv, z_give, b_far)
    b0, b0_side, sl0 = b, b_side, sl
    held = {}
    extras = [
        lambda h: dict(z_got=swap(z_give, 2), b_diag=swap(b_far, 1)),
        lambda h: dict(s1=swap(sl0[1], 1), s2=swap(sl0[2], 2)),
        lambda h: dict(s3=swap(sl0[3], 3), top_side=swap(top, 1)),
        lambda h: dict(top_far=swap(top, 2)),
    ]
    every = ring_keys(kv, extras, held)
    kept0 += [
        held["z_got"],
        [b0, b0_side, b_far, held["b_diag"]],
        [sl0[0], held["s1"], held["s2"], held["s3"]],
    ]
    top_side, top_far = held["top_side"], held["top_far"]
    *sl, o_t, lse, m, b = attend(scal, sched, qinfo, q3, every, x, a4, gain_m, out_parts)
    m, b = bar(m, b)
    b_side = swap(b, 1)
    b_far = swap(b, 2)
    z, z_give, gu, y_own, y_side = mlp(scal, b, b_side, ff_parts)
    y_own, y_side, b_far, z_give, z, top = bar(y_own, y_side, b_far, z_give, z, top)

    y_got = swap(y_side, 1)
    z_got = swap(z_give, 2)
    keep_d, give_d, db_own, db_side = mlp_back(scal, top, top_side, gu, ff_parts)
    db_own, db_side, give_d, z_got, y_got = bar(db_own, db_side, give_d, z_got, y_got)
    output = (m + y_own + y_got).astype(bf16)[None]
    db_got = swap(db_side, 1)
    got_d = swap(give_d, 2)
    b_diag = swap(b_far, 1)
    top_diag = swap(top_far, 1)
    dm, dml, gain_m_1, dq, dkv = attend_back(
        False, scal, sched, qinfo, top, db_own, db_got, m, gain_m, out_parts, q3, every, o_t, lse, tables
    )
    dkv, dq, dml, b_diag, top_diag = bar(dkv, dq, dml, b_diag, top_diag)
    lows = [top, top_side, top_far, top_diag]
    bs = [b, b_side, b_far, b_diag]
    sl1, keep_d1, z1 = sl, keep_d, z
    held = {}
    extras = [
        lambda h: dict(got_d=got_d),
        lambda h: dict(
            s1=swap(sl1[1], 1), s2=swap(sl1[2], 2), da=query_back(scal, dq, qkv_parts)
        ),
        lambda h: dict(
            s3=swap(sl1[3], 3),
            dq_far=swap(dq, 2),
            ff_1=grad_ffd(scal, bs, keep_d1, h["got_d"], z1, z_got, lows, None),
        ),
        lambda h: dict(dq_side=swap(dq, 1), dml_side=swap(dml, 1), dml_far=swap(dml, 2)),
    ]
    addends = spread(dkv, extras, held)
    ff_1 = held["ff_1"]
    dq_diag, dml_diag = swap(held["dq_far"], 1), swap(held["dml_far"], 1)
    dkv0, dx, low = project_back(
        scal, addends, tables, held["da"], qkv_parts, x, dm, gain_a, gain_m_1
    )
    dx, low, dkv0, dq_diag, dml_diag = bar(dx, low, dkv0, dq_diag, dml_diag)
    slices_1 = [sl[0], held["s1"], held["s2"], held["s3"]]
    dqs_1 = [dq, held["dq_side"], held["dq_far"], dq_diag]
    dmls_1 = [dml, held["dml_side"], held["dml_far"], dml_diag]

    x, q3, every, o_t, lse, m, gu, z, z_got, bs0, slices = kept0
    low_side = swap(low, 1)
    low_far = swap(low, 2)
    keep_d, give_d, db_own, db_side = mlp_back(scal, low, low_side, gu, ff_parts)
    db_own, db_side, give_d, low_far = bar(db_own, db_side, give_d, low_far)
    db_got = swap(db_side, 1)
    got_d = swap(give_d, 2)
    low_diag = swap(low_far, 1)
    dkv_side, dkv_far = swap(dkv0, 1), swap(dkv0, 2)
    dm, dml, gain_m_0, dq, dkv = attend_back(
        True, scal, sched, qinfo, dx, db_own, db_got, m, gain_m, out_parts, q3, every, o_t, lse, tables
    )
    dkv, dq, dml, got_d, dkv_side, dkv_far, low_diag = bar(
        dkv, dq, dml, got_d, dkv_side, dkv_far, low_diag
    )
    dkvs_1 = [dkv0, dkv_side, dkv_far]
    lows_0 = [low, low_side, low_far, low_diag]

    def ff_piece_of(ff):
        sub = n // 8
        pieces = ff.reshape(8, WA + 2, sub, 64 // sub, FFQ).transpose(0, 2, 1, 3, 4)
        return pieces.reshape(n, WA + 2, 64 // sub, FFQ)

    keep_d0, dq0, dml0 = keep_d, dq, dml
    held = {}

    def ff_ring(h, k):
        if n != 8:
            return {}
        if k == 4:
            h["ff_piece"] = at_position(ff_piece_of(h["ff"]), n, position)
            go, back = ring_far(h["ff_piece"], n)
        else:
            go, back = ring_near(h["ff_piece"], n, k, h["ff_go"], h["ff_back"])
        return dict(ff_go=go, ff_back=back)

    extras = [
        lambda h: dict(dq_far=swap(dq0, 2), ff=grad_ffd(scal, bs0, keep_d0, got_d, z, z_got, lows_0, ff_1)),
        lambda h: dict(dml_far=swap(dml0, 2), **ff_ring(h, 4)),
        lambda h: dict(da=query_back(scal, dq0, qkv_parts), dkv_diag=swap(dkv_far, 1)),
        lambda h: dict(dq_side=swap(dq0, 1), dml_side=swap(dml0, 1), **ff_ring(h, 3)),
    ]
    addends = spread(dkv, extras, held)
    dkv0, dx, low = project_back(
        scal, addends, tables, held["da"], qkv_parts, x, dm, gain_a, gain_m_0
    )
    rows_0 = [held["dq_far"], held["dml_far"]]

    if n == 8:
        ff_piece = held["ff_piece"]
        ff_go, ff_back = ring_near(ff_piece, n, 2, held["ff_go"], held["ff_back"])
        dkv_sent = dkv0
        dkv_side, dkv_far_0 = swap(dkv0, 1), swap(dkv0, 2)
        dq_diag, dml_diag = swap(rows_0[0], 1), swap(rows_0[1], 1)
        rows_1 = grad_rows(scal, slices_1, dkvs_1 + [held["dkv_diag"]], dqs_1, dmls_1, None)
        dkv_side, dkv_far_0, dq_diag, dml_diag, rows_1, ff_go, ff_back, low = bar(
            dkv_side, dkv_far_0, dq_diag, dml_diag, rows_1, ff_go, ff_back, low
        )
        ff_go, ff_back = ring_near(ff_piece, n, 1, ff_go, ff_back)
        dkvs = [dkv_sent, dkv_side, dkv_far_0, swap(dkv_far_0, 1)]
        dqs = [dq, held["dq_side"], rows_0[0], dq_diag]
        dmls = [dml, held["dml_side"], rows_0[1], dml_diag]
        rows_grad = grad_rows(scal, slices, dkvs, dqs, dmls, rows_1)
        rows_grad, ff_go, ff_back = bar(rows_grad, ff_go, ff_back)
        piece = at_position(rows_grad.reshape(n, 256 // n, QKV + D), n, position)
        go, back = ring_far(piece, n)
        ff_mine = total_low(ff_piece(0), ff_go, ff_back)
        home = rows_home(ff_mine[:WA], w)
        go, back, home, down_mine = bar(go, back, home, ff_mine[WA:])
        ff_ahead = [jnp.concatenate([home, down_mine], axis=0)]
        ff_behind = list(ff_ahead)
        for k in (3, 2, 1):
            go, back = ring_near(piece, n, k, go, back)
            f, g = ring_shift(ff_ahead[-1], n, 1), ring_shift(ff_behind[-1], n, -1)
            go, back, f, g = bar(go, back, f, g)
            ff_ahead.append(f)
            ff_behind.append(g)
        mine = total_low(piece(0), go, back)
        f, g = ring_shift(ff_ahead[-1][:3], n, 1), ring_shift(ff_behind[-1][3:], n, -1)
        ahead, behind = [mine], [mine]
        a, c = ring_shift(mine, n, 1), ring_shift(mine, n, -1)
        a, c, f, g = bar(a, c, f, g)
        ahead.append(a)
        behind.append(c)
        ff_far = jnp.concatenate([f, g], axis=0)
        ff_all = ff_ahead + [ff_far] + ff_behind[:0:-1]
        gate_total, up_total, down_total = finish_ff(scal, ff_all)
        for _ in range(2):
            a, c = ring_shift(ahead[-1], n, 1), ring_shift(behind[-1], n, -1)
            a, c, gate_total, up_total, down_total = bar(a, c, gate_total, up_total, down_total)
            ahead.append(a)
            behind.append(c)
        half = mine.shape[0] // 2
        far = jnp.concatenate(
            [ring_shift(ahead[-1][:half], n, 1), ring_shift(behind[-1][half:], n, -1)], axis=0
        )
        rows_all = ahead + [far] + behind[:0:-1]
        key_total, value_total, query_total, out_total, gain_rows = finish_rows(scal, rows_all)
    else:
        ff_mine = lax.psum_scatter(
            ff_piece_of(held["ff"]), "ctx", scatter_dimension=0, tiled=False
        )
        ff_home = jnp.concatenate([rows_home(ff_mine[:WA], w), ff_mine[WA:]], axis=0)
        ff_all = ring_gather(ff_home, n, position)
        rows_1 = grad_rows(scal, slices_1, dkvs_1 + [held["dkv_diag"]], dqs_1, dmls_1, None)
        dqs = [dq, held["dq_side"], held["dq_far"], swap(held["dq_far"], 1)]
        dmls = [dml, held["dml_side"], held["dml_far"], swap(held["dml_far"], 1)]
        rows_grad = grad_rows(scal, slices, everyone(dkv0), dqs, dmls, rows_1)
        rows_all = ring_sum(rows_grad.reshape(n, 256 // n, QKV + D), n, position)
        sub = n // 8
        whole = placed(ff_all, n, position).reshape(8, sub, WA + 2, 64 // sub, FFQ)
        whole = whole.transpose(0, 2, 1, 3, 4).reshape(8, WA + 2, 64, FFQ)
        down = whole[:, WA:].reshape(8, 128, FFQ)
        right = down[:, 80:120].reshape(8, 40, 2, FFQ // 2).transpose(0, 2, 1, 3)
        down = jnp.concatenate([down[:, :80], right.reshape(8, 80, FFQ // 2)], axis=2)
        down_total = down.reshape(FFQ, D).astype(f32)
        whole = whole[:, :WA].reshape(2, 4, WA, 64, FFQ).transpose(0, 2, 1, 3, 4)
        whole = whole.reshape(2, WA, 256, FFQ)[:, :, :SL]
        whole = jnp.take(whole, w ^ jnp.arange(WA, dtype=i32), axis=1).transpose(0, 2, 1, 3)
        gate_total, up_total = whole.reshape(2, SL, -1).astype(f32)
        rows_total = placed(rows_all, n, position).reshape(256, QKV + D).astype(f32)
        gain_rows = rows_total[SL:, :D]
        rows_total = rows_total[:SL]
        key_total, value_total, query_total, out_total = (
            rows_total[:, :KV],
            rows_total[:, KV : 2 * KV],
            rows_total[:, 2 * KV : QKV],
            rows_total[:, QKV:],
        )
    input_grad = low[None]
    gain_rows = lax.dynamic_slice_in_dim(gain_rows[:2], w * SL, SL, 1)
    return (
        output,
        input_grad,
        gain_rows[0],
        query_total,
        key_total,
        value_total,
        out_total,
        gain_rows[1],
        gate_total,
        up_total,
        down_total,
    )


def solution(mesh):
    rows = P("wa", None)
    flat = P("wa")
    act = P("wa", "ctx", None)
    return jax.shard_map(
        body,
        mesh=mesh,
        in_specs=(act, act, rows, rows, flat, rows, rows, rows, rows, flat, rows, rows, rows),
        out_specs=(act, act, flat, rows, rows, rows, rows, flat, rows, rows, rows),
        check_vma=False,
    )
```

```python
import functools

import jax
import jax.numpy as jnp
from jax import lax
from jax.experimental import pallas as pl
from jax.experimental.pallas import tpu as pltpu
from jax.sharding import PartitionSpec as P

QH = 15
KVH = 5
GQ = QH // KVH
HS = 64
SEQS = 8
REPEATS = 2
WA = 4
BLK = 128
D = 960
SL = D // WA
KV = KVH * HS
QKV = 2 * KV + D
FFQ = 640
R3 = GQ * BLK
QKVP = 1664

epsilon = 1e-05
masked_score = -1e30
rope_base = 10000.0
bf16 = jnp.bfloat16
f32 = jnp.float32
i32 = jnp.int32
MB = 1 << 20


def swap(x, mask):
    return lax.ppermute(x, "wa", [(i, i ^ mask) for i in range(WA)])


def side_swap(x, n):
    return lax.ppermute(x, "ctx", [(i, i ^ 1) for i in range(n)])


def ring_order(n):
    return [i for i in range(0, n, 2)] + [i for i in range(n - 1, 0, -2)]


def ring_shift(x, n, step):
    order = ring_order(n)
    return lax.ppermute(x, "ctx", [(order[i], order[(i + step) % n]) for i in range(n)])


def ring_position(r, n):
    return jnp.where(r % 2 == 0, r // 2, n - 1 - r // 2) if n == 8 else r


def ring_device(p, n):
    return jnp.where(p < n // 2, 2 * p, 2 * (n - 1 - p) + 1) if n == 8 else p


def after(x, *others):
    return lax.optimization_barrier((x,) + others)[0]


def bar(*xs):
    return lax.optimization_barrier(xs)


def by_distance(x, n, position):
    return jnp.take(x, (position - jnp.arange(n, dtype=i32)) % n, axis=0)


def ring_gather(x, n, position):
    if n != 8:
        return by_distance(lax.all_gather(x, "ctx"), n, position)
    half = n // 2
    rows = x.shape[0] // 2
    ahead = [x]
    behind = [x]
    for _ in range(half - 1):
        ahead.append(ring_shift(ahead[-1], n, 1))
        behind.append(ring_shift(behind[-1], n, -1))
    far = jnp.concatenate(
        [ring_shift(ahead[-1][:rows], n, 1), ring_shift(behind[-1][rows:], n, -1)], axis=0
    )
    return ahead + [far] + behind[:0:-1]


def add_low(x, y):
    return (x.astype(f32) + y.astype(f32)).astype(bf16)


def ring_far(piece, n):
    far = piece(n // 2)
    rows = far.shape[0] // 2
    return ring_shift(far[:rows], n, 1), ring_shift(far[rows:], n, -1)


def ring_near(piece, n, k, go, back):
    ahead, behind = piece(n - k), piece(k)
    if go.shape != ahead.shape:
        rows = go.shape[0]
        go = jnp.concatenate([add_low(ahead[:rows], go), ahead[rows:]], axis=0)
        back = jnp.concatenate([behind[:rows], add_low(behind[rows:], back)], axis=0)
    else:
        go, back = add_low(ahead, go), add_low(behind, back)
    return ring_shift(go, n, 1), ring_shift(back, n, -1)


def ring_scatter(piece, n):
    go, back = ring_far(piece, n)
    for k in range(n // 2 - 1, 0, -1):
        go, back = ring_near(piece, n, k, go, back)
    return piece(0), go, back


def total_low(own, go, back):
    return (own.astype(f32) + go.astype(f32) + back.astype(f32)).astype(bf16)


def at_position(pieces, n, position):
    return lambda k: lax.dynamic_index_in_dim(pieces, (position - k) % n, 0, keepdims=False)


def ring_sum(pieces, n, position):
    if n != 8:
        mine = lax.psum_scatter(pieces, "ctx", scatter_dimension=0, tiled=False)
    else:
        mine = total_low(*ring_scatter(at_position(pieces, n, position), n))
    return ring_gather(mine, n, position)


def rows_home(mine, w):
    out = []
    for mask in range(WA):
        block = lax.dynamic_index_in_dim(mine, w ^ mask, 0, keepdims=False)
        out.append(swap(block, mask) if mask else block)
    return jnp.stack(out)


def placed(gathered, n, position):
    if n != 8:
        return by_distance(gathered, n, position)
    out = jnp.zeros((n,) + gathered[0].shape, bf16)
    for k in range(n):
        out = lax.dynamic_update_index_in_dim(out, gathered[k], (position - k) % n, 0)
    return out


def everyone(x):
    side = swap(x, 1)
    across = swap(x, 2)
    return [x, side, across, swap(across, 1)]


VMEM = pl.BlockSpec(memory_space=pltpu.VMEM)
SMEM = pl.BlockSpec(memory_space=pltpu.SMEM)


ANY = pl.BlockSpec(memory_space=pl.ANY)
HBM = pl.BlockSpec(memory_space=pltpu.HBM)


def call(body, name, n_scalar, ins, outs, scratch=(), us=2.0, limit=10, specs=None, out_specs=None):
    specs = specs or [VMEM] * (len(ins) - n_scalar)
    ins = list(ins[:n_scalar]) + [
        pltpu.with_memory_space_constraint(x, pltpu.HBM) if spec is HBM else x
        for x, spec in zip(ins[n_scalar:], specs)
    ]
    return pl.pallas_call(
        body,
        name=name,
        in_specs=[SMEM] * n_scalar + specs,
        out_specs=out_specs or [VMEM] * len(outs),
        out_shape=list(outs),
        scratch_shapes=list(scratch),
        cost_estimate=pl.CostEstimate(flops=int(us * 1.15e9), transcendentals=0, bytes_accessed=1 << 16),
        compiler_params=pltpu.CompilerParams(vmem_limit_bytes=limit * MB),
    )(*ins)


def fetched(refs, bufs, sem):
    copies = [pltpu.make_async_copy(r, b, sem.at[i]) for i, (r, b) in enumerate(zip(refs, bufs))]
    for c in copies:
        c.start()
    for c in copies:
        c.wait()


def call_fetched(body, name, scal, ins, outs, us, limit, scratch=(), far=None, far_out=False):
    count, n_out = len(ins), len(outs)
    far = far or [False] * count

    def whole(sc, *refs):
        sources, results = refs[:count], refs[count : count + n_out]
        bufs = refs[count + n_out : 2 * count + n_out]
        sem, rest = refs[2 * count + n_out], refs[2 * count + n_out + 1 :]
        fetched(sources, bufs, sem)
        if not far_out:
            body(sc, *bufs, *results, *rest)
            return
        body(sc, *bufs, *rest)
        fetched(rest[:n_out], results, sem)

    bufs = [pltpu.VMEM(x.shape, x.dtype) for x in ins]
    held = [pltpu.VMEM(x.shape, x.dtype) for x in outs] if far_out else []
    return call(
        whole,
        name,
        1,
        [scal, *ins],
        outs,
        bufs + [pltpu.SemaphoreType.DMA((max(count, n_out),)), *held, *scratch],
        us=us,
        limit=limit,
        specs=[HBM if f else ANY for f in far],
        out_specs=[ANY] * n_out if far_out else None,
    )


def shape(dims, dtype):
    return jax.ShapeDtypeStruct(dims, dtype)


def mm(a, b):
    return jnp.dot(a, b, preferred_element_type=f32)


def nt(a, b):
    return lax.dot_general(a, b, (((1,), (1,)), ((), ())), preferred_element_type=f32)


def tn(a, b):
    return lax.dot_general(a, b, (((0,), (0,)), ((), ())), preferred_element_type=f32)


def turn(u):
    lane = lax.broadcasted_iota(i32, u.shape, 1) % HS
    return jnp.where(lane < HS // 2, -pltpu.roll(u, 128 - HS // 2, 1), pltpu.roll(u, HS // 2, 1))


def turn_back(u):
    lane = lax.broadcasted_iota(i32, u.shape, 1) % HS
    return jnp.where(lane < HS // 2, pltpu.roll(u, 128 - HS // 2, 1), -pltpu.roll(u, HS // 2, 1))


def rope(u, cos, sin):
    return u * cos + turn(u) * sin


def rope_back(u, cos, sin):
    return u * cos + turn_back(u * sin)


def pack_qkv_body(sc, wq, wk, wv, gains, out):
    out[:SL, :KV] = wk[...].T.astype(bf16)
    out[:SL, KV : 2 * KV] = wv[...].T.astype(bf16)
    out[:SL, 2 * KV : QKV] = wq[...].astype(bf16)
    out[:SL, QKV:] = jnp.zeros((SL, QKVP - QKV), bf16)
    out[SL:, :] = jnp.zeros((8, QKVP), bf16)
    out[SL:, :SL] = gains[...].astype(bf16)


def pack_qkv(scal, wq, wk, wv, gains):
    ins = [wq, wk.T, wv.T, gains]
    outs = [shape((SL + 8, QKVP), bf16)]
    return call_fetched(pack_qkv_body, "pack_qkv", scal, ins, outs, us=3, limit=8, far=[True] * 3 + [False])[0]


def pack_rest_body(sc, w_out, w_gate, w_up, w_down, out_ref, keep, give, down):
    core = sc[4]
    out_ref[...] = w_out[...].astype(bf16)
    down[...] = w_down[...].T.astype(bf16)
    for gu, src in enumerate((w_gate, w_up)):
        for t in range(2):
            lo = pl.multiple_of(FFQ * (2 * t + core), 128)
            keep[gu, t] = src[:, pl.ds(lo, FFQ)].astype(bf16)
            lo = pl.multiple_of(FFQ * (2 * t + 1 - core), 128)
            give[gu, t] = src[:, pl.ds(lo, FFQ)].astype(bf16)


def pack_rest(scal, w_out, w_gate, w_up, w_down):
    quarters = shape((2, 2, SL, FFQ), bf16)
    outs = [shape((SL, D), bf16), quarters, quarters, shape((FFQ, D), bf16)]
    ins = [w_out, w_gate, w_up, w_down.T]
    return call_fetched(pack_rest_body, "pack_rest", scal, ins, outs, us=6, limit=24, far=[True] * 4)


def head_only(tables):
    cos, sin = tables
    lane = lax.broadcasted_iota(i32, cos.shape, 1)
    return jnp.where(lane < HS, cos, 1.0), jnp.where(lane < HS, sin, 0.0)


def project_body(n_in, sc, *refs):
    xs = refs[:n_in]
    cos_ref, sin_ref, *parts = refs[n_in : n_in + 6]
    x_ref, a4, q3, kv, gains, acc_ref, x4, g4, buf, sem = refs[n_in + 6 :]
    copies = [pltpu.make_async_copy(p, buf.at[m], sem.at[m]) for m, p in enumerate(parts)]
    for c in copies:
        c.start()
    x = xs[0][...].astype(f32)
    for r in xs[1:]:
        x = x + r[...]
    x_ref[...] = x
    ratio = lax.rsqrt(jnp.mean(x * x, axis=1, keepdims=True) + epsilon)
    x = x * ratio
    for j in range(WA):
        x4[j] = x[:, SL * j : SL * (j + 1)]
    acc = None
    for m in range(WA):
        copies[m].wait()
        j = sc[0] ^ m
        gain = buf[m, SL:, :SL].astype(f32)
        g4[j] = gain
        a = (x4[j] * gain[:1]).astype(bf16)
        a4[j] = a
        part = mm(a, buf[m, :SL, :])
        acc = part if acc is None else acc + part
    gains[...] = jnp.concatenate([g4[j] for j in range(WA)], axis=1)
    acc_ref[...] = acc
    cos, sin = cos_ref[...], sin_ref[...]
    edge = head_only((cos, sin))
    for i in range(2):
        kv[:, 128 * i : 128 * (i + 1)] = rope(acc_ref[:, 128 * i : 128 * (i + 1)], cos, sin).astype(bf16)
    kv[:, 256:384] = rope(acc_ref[:, 256:384], *edge).astype(bf16)
    kv[:, 384:640] = acc_ref[:, 384:640].astype(bf16)
    for i in range(8):
        lo = 2 * KV + 128 * i
        u = rope(acc_ref[:, lo : lo + 128], cos, sin).astype(bf16) * bf16(0.125)
        for j in range(2):
            h = 2 * i + j
            if h < QH:
                q3[h // GQ, BLK * (h % GQ) : BLK * (h % GQ + 1), :] = u[:, HS * j : HS * (j + 1)]


def project(scal, xs, tables, parts):
    return call(
        functools.partial(project_body, len(xs)),
        "project",
        1,
        [scal, *xs, *tables, *parts],
        [
            shape((BLK, D), f32),
            shape((WA, BLK, SL), bf16),
            shape((KVH, R3, HS), bf16),
            shape((BLK, 2 * KV), bf16),
            shape((8, D), f32),
        ],
        [
            pltpu.VMEM((BLK, QKVP), f32),
            pltpu.VMEM((WA, BLK, SL), f32),
            pltpu.VMEM((WA, 8, SL), f32),
            pltpu.VMEM((WA, SL + 8, QKVP), bf16),
            pltpu.SemaphoreType.DMA((WA,)),
        ],
        us=3,
        limit=10,
        specs=[VMEM] * (len(xs) + 2) + [ANY] * WA,
    )


def list_blocks(sched, lst, n):
    def step(k, count):
        first = sched[k] * BLK
        seen = (sched[k] <= sched[0]) & (first + BLK > sched[n])

        @pl.when(seen)
        def _():
            lst[count] = k

        return count + seen.astype(i32)

    return lax.fori_loop(0, n, step, jnp.int32(0))


def block_bias(sched, qinfo, k):
    key = sched[k] * BLK + lax.broadcasted_iota(i32, (BLK, R3), 0)
    ok = (key <= qinfo[0:1, :]) & (key >= qinfo[1:2, :])
    return jnp.where(ok, 0.0, masked_score).astype(f32)


def attend_body(n, sc, sched, qinfo, q3, kv, x, a4, gain, p0, p1, p2, p3, *refs):
    sl = refs[:WA]
    o_t, lse, m_ref, b_ref, lst, o_scr, ol4 = refs[WA:]
    count = list_blocks(sched, lst, n)
    o_t[...] = jnp.zeros(o_t.shape, f32)

    def step(i, state):
        k = lst[i]
        bias = block_bias(sched, qinfo, k)
        out = []
        for h in range(KVH):
            top, total = state[h]
            s = nt(kv[k, :, HS * h : HS * (h + 1)], q3[h]) + bias
            new = jnp.maximum(top, jnp.max(s, axis=0, keepdims=True))
            p = jnp.exp(s - new)
            fix = jnp.exp(top - new)
            values = kv[k, :, KV + HS * h : KV + HS * (h + 1)]
            o_t[h] = o_t[h] * fix + tn(values, p.astype(bf16))
            out.append((new, total * fix + jnp.sum(p, axis=0, keepdims=True)))
        return tuple(out)

    start = tuple(
        (jnp.full((1, R3), masked_score, f32), jnp.zeros((1, R3), f32)) for _ in range(KVH)
    )
    state = lax.fori_loop(0, count, step, start)
    for h in range(KVH):
        top, total = state[h]
        out = o_t[h] * (1.0 / total)
        o_t[h] = out
        lse[h : h + 1, :] = top + jnp.log(total)
        rows = out.T
        for g in range(GQ):
            j = GQ * h + g
            o_scr[:, HS * j : HS * (j + 1)] = rows[BLK * g : BLK * (g + 1), :]
    low = o_scr[...].astype(bf16)
    for j in range(WA):
        ol4[j] = low[:, SL * j : SL * (j + 1)]
    m = x[...]
    for k, p in enumerate((p0, p1, p2, p3)):
        j = sc[0] ^ k
        sl[k][0] = a4[j]
        sl[k][1] = ol4[j]
        m = m + mm(ol4[j], p[...])
    m_ref[...] = m
    ratio = lax.rsqrt(jnp.mean(m * m, axis=1, keepdims=True) + epsilon)
    b = (m * ratio * gain[...]).astype(bf16)
    b_ref[...] = b


def attend(scal, sched, qinfo, q3, kv, x, a4, gain, parts):
    n = kv.shape[0]
    return call(
        functools.partial(attend_body, n),
        "attend",
        2,
        [scal, sched, qinfo, q3, kv, x, a4, gain, *parts],
        [
            *[shape((2, BLK, SL), bf16)] * WA,
            shape((KVH, HS, R3), f32),
            shape((8, R3), f32),
            shape((BLK, D), f32),
            shape((BLK, D), bf16),
        ],
        [
            pltpu.SMEM((n,), i32),
            pltpu.VMEM((BLK, D), f32),
            pltpu.VMEM((WA, BLK, SL), bf16),
        ],
        limit=8,
        us=10,
    )


def mlp_body(sc, b_own, b_side, keep, core, gm, um, go, uo, d_own, d_far, *refs):
    z_hbm, z_give, gu_hbm, y_own, y_side, bs, z_ref, gu_ref, sem = refs
    copies = []
    w = sc[0]
    for half, b in enumerate((b_own, b_side)):
        for j in range(WA):
            bs[j, BLK * half : BLK * (half + 1), :] = b[:, SL * j : SL * (j + 1)]
    for t, fars in ((sc[1], (gm, um)), (1 - sc[1], (go, uo))):
        lin = []
        for gu in range(2):
            acc = mm(bs[w], keep[gu, t]) + mm(bs[w ^ 1], core[gu, t])
            acc = acc + mm(bs[w ^ 2], fars[gu][0]) + mm(bs[w ^ 3], fars[gu][1])
            gu_ref[gu, t] = acc
            lin.append(acc)
        for gu in range(2):
            c = pltpu.make_async_copy(gu_ref.at[gu, t], gu_hbm.at[gu, t], sem.at[len(copies)])
            c.start()
            copies.append(c)
        gate, up = lin
        z_ref[t] = (gate / (1.0 + jnp.exp(-gate)) * up).astype(bf16)
    row = sc[2]
    copies.append(pltpu.make_async_copy(z_ref.at[row], z_hbm, sem.at[4]))
    copies[4].start()
    out = mm(z_ref[row], d_own[...]) + mm(z_ref[1 - row], d_far[...])
    y_own[...] = out[:BLK]
    y_side[...] = out[BLK:]
    z_give[...] = z_ref[1 - row]
    for c in copies:
        c.wait()


def mlp(scal, b_own, b_side, wts):
    return call(
        mlp_body,
        "mlp",
        1,
        [scal, b_own, b_side, *wts],
        [
            shape((2 * BLK, FFQ), bf16),
            shape((2 * BLK, FFQ), bf16),
            shape((2, 2, 2 * BLK, FFQ), f32),
            shape((BLK, D), f32),
            shape((BLK, D), f32),
        ],
        [
            pltpu.VMEM((WA, 2 * BLK, SL), bf16),
            pltpu.VMEM((2, 2 * BLK, FFQ), bf16),
            pltpu.VMEM((2, 2, 2 * BLK, FFQ), f32),
            pltpu.SemaphoreType.DMA((5,)),
        ],
        out_specs=[ANY, VMEM, ANY, VMEM, VMEM],
        limit=12,
        us=5.5,
    )


def mlp_back_body(sc, l_own, l_side, gu_hbm, keep, core, gm, um, go, uo, d_own, d_far, *refs):
    keep_ref, give_ref, db_own, db_side, low, acc, gu_ref, sem = refs
    copies = [
        [pltpu.make_async_copy(gu_hbm.at[gu, t], gu_ref.at[gu, t], sem.at[2 * i + gu]) for gu in range(2)]
        for i, t in enumerate((sc[1], 1 - sc[1]))
    ]
    for c in copies[0] + copies[1]:
        c.start()
    w, row = sc[0], sc[2]
    low[:BLK] = l_own[...]
    low[BLK:] = l_side[...]
    for first, (t, fg, fu) in enumerate(((sc[1], gm, um), (1 - sc[1], go, uo))):
        dz = jnp.where(t == row, nt(low[...], d_own[...]), nt(low[...], d_far[...]))
        for c in copies[first]:
            c.wait()
        gate, up = gu_ref[0, t], gu_ref[1, t]
        sig = 1.0 / (1.0 + jnp.exp(-gate))
        dg = (dz * up * sig * (1.0 + gate * (1.0 - sig))).astype(bf16)
        du = (dz * gate * sig).astype(bf16)

        @pl.when(t == row)
        def _():
            keep_ref[0] = dg
            keep_ref[1] = du

        @pl.when(t != row)
        def _():
            give_ref[0] = dg
            give_ref[1] = du

        for j, p in ((w, keep.at[0, t]), (w ^ 1, core.at[0, t]), (w ^ 2, fg.at[0]), (w ^ 3, fg.at[1])):
            part = nt(dg, p[...])
            acc[j] = part if first == 0 else acc[j] + part
        for j, p in ((w, keep.at[1, t]), (w ^ 1, core.at[1, t]), (w ^ 2, fu.at[0]), (w ^ 3, fu.at[1])):
            acc[j] = acc[j] + nt(du, p[...])
    for j in range(WA):
        db_own[:, SL * j : SL * (j + 1)] = acc[j, :BLK, :]
        db_side[:, SL * j : SL * (j + 1)] = acc[j, BLK:, :]


def mlp_back(scal, l_own, l_side, gu, wts):
    return call(
        mlp_back_body,
        "mlp_back",
        1,
        [scal, l_own, l_side, gu, *wts],
        [
            shape((2, 2 * BLK, FFQ), bf16),
            shape((2, 2 * BLK, FFQ), bf16),
            shape((BLK, D), f32),
            shape((BLK, D), f32),
        ],
        [
            pltpu.VMEM((2 * BLK, D), bf16),
            pltpu.VMEM((WA, 2 * BLK, SL), f32),
            pltpu.VMEM((2, 2, 2 * BLK, FFQ), f32),
            pltpu.SemaphoreType.DMA((4,)),
        ],
        specs=[VMEM, VMEM, ANY] + [VMEM] * 8,
        limit=12,
        us=6.7,
    )


def norm_back(grads, hidden, gain):
    ratio = lax.rsqrt(jnp.mean(hidden * hidden, axis=1, keepdims=True) + epsilon)
    scaled = hidden * ratio
    gain_grad = jnp.sum(grads * scaled, axis=0, keepdims=True)
    inner = grads * gain
    out = ratio * (inner - scaled * jnp.mean(inner * scaled, axis=1, keepdims=True))
    return out, gain_grad


def attend_back_body(n, far, sc, sched, qinfo, dy, db_own, db_got, gain, lse, cos_ref, sin_ref, *refs):
    (m, *parts, q3, kv, o_t), refs = refs[:8], refs[8:]
    dm_ref, dml_ref, gg, dq_ref, dkv_ref, lst, do3, d_scr, dq_scr, dq_t = refs[:10]
    waits = []
    if far:
        bufs, sem = refs[10:18], refs[18]
        copies = [
            pltpu.make_async_copy(a, b, sem.at[i])
            for i, (a, b) in enumerate(zip((m, *parts, q3, kv, o_t), bufs))
        ]
        for c in copies:
            c.start()
        m, *parts, q3, kv, o_t = bufs
        copies[0].wait()
        waits = copies[1:]
    count = list_blocks(sched, lst, n)
    part, gain_grad = norm_back(db_own[...] + db_got[...], m[...], gain[...])
    gg[...] = gain_grad
    dm = dy[...].astype(f32) + part
    dm_ref[...] = dm
    dml = dm.astype(bf16)
    dml_ref[...] = dml
    for c in waits:
        c.wait()
    for k, p in enumerate(parts):
        d_scr[sc[0] ^ k] = nt(dml, p[...]).astype(bf16).astype(f32)
    whole = jnp.concatenate([d_scr[j] for j in range(WA)], axis=1)
    for j in range(QH):
        do3[j // GQ, BLK * (j % GQ) : BLK * (j % GQ + 1), :] = whole[:, HS * j : HS * (j + 1)].astype(bf16)

    @pl.loop(1, n)
    def _(k):
        seen = (sched[k] <= sched[0]) & (sched[k] * BLK + BLK > sched[n])

        @pl.when(jnp.logical_not(seen))
        def _():
            dkv_ref[k] = jnp.zeros((BLK, 2 * KV), bf16)

    deltas = [
        jnp.sum(do3[h].astype(f32).T * o_t[h], axis=0, keepdims=True) for h in range(KVH)
    ]
    dq_t[...] = jnp.zeros(dq_t.shape, f32)

    @pl.loop(0, count)
    def _(i):
        k = lst[i]
        bias = block_bias(sched, qinfo, k)
        for h in range(KVH):
            keys = kv[k, :, HS * h : HS * (h + 1)]
            values = kv[k, :, KV + HS * h : KV + HS * (h + 1)]
            s = nt(keys, q3[h]) + bias
            p = jnp.exp(s - lse[h : h + 1, :])
            ds = (p * (nt(values, do3[h]) - deltas[h])).astype(bf16)
            dkv_ref[k, :, HS * h : HS * (h + 1)] = mm(ds, q3[h]).astype(bf16)
            dkv_ref[k, :, KV + HS * h : KV + HS * (h + 1)] = mm(p.astype(bf16), do3[h]).astype(bf16)
            dq_t[h] = dq_t[h] + tn(keys, ds)

    for h in range(KVH):
        rows = (dq_t[h] * 0.125).T
        for g in range(GQ):
            j = GQ * h + g
            dq_scr[:, HS * j : HS * (j + 1)] = rows[BLK * g : BLK * (g + 1), :]
    cos, sin = cos_ref[...], sin_ref[...]
    for i in range(8):
        u = rope_back(dq_scr[:, 128 * i : 128 * (i + 1)], cos, sin).astype(bf16)
        if i < 7:
            dq_ref[:, 128 * i : 128 * (i + 1)] = u
        else:
            dq_ref[:, 128 * i :] = u[:, :HS]


def attend_back(far, scal, sched, qinfo, dy, db_own, db_got, m, gain, parts, q3, kv, o_t, lse, tables):
    n = kv.shape[0]
    kept = [m, *parts, q3, kv, o_t]
    bufs = [pltpu.VMEM(x.shape, x.dtype) for x in kept] + [pltpu.SemaphoreType.DMA((8,))]
    return call(
        functools.partial(attend_back_body, n, far),
        "attend_back",
        2,
        [scal, sched, qinfo, dy, db_own, db_got, gain, lse, *tables, *kept],
        [
            shape((BLK, D), f32),
            shape((BLK, D), bf16),
            shape((1, D), f32),
            shape((BLK, D), bf16),
            shape((n, BLK, 2 * KV), bf16),
        ],
        [
            pltpu.SMEM((n,), i32),
            pltpu.VMEM((KVH, R3, HS), bf16),
            pltpu.VMEM((WA, BLK, SL), f32),
            pltpu.VMEM((BLK, D + 64), f32),
            pltpu.VMEM((KVH, HS, R3), f32),
            *(bufs if far else []),
        ],
        specs=[VMEM] * 8 + [HBM if far else VMEM] * 8,
        limit=(16 if n == 8 else 40) if far else 8,
        us=12,
    )


def query_back_body(sc, dq, p0, p1, p2, p3, da, buf, sem):
    copies = [
        pltpu.make_async_copy(p, buf.at[m], sem.at[m]) for m, p in enumerate((p0, p1, p2, p3))
    ]
    for c in copies:
        c.start()
    for k, c in enumerate(copies):
        c.wait()
        da[sc[0] ^ k] = nt(dq[...], buf[k, :SL, 2 * KV : QKV])


def query_back(scal, dq, parts):
    return call(
        query_back_body,
        "query_back",
        1,
        [scal, dq, *parts],
        [shape((WA, BLK, SL), f32)],
        [pltpu.VMEM((WA, SL + 8, QKVP), bf16), pltpu.SemaphoreType.DMA((WA,))],
        specs=[VMEM] + [ANY] * WA,
        us=2,
    )[0]


def project_back_body(sc, own, go, back, cos_ref, sin_ref, da, x, dm, gain, gain_m, p0, p1, p2, p3, *refs):
    dkv_ref, dx_ref, dxl_ref, d4, buf, sem = refs
    copies = [
        pltpu.make_async_copy(p.at[:, pl.ds(0, 2 * KV)], buf.at[m], sem.at[m])
        for m, p in enumerate((p0, p1, p2, p3))
    ]
    for c in copies:
        c.start()
    total = own[...].astype(f32) + go[...].astype(f32) + back[...].astype(f32)
    cos, sin = cos_ref[...], sin_ref[...]
    edge = head_only((cos, sin))
    for i in range(2):
        dkv_ref[:BLK, 128 * i : 128 * (i + 1)] = rope_back(total[:, 128 * i : 128 * (i + 1)], cos, sin).astype(bf16)
    dkv_ref[:BLK, 256:384] = rope_back(total[:, 256:384], *edge).astype(bf16)
    dkv_ref[:BLK, 384:] = total[:, 384:].astype(bf16)
    for k, c in enumerate(copies):
        c.wait()
        d4[sc[0] ^ k] = da[sc[0] ^ k] + nt(dkv_ref[:BLK, :], buf[k, :SL, :])
    grads = jnp.concatenate([d4[j] for j in range(WA)], axis=1)
    part, gain_grad = norm_back(grads, x[...], gain[...])
    dkv_ref[BLK:, :] = jnp.zeros((8, 2 * KV), bf16)
    for i, g in enumerate((gain_grad, gain_m[...])):
        dkv_ref[BLK + 2 * i : BLK + 2 * i + 1, :] = g[:, : 2 * KV].astype(bf16)
        dkv_ref[BLK + 2 * i + 1 : BLK + 2 * i + 2, : D - 2 * KV] = g[:, 2 * KV :].astype(bf16)
    dx = dm[...] + part
    dx_ref[...] = dx
    dxl_ref[...] = dx.astype(bf16)


def project_back(scal, addends, tables, da, parts, x, dm, gain, gain_m_grad):
    return call(
        project_back_body,
        "project_back",
        1,
        [scal, *addends, *tables, da, x, dm, gain, gain_m_grad, *parts],
        [shape((BLK + 8, 2 * KV), bf16), shape((BLK, D), f32), shape((BLK, D), bf16)],
        [
            pltpu.VMEM((WA, BLK, SL), f32),
            pltpu.VMEM((WA, SL + 8, 2 * KV), bf16),
            pltpu.SemaphoreType.DMA((WA,)),
        ],
        us=2.5,
        specs=[VMEM] * 10 + [ANY] * WA,
    )


def grad_rows_body(has_prev, sc, *refs):
    out = refs[-1]
    slices = refs[:WA]
    lo = 0
    for kind, lows in ((0, refs[WA : 2 * WA]), (0, refs[2 * WA : 3 * WA]), (1, refs[3 * WA : 4 * WA])):
        acc = None
        for sl, low in zip(slices, lows):
            part = tn(sl[kind], low[:BLK])
            acc = part if acc is None else acc + part
        width = acc.shape[1]
        if has_prev:
            acc = acc + refs[4 * WA][:SL, lo : lo + width]
            out[:SL, lo : lo + width] = acc.astype(bf16)
        else:
            out[:SL, lo : lo + width] = acc.astype(bf16)
        lo += width
    gains = sum(low[BLK:, :].astype(f32) for low in refs[WA : 2 * WA])
    rest = D - 2 * KV
    whole = jnp.concatenate(
        [
            jnp.concatenate([gains[2 * i : 2 * i + 1], gains[2 * i + 1 : 2 * i + 2, :rest]], axis=1)
            for i in range(2)
        ],
        axis=0,
    )
    if has_prev:
        whole = whole + refs[4 * WA][SL : SL + 2, :D].astype(f32)
    out[SL:, :] = jnp.zeros((256 - SL, lo), out.dtype)
    out[SL : SL + 2, :D] = whole.astype(out.dtype)


def grad_rows(scal, slices, dkvs, dqs, dmls, prev):
    has_prev = prev is not None
    cols = QKV + D
    return call_fetched(
        functools.partial(grad_rows_body, has_prev),
        "grad_rows",
        scal,
        [*slices, *dkvs, *dqs, *dmls] + ([prev] if has_prev else []),
        [shape((256, cols), bf16)],
        us=4,
        limit=12,
        far=[True] * WA + [not has_prev] * (3 * WA) + [True] * has_prev,
        far_out=not has_prev,
    )[0]


def grad_ffd_body(has_prev, sc, b0, b1, b2, b3, keep, got, z, zg, l0, l1, l2, l3, *refs):
    out, bt = refs[-2:]

    def put(piece, block, lo, part):
        rows, cols = part.shape
        if has_prev:
            part = part + refs[0][piece, block, lo : lo + rows, :cols]
        out[piece, block, lo : lo + rows, :] = part.astype(out.dtype)

    for m, b in enumerate((b0, b1, b2, b3)):
        bt[:, BLK * m : BLK * (m + 1)] = b[...].astype(f32).T.astype(bf16)
    for gu in range(2):
        for j in range(WA):
            lhs = bt[SL * j : SL * (j + 1), :]
            acc = mm(lhs[:, : 2 * BLK], keep[gu]) + mm(lhs[:, 2 * BLK :], got[gu])
            for i in range(4):
                rows = min(64, SL - 64 * i)
                put(4 * gu + i, j, 0, acc[64 * i : 64 * i + rows])
                if rows < 64:
                    out[4 * gu + i, j, rows:] = jnp.zeros((64 - rows, FFQ), out.dtype)
    acc = tn(z[:BLK], l0[...]) + tn(z[BLK:], l1[...])
    acc = acc + tn(zg[:BLK], l2[...]) + tn(zg[BLK:], l3[...])
    for p in range(8):
        d = acc[80 * p : 80 * (p + 1)]
        put(p, 4, 0, d[:64, :FFQ])
        put(p, 5, 0, d[64:, :FFQ])
        put(p, 5, 16, jnp.concatenate([d[:40, FFQ:], d[40:, FFQ:]], axis=1))
        out[p, 5, 56:] = jnp.zeros((8, FFQ), out.dtype)


def grad_ffd(scal, bs, keep, got, z, z_got, lows, prev):
    has_prev = prev is not None
    return call_fetched(
        functools.partial(grad_ffd_body, has_prev),
        "grad_ffd",
        scal,
        [*bs, keep, got, z, z_got, *lows] + ([prev] if has_prev else []),
        [shape((8, WA + 2, 64, FFQ), bf16)],
        us=7,
        limit=24,
        scratch=[pltpu.VMEM((D, WA * BLK), bf16)],
        far=[has_prev] * 4 + [False, False] + [has_prev] * 2 + [False] * WA + [True] * has_prev,
        far_out=not has_prev,
    )[0]


def finish_ff_body(n, sc, *refs):
    gate, up, down, whole = refs[n:]
    position, w = sc[3], sc[0]
    for k in range(n):
        p = (position - k + n) % n
        first = pl.multiple_of(64 * (p % 4), 8)
        for gu, out in enumerate((gate, up)):
            for rows in (64, SL - 192):

                @pl.when((p // 4 == gu) & ((p % 4 < 3) == (rows == 64)))
                def _():
                    for m in range(WA):
                        lo = pl.multiple_of(FFQ * (w ^ m), 128)
                        out[pl.ds(first, rows), pl.ds(lo, FFQ)] = refs[k][m, :rows].astype(f32)

        at = pl.multiple_of(80 * p, 8)
        whole[pl.ds(at, 64), :FFQ] = refs[k][4].astype(f32)
        whole[pl.ds(at + 64, 16), :FFQ] = refs[k][5, :16].astype(f32)
        for i in range(2):
            part = refs[k][5, 16:56, 320 * i : 320 * (i + 1)]
            whole[pl.ds(at + 40 * i, 40), FFQ:] = part.astype(f32)
    down[...] = whole[...].T


def finish_ff(scal, gathered):
    gate, up, down = call_fetched(
        functools.partial(finish_ff_body, len(gathered)),
        "finish_ff",
        scal,
        list(gathered),
        [shape((SL, 4 * FFQ), f32), shape((SL, 4 * FFQ), f32), shape((D, FFQ), f32)],
        us=6,
        limit=32,
        far=[True] * len(gathered),
        scratch=[pltpu.VMEM((FFQ, D), f32)],
    )
    return gate, up, down.T


def finish_rows_body(n, sc, *refs):
    keys, values, query, rows_out, gains, whole = refs[n:]
    for k in range(n):
        p = (sc[3] - k + n) % n
        rows = refs[k].shape[0]
        tail = SL - rows * (n - 1)
        first = pl.multiple_of(p * rows, 8)
        whole[pl.ds(first, rows), :] = refs[k][:, : 2 * KV].astype(f32)

        @pl.when(p < n - 1)
        def _():
            query[pl.ds(first, rows), :] = refs[k][:, 2 * KV : QKV].astype(f32)
            rows_out[pl.ds(first, rows), :] = refs[k][:, QKV:].astype(f32)

        @pl.when(p == n - 1)
        def _():
            query[rows * (n - 1) :, :] = refs[k][:tail, 2 * KV : QKV].astype(f32)
            rows_out[rows * (n - 1) :, :] = refs[k][:tail, QKV:].astype(f32)
            gains[...] = refs[k][tail : tail + 8, :D].astype(f32)

    keys[...] = whole[:SL, :KV].T
    values[...] = whole[:SL, KV:].T


def finish_rows(scal, gathered):
    wide = shape((SL, D), f32)
    keys, values, query, rows_out, gains = call_fetched(
        functools.partial(finish_rows_body, len(gathered)),
        "finish_rows",
        scal,
        list(gathered),
        [shape((KV, SL), f32), shape((KV, SL), f32), wide, wide, shape((8, D), f32)],
        us=4,
        limit=20,
        far=[True] * len(gathered),
        scratch=[pltpu.VMEM((256, 2 * KV), f32)],
    )
    return keys.T, values.T, query, rows_out, gains


def body(
    tokens,
    cotangent,
    segment_ids,
    block_order,
    gain_attn,
    w_query,
    key_projection,
    value_projection,
    w_out,
    gain_mlp,
    w_gate,
    w_up,
    w_down,
):
    n = block_order.shape[1]
    w = lax.axis_index("wa")
    r = lax.axis_index("ctx")
    core = w % 2
    row = w // 2
    position = ring_position(r, n)
    x_side = r % 2
    scal = jnp.stack([w, x_side, row, position, core]).astype(i32)

    blocks = ring_device((position - jnp.arange(n, dtype=i32)) % n, n)
    labels = jnp.arange(n, dtype=i32)
    order_row = block_order[0]
    anchors = jnp.sum(jnp.where(blocks[:, None] == labels[None, :], order_row[None, :], 0), axis=1)
    natural = anchors[0] * BLK + jnp.arange(BLK, dtype=i32)
    seg_labels = jnp.arange(SEQS, dtype=i32)
    sizes = jnp.sum((segment_ids[0][None, :] == seg_labels[:, None]).astype(i32), axis=1)
    before = (seg_labels[None, :] < seg_labels[:, None]).astype(i32)
    starts = jnp.sum(before * sizes[None, :], axis=1)
    start_of = jnp.max(jnp.where(starts[None, :] <= natural[:, None], starts[None, :], 0), axis=1)
    sched = jnp.concatenate([anchors, start_of[:1]]).astype(i32)
    qinfo = jnp.pad(
        jnp.stack([jnp.tile(natural, GQ), jnp.tile(start_of, GQ)]), ((0, 6), (0, 0))
    ).astype(i32)
    frequency = rope_base ** (-jnp.arange(HS // 2, dtype=f32) * 2.0 / HS)
    angles = (natural - start_of).astype(f32)[:, None] * frequency[None, :]
    tables = (jnp.tile(jnp.cos(angles), (1, 4)), jnp.tile(jnp.sin(angles), (1, 4)))

    gains_own = jnp.pad(jnp.stack([gain_attn, gain_mlp]), ((0, 6), (0, 0)))
    qkv_own = pack_qkv(scal, w_query, key_projection, value_projection, gains_own)
    qkv_across = swap(qkv_own, 2)
    qkv_side = swap(qkv_own, 1)
    out_own, keep, give, down_own = pack_rest(scal, after(w_out, qkv_own), w_gate, w_up, w_down)
    core_part = swap(give, 1)

    def y_half(gu):
        return jnp.stack(
            [
                lax.dynamic_index_in_dim(keep[gu], x_side, 0, keepdims=False),
                lax.dynamic_index_in_dim(core_part[gu], x_side, 0, keepdims=False),
            ]
        )

    gate_half, up_half = y_half(0), y_half(1)
    down_half = lax.dynamic_slice_in_dim(down_own, x_side * (FFQ // 2), FFQ // 2, 0)
    top = cotangent[0]
    first = tokens[0]
    cos, sin = tables
    (qkv_across, qkv_side, core_part, out_own, gate_half, up_half, down_half, top, first, cos, sin,
     sched, qinfo) = bar(
        qkv_across, qkv_side, core_part, out_own, gate_half, up_half, down_half, top, first, cos, sin,
        sched, qinfo)
    tables = (cos, sin)
    qkv_parts = [qkv_own, qkv_side, qkv_across, swap(qkv_across, 1)]

    def ring_keys(kv, extras, held):
        if n != 8:
            for e in extras:
                held.update(e(held))
            return ring_gather(kv, n, position)
        rows = BLK // 2
        ahead, behind = [kv], [kv]
        for step in range(4):
            more = extras[step](held)
            if step < 3:
                f, b = ring_shift(ahead[-1], n, 1), ring_shift(behind[-1], n, -1)
            else:
                f = ring_shift(ahead[-1][:rows], n, 1)
                b = ring_shift(behind[-1][rows:], n, -1)
            f, b, *values = bar(f, b, *more.values())
            ahead.append(f)
            behind.append(b)
            held.update(zip(more.keys(), values))
        far = jnp.concatenate([ahead[4], behind[4]], axis=0)
        return jnp.stack(ahead[:4] + [far] + behind[3:0:-1])

    def spread(dkv, extras, held):
        if n != 8:
            for e in extras:
                held.update(e(held))
            total = lax.psum_scatter(
                by_distance(dkv, n, position), "ctx", scatter_dimension=0, tiled=False
            )
            return (total, jnp.zeros_like(total), jnp.zeros_like(total))
        go = back = None
        for step in range(4):
            more = extras[step](held)
            if step == 0:
                go, back = ring_far(lambda k: dkv[k], n)
            else:
                go, back = ring_near(lambda k: dkv[k], n, 4 - step, go, back)
            go, back, *values = bar(go, back, *more.values())
            held.update(zip(more.keys(), values))
        return (dkv[0], go, back)

    gate_mine = swap(gate_half, 2)
    x, a4, q3, kv, gains = project(scal, [first], tables, qkv_parts)
    gain_a, gain_m = gains[0:1], gains[1:2]
    kv, out_own = bar(kv, out_own)
    held = dict(gate_mine=gate_mine)
    out_across = swap(out_own, 2)
    up_mine = swap(after(up_half, kv), 2)

    def gate_other(h):
        return side_swap(h["gate_mine"], n)

    extras = [
        lambda h: dict(out_side=swap(out_own, 1), gate_mine=h["gate_mine"]),
        lambda h: dict(out_across=out_across),
        lambda h: dict(out_diag=swap(h["out_across"], 1)),
        lambda h: dict(gate_other=gate_other(h), up_mine=up_mine),
    ]
    every = ring_keys(kv, extras, held)
    out_parts = [out_own, held["out_side"], held["out_across"], held["out_diag"]]
    up_other = side_swap(held["up_mine"], n)
    down_mine = swap(after(down_half, every), 2)
    *sl, o_t, lse, m, b = attend(scal, sched, qinfo, q3, every, x, a4, gain_m, out_parts)
    m, b, up_other, down_mine = bar(m, b, up_other, down_mine)
    b_side = swap(b, 1)
    down_other = side_swap(down_mine, n)
    down_far = jnp.concatenate(
        [
            jnp.where(x_side == 0, down_mine, down_other),
            jnp.where(x_side == 0, down_other, down_mine),
        ],
        axis=0,
    )
    ff_parts = [
        keep,
        core_part,
        held["gate_mine"],
        held["up_mine"],
        held["gate_other"],
        up_other,
        down_own,
        down_far,
    ]
    b_far = swap(b, 2)
    z, z_give, gu, y_own, y_side = mlp(scal, b, b_side, ff_parts)
    y_own, y_side, b_far, z_give = bar(y_own, y_side, b_far, z_give)
    kept0 = [x, q3, every, o_t, lse, m, gu, z]

    x, a4, q3, kv, _ = project(scal, [m, y_own, swap(y_side, 1)], tables, qkv_parts)
    kv, z_give, b_far = bar(kv, z_give, b_far)
    b0, b0_side, sl0 = b, b_side, sl
    held = {}
    extras = [
        lambda h: dict(z_got=swap(z_give, 2), b_diag=swap(b_far, 1)),
        lambda h: dict(s1=swap(sl0[1], 1), s2=swap(sl0[2], 2)),
        lambda h: dict(s3=swap(sl0[3], 3), top_side=swap(top, 1)),
        lambda h: dict(top_far=swap(top, 2)),
    ]
    every = ring_keys(kv, extras, held)
    kept0 += [
        held["z_got"],
        [b0, b0_side, b_far, held["b_diag"]],
        [sl0[0], held["s1"], held["s2"], held["s3"]],
    ]
    top_side, top_far = held["top_side"], held["top_far"]
    *sl, o_t, lse, m, b = attend(scal, sched, qinfo, q3, every, x, a4, gain_m, out_parts)
    m, b = bar(m, b)
    b_side = swap(b, 1)
    b_far = swap(b, 2)
    z, z_give, gu, y_own, y_side = mlp(scal, b, b_side, ff_parts)
    y_own, y_side, b_far, z_give, z, top = bar(y_own, y_side, b_far, z_give, z, top)

    y_got = swap(y_side, 1)
    z_got = swap(z_give, 2)
    keep_d, give_d, db_own, db_side = mlp_back(scal, top, top_side, gu, ff_parts)
    db_own, db_side, give_d, z_got, y_got = bar(db_own, db_side, give_d, z_got, y_got)
    output = (m + y_own + y_got).astype(bf16)[None]
    db_got = swap(db_side, 1)
    got_d = swap(give_d, 2)
    b_diag = swap(b_far, 1)
    top_diag = swap(top_far, 1)
    dm, dml, gain_m_1, dq, dkv = attend_back(
        False, scal, sched, qinfo, top, db_own, db_got, m, gain_m, out_parts, q3, every, o_t, lse, tables
    )
    dkv, dq, dml, b_diag, top_diag = bar(dkv, dq, dml, b_diag, top_diag)
    lows = [top, top_side, top_far, top_diag]
    bs = [b, b_side, b_far, b_diag]
    sl1, keep_d1, z1 = sl, keep_d, z
    held = {}
    extras = [
        lambda h: dict(got_d=got_d),
        lambda h: dict(
            s1=swap(sl1[1], 1), s2=swap(sl1[2], 2), da=query_back(scal, dq, qkv_parts)
        ),
        lambda h: dict(
            s3=swap(sl1[3], 3),
            dq_far=swap(dq, 2),
            ff_1=grad_ffd(scal, bs, keep_d1, h["got_d"], z1, z_got, lows, None),
        ),
        lambda h: dict(dq_side=swap(dq, 1), dml_side=swap(dml, 1), dml_far=swap(dml, 2)),
    ]
    addends = spread(dkv, extras, held)
    ff_1 = held["ff_1"]
    dq_diag, dml_diag = swap(held["dq_far"], 1), swap(held["dml_far"], 1)
    dkv0, dx, low = project_back(
        scal, addends, tables, held["da"], qkv_parts, x, dm, gain_a, gain_m_1
    )
    dx, low, dkv0, dq_diag, dml_diag = bar(dx, low, dkv0, dq_diag, dml_diag)
    slices_1 = [sl[0], held["s1"], held["s2"], held["s3"]]
    dqs_1 = [dq, held["dq_side"], held["dq_far"], dq_diag]
    dmls_1 = [dml, held["dml_side"], held["dml_far"], dml_diag]

    x, q3, every, o_t, lse, m, gu, z, z_got, bs0, slices = kept0
    low_side = swap(low, 1)
    low_far = swap(low, 2)
    keep_d, give_d, db_own, db_side = mlp_back(scal, low, low_side, gu, ff_parts)
    db_own, db_side, give_d, low_far = bar(db_own, db_side, give_d, low_far)
    db_got = swap(db_side, 1)
    got_d = swap(give_d, 2)
    low_diag = swap(low_far, 1)
    dkv_side, dkv_far = swap(dkv0, 1), swap(dkv0, 2)
    dm, dml, gain_m_0, dq, dkv = attend_back(
        True, scal, sched, qinfo, dx, db_own, db_got, m, gain_m, out_parts, q3, every, o_t, lse, tables
    )
    dkv, dq, dml, got_d, dkv_side, dkv_far, low_diag = bar(
        dkv, dq, dml, got_d, dkv_side, dkv_far, low_diag
    )
    dkvs_1 = [dkv0, dkv_side, dkv_far]
    lows_0 = [low, low_side, low_far, low_diag]

    def ff_piece_of(ff):
        sub = n // 8
        pieces = ff.reshape(8, WA + 2, sub, 64 // sub, FFQ).transpose(0, 2, 1, 3, 4)
        return pieces.reshape(n, WA + 2, 64 // sub, FFQ)

    keep_d0, dq0, dml0 = keep_d, dq, dml
    held = {}

    def ff_ring(h, k):
        if n != 8:
            return {}
        if k == 4:
            h["ff_piece"] = at_position(ff_piece_of(h["ff"]), n, position)
            go, back = ring_far(h["ff_piece"], n)
        else:
            go, back = ring_near(h["ff_piece"], n, k, h["ff_go"], h["ff_back"])
        return dict(ff_go=go, ff_back=back)

    extras = [
        lambda h: dict(dq_far=swap(dq0, 2), ff=grad_ffd(scal, bs0, keep_d0, got_d, z, z_got, lows_0, ff_1)),
        lambda h: dict(dml_far=swap(dml0, 2), **ff_ring(h, 4)),
        lambda h: dict(da=query_back(scal, dq0, qkv_parts), dkv_diag=swap(dkv_far, 1)),
        lambda h: dict(dq_side=swap(dq0, 1), dml_side=swap(dml0, 1), **ff_ring(h, 3)),
    ]
    addends = spread(dkv, extras, held)
    dkv0, dx, low = project_back(
        scal, addends, tables, held["da"], qkv_parts, x, dm, gain_a, gain_m_0
    )
    rows_0 = [held["dq_far"], held["dml_far"]]

    if n == 8:
        ff_piece = held["ff_piece"]
        ff_go, ff_back = ring_near(ff_piece, n, 2, held["ff_go"], held["ff_back"])
        dkv0, rows_0[0], rows_0[1] = bar(dkv0, rows_0[0], rows_0[1])
        dkv_sent = dkv0
        dkv_side, dkv_far_0 = swap(dkv0, 1), swap(dkv0, 2)
        dq_diag, dml_diag = swap(rows_0[0], 1), swap(rows_0[1], 1)
        rows_1 = grad_rows(scal, slices_1, dkvs_1 + [held["dkv_diag"]], dqs_1, dmls_1, None)
        dkv_side, dkv_far_0, dq_diag, dml_diag, rows_1, ff_go, ff_back, low = bar(
            dkv_side, dkv_far_0, dq_diag, dml_diag, rows_1, ff_go, ff_back, low
        )
        ff_go, ff_back = ring_near(ff_piece, n, 1, ff_go, ff_back)
        dkvs = [dkv_sent, dkv_side, dkv_far_0, swap(dkv_far_0, 1)]
        dqs = [dq, held["dq_side"], rows_0[0], dq_diag]
        dmls = [dml, held["dml_side"], rows_0[1], dml_diag]
        rows_grad = grad_rows(scal, slices, dkvs, dqs, dmls, rows_1)
        rows_grad, ff_go, ff_back = bar(rows_grad, ff_go, ff_back)
        piece = at_position(rows_grad.reshape(n, 256 // n, QKV + D), n, position)
        go, back = ring_far(piece, n)
        ff_mine = total_low(ff_piece(0), ff_go, ff_back)
        home = rows_home(ff_mine[:WA], w)
        go, back, home, down_mine = bar(go, back, home, ff_mine[WA:])
        ff_ahead = [jnp.concatenate([home, down_mine], axis=0)]
        ff_behind = list(ff_ahead)
        for k in (3, 2, 1):
            go, back = ring_near(piece, n, k, go, back)
            f, g = ring_shift(ff_ahead[-1], n, 1), ring_shift(ff_behind[-1], n, -1)
            go, back, f, g = bar(go, back, f, g)
            ff_ahead.append(f)
            ff_behind.append(g)
        mine = total_low(piece(0), go, back)
        f, g = ring_shift(ff_ahead[-1][:3], n, 1), ring_shift(ff_behind[-1][3:], n, -1)
        ahead, behind = [mine], [mine]
        a, c = ring_shift(mine, n, 1), ring_shift(mine, n, -1)
        a, c, f, g = bar(a, c, f, g)
        ahead.append(a)
        behind.append(c)
        ff_far = jnp.concatenate([f, g], axis=0)
        ff_all = ff_ahead + [ff_far] + ff_behind[:0:-1]
        gate_total, up_total, down_total = finish_ff(scal, ff_all)
        for _ in range(2):
            a, c = ring_shift(ahead[-1], n, 1), ring_shift(behind[-1], n, -1)
            a, c, gate_total, up_total, down_total = bar(a, c, gate_total, up_total, down_total)
            ahead.append(a)
            behind.append(c)
        half = mine.shape[0] // 2
        far = jnp.concatenate(
            [ring_shift(ahead[-1][:half], n, 1), ring_shift(behind[-1][half:], n, -1)], axis=0
        )
        rows_all = ahead + [far] + behind[:0:-1]
        key_total, value_total, query_total, out_total, gain_rows = finish_rows(scal, rows_all)
    else:
        ff_mine = lax.psum_scatter(
            ff_piece_of(held["ff"]), "ctx", scatter_dimension=0, tiled=False
        )
        ff_home = jnp.concatenate([rows_home(ff_mine[:WA], w), ff_mine[WA:]], axis=0)
        ff_all = ring_gather(ff_home, n, position)
        rows_1 = grad_rows(scal, slices_1, dkvs_1 + [held["dkv_diag"]], dqs_1, dmls_1, None)
        dqs = [dq, held["dq_side"], held["dq_far"], swap(held["dq_far"], 1)]
        dmls = [dml, held["dml_side"], held["dml_far"], swap(held["dml_far"], 1)]
        rows_grad = grad_rows(scal, slices, everyone(dkv0), dqs, dmls, rows_1)
        rows_all = ring_sum(rows_grad.reshape(n, 256 // n, QKV + D), n, position)
        sub = n // 8
        whole = placed(ff_all, n, position).reshape(8, sub, WA + 2, 64 // sub, FFQ)
        whole = whole.transpose(0, 2, 1, 3, 4).reshape(8, WA + 2, 64, FFQ)
        down = whole[:, WA:].reshape(8, 128, FFQ)
        right = down[:, 80:120].reshape(8, 40, 2, FFQ // 2).transpose(0, 2, 1, 3)
        down = jnp.concatenate([down[:, :80], right.reshape(8, 80, FFQ // 2)], axis=2)
        down_total = down.reshape(FFQ, D).astype(f32)
        whole = whole[:, :WA].reshape(2, 4, WA, 64, FFQ).transpose(0, 2, 1, 3, 4)
        whole = whole.reshape(2, WA, 256, FFQ)[:, :, :SL]
        whole = jnp.take(whole, w ^ jnp.arange(WA, dtype=i32), axis=1).transpose(0, 2, 1, 3)
        gate_total, up_total = whole.reshape(2, SL, -1).astype(f32)
        rows_total = placed(rows_all, n, position).reshape(256, QKV + D).astype(f32)
        gain_rows = rows_total[SL:, :D]
        rows_total = rows_total[:SL]
        key_total, value_total, query_total, out_total = (
            rows_total[:, :KV],
            rows_total[:, KV : 2 * KV],
            rows_total[:, 2 * KV : QKV],
            rows_total[:, QKV:],
        )
    input_grad = low[None]
    gain_rows = lax.dynamic_slice_in_dim(gain_rows[:2], w * SL, SL, 1)
    return (
        output,
        input_grad,
        gain_rows[0],
        query_total,
        key_total,
        value_total,
        out_total,
        gain_rows[1],
        gate_total,
        up_total,
        down_total,
    )


def solution(mesh):
    rows = P("wa", None)
    flat = P("wa")
    act = P("wa", "ctx", None)
    return jax.shard_map(
        body,
        mesh=mesh,
        in_specs=(act, act, rows, rows, flat, rows, rows, rows, rows, flat, rows, rows, rows),
        out_specs=(act, act, flat, rows, rows, rows, rows, flat, rows, rows, rows),
        check_vma=False,
    )
```
